32 devices in a mesh: context: 8 (over y, x, core), tensor: 4 (over z).
Axes of the slice: x: 2, y: 2, z: 4, core: 2. Of those that a mesh axis runs over, the one named last changes fastest.
Arguments:
- inputs: bfloat16 [2048, 8192], P('context', 'tensor'), may hold values from -6 to 6
- step_size: float32 [128, 2048], P('tensor', 'context'), as said below
- decay_rate: float32 [128], P('tensor'), as said below
- skip: float32 [128], P('tensor'), may hold values from 0.5 to 1.5
- b_in: bfloat16 [2048, 128], P('context'), may hold values from -1.796875 to 1.796875
- c_in: bfloat16 [2048, 128], P('context'), may hold values from -1.796875 to 1.796875
- doc_start: int32 [2048], P('context'), may hold values 0 or 1
- cotangent: bfloat16 [2048, 8192], P('context', 'tensor'), may hold values from -6 to 6
Outputs:
- mixed: bfloat16 [2048, 8192], P('context', 'tensor')
- grad_inputs: bfloat16 [2048, 8192], P('context', 'tensor')
- grad_b: bfloat16 [2048, 128], P('context')
- grad_c: bfloat16 [2048, 128], P('context')
The draws below stay inside these ranges and needn't reach their ends.
Inputs may be any that keep to these rules, and one draw needn't show every extreme that they name: `step_size`: positive. `decay_rate`: positive. `doc_start`: a 1 marks the first token of a document; the state before the first token is zero.
All inputs are finite; a program needn't handle non-finite values. No bound on the sum of `doc_start` on one device may be relied on, other than what follows from the above.
Results may differ from the reference program's by a relative error of at most 0.001.
Values may be sent and summed in bfloat16 or wider, within the bound.
No kernel may reach another device: no remote copies, remote signals or barrier semaphores. Data moves between devices by JAX's collectives and lax.ppermute only.
A program may use at most 128 MiB of HBM per device.

```python
import math
from functools import partial
import jax
import jax.numpy as jnp
from jax import lax

HEADS = 128
HEAD_DIM = 64
STATE = 128
BLOCK = 128
TOK_DEV = 256
TOKENS = 2048


def head_memory(key):
    inner = jax.random.fold_in(key, 11)
    key_kind, key_fast, key_slow, key_balance = jax.random.split(inner, 4)
    share = 0.5
    quick = jax.random.uniform(key_kind, (HEADS,), jnp.float32) < share
    fast_len = jnp.exp(jax.random.uniform(key_fast, (HEADS,), jnp.float32, math.log(30.0), math.log(50.0)))
    slow_len = TOKENS * jnp.exp(jax.random.uniform(key_slow, (HEADS,), jnp.float32, 0.0, math.log(3.0)))
    memory = jnp.where(quick, fast_len, slow_len)
    balance = jnp.exp(jax.random.uniform(key_balance, (HEADS,), jnp.float32, math.log(0.7), math.log(1.4)))
    return (memory, balance)


def draw_decay_rate(key, part):
    memory, balance = head_memory(key)
    return (balance / jnp.sqrt(memory)).astype(jnp.float32)


def draw_step_size(key, part):
    memory, balance = head_memory(key)
    base = 1.0 / (jnp.sqrt(memory) * balance)
    rough = jnp.exp(jax.random.uniform(jax.random.fold_in(key, 21), (HEADS, TOKENS), jnp.float32, -math.log(2.0), math.log(2.0)))
    pieces = TOKENS // TOK_DEV
    device_factor = jnp.exp(jax.random.uniform(jax.random.fold_in(key, 22), (HEADS, pieces), jnp.float32, -math.log(2.0), math.log(2.0)))
    device_factor = jnp.repeat(device_factor, TOK_DEV, axis=1)
    return (base[:, None] * rough * device_factor).astype(jnp.float32)


def set_ends(entries, rng, least, largest):
    longest = entries.shape.index(max(entries.shape))
    spots = []
    for shift in (0, 1):
        where = [jax.random.randint(jax.random.fold_in(rng, axis), (), 0, length) for axis, length in enumerate(entries.shape)]
        where[longest] = (where[longest] + shift) % entries.shape[longest]
        spots.append(tuple(where))
    return entries.at[spots[0]].set(least).at[spots[1]].set(largest)


def levels(stream_key, extent, cuts, low, top_value):
    factor_of = 1.0
    for axis_at, shards_of in cuts:
        heights = jax.random.uniform(jax.random.fold_in(jax.random.fold_in(stream_key, 6), axis_at), (shards_of,), jnp.float32, low / len(cuts), top_value / len(cuts))
        factor_of = factor_of * jnp.repeat(jnp.exp(heights), extent[axis_at] // shards_of).reshape((-1,) + (1,) * (len(extent) - 1 - axis_at))
    return factor_of


def bell_draw(key, dims, scale, bound, cuts=(), kind=jnp.bfloat16):
    entries = jax.random.normal(key, dims, jnp.float32) * scale
    if len(cuts) > 0:
        entries = levels(key, dims, cuts, -0.22, 0.18) * entries
    return jnp.clip(entries, min=-bound, max=bound).astype(kind)


def setup_inputs(seed: int = 0) -> dict:
    splits = jax.random.split(jax.random.key(seed), 9)
    inputs = bell_draw(splits[0], (TOKENS, HEADS * HEAD_DIM), 1.0, 6.0, ((0, 8), (1, 4)))
    step_size = draw_step_size(jax.random.fold_in(splits[8], 71), 0)
    decay_rate = draw_decay_rate(jax.random.fold_in(splits[8], 71), 0)
    skip = jnp.clip(0.5 + 1.0 * jax.random.uniform(splits[3], (HEADS,), jnp.float32) ** levels(splits[3], (HEADS,), ((0, 4),), -0.2, 0.2), 0.5, 1.5)
    b_in = bell_draw(splits[4], (TOKENS, STATE), 0.3, 1.796875, ((0, 8),))
    c_in = bell_draw(splits[5], (TOKENS, STATE), 0.3, 1.796875, ((0, 8),))
    doc_start = set_ends((jax.random.randint(splits[6], (TOKENS,), 0, 4 * TOK_DEV) < 1).astype(jnp.int32), jax.random.fold_in(splits[6], 1), 0, 1)
    cotangent = bell_draw(splits[7], (TOKENS, HEADS * HEAD_DIM), 1.0, 6.0, ((0, 8), (1, 4)))
    return {"inputs": inputs, "step_size": step_size, "decay_rate": decay_rate, "skip": skip, "b_in": b_in, "c_in": c_in, "doc_start": doc_start, "cotangent": cotangent}


HIGH = lax.Precision.HIGHEST

def contract(spec, *operands):
    return jnp.einsum(spec, *operands, precision=HIGH)

def block_step(skip, carried, item):
    values, b_blk, c_blk, log_decay, steps, starts = item
    decay_sum = jnp.cumsum(log_decay, axis=1)
    doc_count = jnp.cumsum(starts)
    order = jnp.arange(BLOCK)
    mask = (order[:, None] >= order[None, :]) & (doc_count[:, None] == doc_count[None, :])
    spread = decay_sum[:, :, None] - decay_sum[:, None, :]
    weights = jnp.where(mask[None], jnp.exp(jnp.minimum(spread, 0.0)), 0.0)
    intersection = jnp.dot(c_blk, b_blk.T, precision=HIGH)
    scores = weights * intersection[None] * steps[:, None, :]
    carry_keep = jnp.exp(decay_sum) * (doc_count == 0).astype(jnp.float32)[None, :]
    mixed = contract('hts,hsp->htp', scores, values)
    mixed = mixed + carry_keep[:, :, None] * contract('tn,hpn->htp', c_blk, carried)
    mixed = mixed + skip[:, None, None] * values
    end_weight = jnp.exp(decay_sum[:, -1:] - decay_sum) * (doc_count == doc_count[-1]).astype(jnp.float32)[None, :] * steps
    carried = carry_keep[:, -1][:, None, None] * carried + contract('hs,hsp,sn->hpn', end_weight, values, b_blk)
    return (carried, mixed)

def reference(inputs, step_size, decay_rate, skip, b_in, c_in, doc_start, cotangent):
    blocks = TOKENS // BLOCK

    def split_heads(arr):
        return arr.astype(jnp.float32).reshape(blocks, BLOCK, HEADS, HEAD_DIM).transpose(0, 2, 1, 3)

    def join_heads(arr):
        return arr.transpose(0, 2, 1, 3).reshape(TOKENS, HEADS * HEAD_DIM).astype(jnp.bfloat16)
    log_decay = (-step_size * decay_rate[:, None]).reshape(HEADS, blocks, BLOCK).transpose(1, 0, 2)
    steps = step_size.reshape(HEADS, blocks, BLOCK).transpose(1, 0, 2)
    starts = doc_start.reshape(blocks, BLOCK)

    def forward(values, b_all, c_all):
        init = jnp.zeros((HEADS, HEAD_DIM, STATE), jnp.float32)
        stepper = jax.checkpoint(partial(block_step, skip))
        final, mixed = lax.scan(stepper, init, (values, b_all, c_all, log_decay, steps, starts))
        return mixed
    values = split_heads(inputs)
    b_all = b_in.astype(jnp.float32).reshape(blocks, BLOCK, STATE)
    c_all = c_in.astype(jnp.float32).reshape(blocks, BLOCK, STATE)
    mixed, pull = jax.vjp(forward, values, b_all, c_all)
    grad_values, grad_b, grad_c = pull(split_heads(cotangent))
    return (join_heads(mixed), join_heads(grad_values), grad_b.reshape(TOKENS, STATE).astype(jnp.bfloat16), grad_c.reshape(TOKENS, STATE).astype(jnp.bfloat16))
```

```python
import functools

import jax
import jax.numpy as jnp
from jax import lax
from jax.experimental import pallas as pl
from jax.experimental.pallas import tpu as pltpu
from jax.sharding import PartitionSpec as P

BLOCK = 128
LANES = 128
F32 = jnp.float32
BF16 = jnp.bfloat16
NEVER = -200.0
MASKED = -1e30
BOUND = 6.0 * 1.796875
META = 8

NN = (((1,), (0,)), ((), ()))
NT = (((1,), (1,)), ((), ()))
TN = (((0,), (0,)), ((), ()))


def dot(a, b, dims):
    return lax.dot_general(a, b, dims, preferred_element_type=F32)


def split2(x):
    hi = x.astype(BF16)
    lo = (x - hi.astype(F32)).astype(BF16)
    return hi, lo


def split3(x):
    hi = x.astype(BF16)
    rest = x - hi.astype(F32)
    mid = rest.astype(BF16)
    lo = (rest - mid.astype(F32)).astype(BF16)
    return hi, mid, lo


def iota(shape, axis):
    return lax.broadcasted_iota(jnp.int32, shape, axis)


def block_sums(step, decay, doc):
    log_decay = -step * decay
    tri = jnp.where(iota((BLOCK, BLOCK), 0) >= iota((BLOCK, BLOCK), 1), 1.0, 0.0).astype(BF16)
    out = []
    for first in range(0, step.shape[1], BLOCK):
        cols = slice(first, first + BLOCK)
        parts = split3(log_decay[:, cols])
        starts = jnp.broadcast_to(doc[:, cols].astype(F32), (16, BLOCK)).astype(BF16)
        down = functools.reduce(jnp.add, [dot(tri, part, NT) for part in parts])
        across = functools.reduce(jnp.add, [dot(part, tri, NT) for part in parts])
        count_down = dot(tri, starts, NT)[:, :1]
        count_across = dot(starts, tri, NT)[:1]
        out.append((down, across, count_down, count_across))
    return out


def edge_weights(step, sums):
    eye = jnp.where(iota((BLOCK, BLOCK), 0) == iota((BLOCK, BLOCK), 1), 1.0, 0.0).astype(BF16)
    blocks = len(sums)
    ends = [s[0][BLOCK - 1 :] for s in sums]
    counts = [s[2][BLOCK - 1 :] for s in sums]
    keep, last = [], []
    for k in range(blocks):
        down, _, count_down, _ = sums[k]
        sum_before = down
        starts_before = count_down
        sum_after = ends[k] - down
        starts_after = counts[k] - count_down
        for j in range(k):
            sum_before = sum_before + ends[j]
            starts_before = starts_before + counts[j]
        for j in range(k + 1, blocks):
            sum_after = sum_after + ends[j]
            starts_after = starts_after + counts[j]
        parts = split3(step[:, k * BLOCK : (k + 1) * BLOCK])
        step_down = functools.reduce(jnp.add, [dot(eye, part, NT) for part in parts])
        keep.append(jnp.where(starts_before == 0.0, jnp.exp(sum_before), 0.0))
        last.append(jnp.where(starts_after == 0.0, jnp.exp(sum_after) * step_down, 0.0))
    total = functools.reduce(jnp.add, ends)
    starts = functools.reduce(jnp.add, counts)
    total = jnp.where(starts == 0.0, jnp.maximum(total, NEVER), NEVER)
    return jnp.concatenate(keep, 0), jnp.concatenate(last, 0), total


def expander(heads, width):
    shape = (heads, heads * width)
    return jnp.where(iota(shape, 0) == iota(shape, 1) // width, 1.0, 0.0).astype(BF16)


def states_kernel(
    group, width, core_ref, x_ref, g_ref, step_ref, decay_ref, doc_ref, b_ref, c_ref,
    mine_ref, send_ref, b_t, c_t, weights, meta,
):
    step_id = pl.program_id(0)
    groups = weights.shape[1]
    half = b_t.shape[0] // 2

    @pl.when(step_id == 0)
    def _():
        swap = core_ref[0] == 1
        for ref, out in ((b_ref, b_t), (c_ref, c_t)):
            turned = ref[...].astype(F32).T
            swapped = jnp.concatenate([turned[half:], turned[:half]], 0)
            out[...] = jnp.where(swap, swapped, turned).astype(BF16)
        step = step_ref[...]
        keep, last, total = edge_weights(step, block_sums(step, decay_ref[...], doc_ref[...]))
        bound_f = BOUND * jnp.sum(last, axis=0, keepdims=True)
        bound_b = BOUND * jnp.sum(keep, axis=0, keepdims=True)
        rows = jnp.concatenate(
            [total, bound_f, bound_b, jnp.zeros((META - 3, total.shape[1]), F32)], 0
        )
        for k in range(groups):
            heads = slice(k * group, (k + 1) * group)
            weights[0, k] = last[:, heads]
            weights[1, k] = keep[:, heads]
            meta[k] = rows[:, heads]

    spread = expander(group, width)
    rows = functools.reduce(jnp.add, [dot(p, spread, NN) for p in split3(meta[step_id])])
    for kind, (ref, turned) in enumerate(((x_ref, b_t), (g_ref, c_t))):
        hi, lo = split2(weights[kind, step_id])
        turned = turned[...]
        for k in range(group * width // LANES):
            lanes = slice(k * LANES, (k + 1) * LANES)
            scale = dot(hi, spread[:, lanes], NN) + dot(lo, spread[:, lanes], NN)
            scaled = split2(ref[:, lanes].astype(F32) * scale)
            state = dot(turned, scaled[0], NN) + dot(turned, scaled[1], NN)
            mine_ref[k, kind * half : (kind + 1) * half] = state[:half]
            send_ref[k, kind * half : (kind + 1) * half] = state[half:]
    for k in range(group * width // LANES):
        lanes = slice(k * LANES, (k + 1) * LANES)
        mine_ref[k, 2 * half :] = rows[:, lanes]
        send_ref[k, 2 * half :] = rows[:, lanes]


def local_kernel(
    group, width, skip_ref, x_ref, g_ref, step_ref, step_blk, decay_ref, doc_ref, b_ref, c_ref,
    mixed_ref, gx_ref, xh_ref, xl_ref, gh_ref, gl_ref, grads_ref,
    weights, down_s, across_s, bias, inter, common,
):
    step_id = pl.program_id(0)
    groups = weights.shape[1]
    pairs = ((0, 0), (1, 0), (1, 1))

    @pl.when(step_id == 0)
    def _():
        step = step_ref[...]
        sums = block_sums(step, decay_ref[...], doc_ref[...])
        keep, last, _ = edge_weights(step, sums)
        for k in range(groups):
            heads = slice(k * group, (k + 1) * group)
            weights[0, k] = last[:, heads]
            weights[1, k] = keep[:, heads]
            for j in range(2):
                down_s[j, k] = sums[j][0][:, heads]
                across_s[j, k] = sums[j][1][heads]
        for n, (t, s) in enumerate(pairs):
            if t == s:
                ok = sums[t][2] == sums[s][3]
                ok = ok & (iota((BLOCK, BLOCK), 0) >= iota((BLOCK, BLOCK), 1))
            else:
                ok = sums[t][2] == sums[s][3] - sums[s][3][:, BLOCK - 1 :]
            bias[n] = jnp.where(ok, 0.0, MASKED)
            inter[n] = dot(
                c_ref[t * BLOCK : (t + 1) * BLOCK], b_ref[s * BLOCK : (s + 1) * BLOCK], NT
            )
        common[...] = jnp.zeros_like(common)

    spread = expander(group, width)
    for ref, high, low, kind in ((x_ref, xh_ref, xl_ref, 0), (g_ref, gh_ref, gl_ref, 1)):
        hi, lo = split2(weights[kind, step_id])
        for k in range(group * width // LANES):
            lanes = slice(k * LANES, (k + 1) * LANES)
            scale = dot(hi, spread[:, lanes], NN) + dot(lo, spread[:, lanes], NN)
            scaled = split2(ref[:, lanes].astype(F32) * scale)
            high[:, lanes] = scaled[0]
            low[:, lanes] = scaled[1]

    down = [down_s[j, step_id] for j in range(2)]
    across = [across_s[j, step_id] for j in range(2)]
    left = iota((BLOCK, LANES), 1) < width
    left2 = iota((2 * BLOCK, LANES), 1) < width
    for k in range(group * width // LANES):
        lanes = slice(k * LANES, (k + 1) * LANES)
        xs = [x_ref[j * BLOCK : (j + 1) * BLOCK, lanes] for j in range(2)]
        gs = [g_ref[j * BLOCK : (j + 1) * BLOCK, lanes] for j in range(2)]
        zero = jnp.zeros_like(gs[0])
        halves = [
            jnp.concatenate([jnp.where(left, v, zero), jnp.where(left, zero, v)], 0) for v in gs
        ]
        inner = [dot(halves[t], xs[s], NT) for t, s in pairs]
        twice_x = [jnp.concatenate([v, v], 0) for v in xs]
        twice_g = [jnp.concatenate([v, v], 0) for v in gs]
        both_x = jnp.concatenate(twice_x, 0)
        both_g = jnp.concatenate(twice_g, 0)
        mixed_parts, gx_parts = [], []
        totals = [None] * 3
        for e in range(2):
            h = 2 * k + e
            parts = []
            for n, (t, s) in enumerate(pairs):
                row = across[s][h : h + 1]
                if t != s:
                    row = row - row[:, BLOCK - 1 :]
                weight = jnp.exp((down[t][:, h : h + 1] + bias[n]) - row)
                weight = weight * step_blk[h : h + 1, s * BLOCK : (s + 1) * BLOCK]
                term = weight * inner[n][e * BLOCK : (e + 1) * BLOCK]
                totals[n] = term if e == 0 else totals[n] + term
                parts.append(split2(weight * inter[n]))
            p00, p10, p11 = parts
            mixed_parts.append(
                (
                    dot(jnp.concatenate(p00, 1), twice_x[0], NN),
                    dot(jnp.concatenate(p10 + p11, 1), both_x, NN),
                )
            )
            gx_parts.append(
                (
                    dot(jnp.concatenate(p00 + p10, 0), both_g, TN),
                    dot(jnp.concatenate(p11, 0), twice_g[1], TN),
                )
            )
        for n in range(3):
            common[n] += totals[n]
        first = step_id * group + 2 * k
        skip = jnp.where(left, skip_ref[first], skip_ref[first + 1])
        for j in range(2):
            rows = slice(j * BLOCK, (j + 1) * BLOCK)
            mixed_ref[rows, lanes] = (
                jnp.where(left, mixed_parts[0][j], mixed_parts[1][j]) + skip * xs[j].astype(F32)
            )
            gx_ref[rows, lanes] = (
                jnp.where(left, gx_parts[0][j], gx_parts[1][j]) + skip * gs[j].astype(F32)
            )

    @pl.when(step_id == pl.num_programs(0) - 1)
    def _():
        c00, c10, c11 = [split2(common[n]) for n in range(3)]
        b0, b1 = b_ref[:BLOCK], b_ref[BLOCK:]
        c0, c1 = c_ref[:BLOCK], c_ref[BLOCK:]
        grads_ref[0, :BLOCK] = sum(dot(v, c0, TN) for v in c00) + sum(dot(v, c1, TN) for v in c10)
        grads_ref[0, BLOCK:] = sum(dot(v, c1, TN) for v in c11)
        grads_ref[1, :BLOCK] = sum(dot(v, b0, NN) for v in c00)
        grads_ref[1, BLOCK:] = sum(dot(v, b0, NN) for v in c10) + sum(dot(v, b1, NN) for v in c11)


def place_state(core, own, other, kind, high, low):
    half = own.shape[2]
    at = pl.multiple_of(core * half, half)
    away = pl.multiple_of((1 - core) * half, half)
    for k in range(own.shape[1]):
        lanes = slice(k * LANES, (k + 1) * LANES)
        hi, lo = split2(own[kind, k])
        high[pl.ds(at, half), lanes] = hi
        low[pl.ds(at, half), lanes] = lo
        hi, lo = split2(other[kind, k])
        high[pl.ds(away, half), lanes] = hi
        low[pl.ds(away, half), lanes] = lo


def grads_kernel(
    parts, core_ref, own_ref, other_ref, xh_ref, xl_ref, gh_ref, gl_ref, local_ref, out_ref,
    high, low, total,
):
    step_id = pl.program_id(0)

    @pl.when(step_id == 0)
    def _():
        total[...] = local_ref[...]

    for slot, kind, vh, vl in ((0, 1, xh_ref, xl_ref), (1, 0, gh_ref, gl_ref)):
        place_state(core_ref[0], own_ref, other_ref, kind, high.at[kind], low.at[kind])
        hi, lo = high[kind], low[kind]
        first = vh[...]
        total[slot] += dot(first, hi, NT) + dot(first, lo, NT) + dot(vl[...], hi, NT)

    @pl.when(step_id == pl.num_programs(0) - 1)
    def _():
        rows = total.shape[1] // parts
        for k in range(parts):
            for slot in range(2):
                out_ref[k, slot] = total[slot, k * rows : (k + 1) * rows]


def outputs_kernel(
    group, width, core_ref, own_ref, other_ref, mixed_ref, gx_ref, step_ref, decay_ref, doc_ref,
    b_ref, c_ref, mixed_out, gx_out, high, low, weights,
):
    step_id = pl.program_id(0)
    groups = weights.shape[1]

    @pl.when(step_id == 0)
    def _():
        step = step_ref[...]
        keep, last, _ = edge_weights(step, block_sums(step, decay_ref[...], doc_ref[...]))
        for k in range(groups):
            heads = slice(k * group, (k + 1) * group)
            weights[0, k] = last[:, heads]
            weights[1, k] = keep[:, heads]

    spread = expander(group, width)
    for kind, weight, proj, base, out in (
        (0, 1, c_ref, mixed_ref, mixed_out),
        (1, 0, b_ref, gx_ref, gx_out),
    ):
        place_state(core_ref[0], own_ref, other_ref, kind, high.at[kind], low.at[kind])
        hi, lo = split2(weights[weight, step_id])
        proj = proj[...]
        for k in range(group * width // LANES):
            lanes = slice(k * LANES, (k + 1) * LANES)
            scale = dot(hi, spread[:, lanes], NN) + dot(lo, spread[:, lanes], NN)
            carried = dot(proj, high[kind, :, lanes], NN) + dot(proj, low[kind, :, lanes], NN)
            out[:, lanes] = (base[:, lanes] + scale * carried).astype(BF16)


def whole(shape):
    return pl.BlockSpec(shape, lambda i: (0,) * len(shape))


SMEM = pl.BlockSpec(memory_space=pltpu.SMEM)
PARAMS = pltpu.CompilerParams(vmem_limit_bytes=48 << 20)


def swap_with(value, axis, mask):
    size = lax.axis_size(axis)
    return lax.ppermute(value, axis, [(i, i ^ mask) for i in range(size)])


def scan_chips(total_f, total_b, total_l, axis):
    size, index = lax.axis_size(axis), lax.axis_index(axis)
    before, after = jnp.zeros_like(total_f), jnp.zeros_like(total_b)
    log_before, log_after = jnp.zeros_like(total_l), jnp.zeros_like(total_l)
    bit = 2
    while bit < size:
        other_f, other_b, other_l = [swap_with(v, axis, bit) for v in (total_f, total_b, total_l)]
        upper = (index & bit) != 0
        before = jnp.where(upper, jnp.exp(log_before) * other_f + before, before)
        after = jnp.where(upper, after, jnp.exp(log_after) * other_b + after)
        log_before = jnp.where(upper, log_before + other_l, log_before)
        log_after = jnp.where(upper, log_after, log_after + other_l)
        scale, other_scale = jnp.exp(total_l), jnp.exp(other_l)
        total_f = jnp.where(upper, scale * other_f + total_f, other_scale * total_f + other_f)
        total_b = jnp.where(upper, other_b + other_scale * total_b, total_b + scale * other_b)
        total_l = jnp.maximum(total_l + other_l, NEVER)
        bit *= 2
    return before, after


def encode(state, bound, log_decay):
    chunks = state.shape[0]
    power = jnp.clip(jnp.ceil(jnp.log2(bound)), -100.0, 120.0)
    data = state * jnp.exp2(14.0 - power)
    first = lax.reduce_precision(log_decay, 5, 10)
    second = lax.reduce_precision(log_decay - first, 5, 10)
    third = lax.reduce_precision(log_decay - first - second, 5, 10)
    rows = [v.reshape(chunks, LANES) for v in (first, second, third, power)]
    return jnp.concatenate([data.reshape(-1, LANES)] + rows, 0).astype(jnp.float16)


def decode(coded, chunks):
    values = coded.astype(F32)
    size = coded.shape[0] - 4 * chunks
    rows = [
        values[size + k * chunks : size + (k + 1) * chunks].reshape(chunks, 1, LANES)
        for k in range(4)
    ]
    state = values[:size].reshape(chunks, -1, LANES) * jnp.exp2(rows[3] - 14.0)
    return state, rows[0] + rows[1] + rows[2]


def meet_chips(total_f, total_b, bound_f, bound_b, total_l, axis):
    index = lax.axis_index(axis)
    chunks = total_f.shape[0]
    x, y = (index >> 1) & 1, (index >> 2) & 1
    near_up, far_up = x == 0, y == 0
    near = encode(
        jnp.where(near_up, total_f, total_b), jnp.where(near_up, bound_f, bound_b), total_l
    )
    far = encode(
        jnp.where(far_up, total_f, total_b), jnp.where(far_up, bound_f, bound_b), total_l
    )
    from_two = swap_with(far, axis, 4)
    from_three = swap_with(far, axis, 6)
    from_one = swap_with(near, axis, 2)
    return from_one, from_two, from_three


def join_chips(arrived, axis, chunks):
    index = lax.axis_index(axis)
    x, y = (index >> 1) & 1, (index >> 2) & 1
    (one, log_one), (two, log_two), (three, log_three) = [decode(v, chunks) for v in arrived]
    same = x == y
    close = jnp.where(same, two, three)
    log_close = jnp.where(same, log_two, log_three)
    distant = jnp.where(same, three, two)
    beyond = close + jnp.exp(log_close) * distant
    main = jnp.where(same, one + jnp.exp(log_one) * beyond, beyond)
    side = jnp.where(same, 0.0, one)
    upper = y == 1
    return jnp.where(upper, main, side), jnp.where(upper, side, main)


def shards(inputs, step_size, decay_rate, skip, b_in, c_in, doc_start, cotangent):
    heads, tokens = step_size.shape
    channels = inputs.shape[1]
    width = channels // heads
    state = b_in.shape[1]
    half = state // 2
    group = min(8, heads)
    groups = heads // group
    wide = group * width
    per = wide // LANES
    chunks = channels // LANES
    context, tensor = lax.axis_size("context"), lax.axis_size("tensor")
    index = lax.axis_index("context")
    core = index & 1
    flag = core.reshape(1).astype(jnp.int32)
    decay = decay_rate.reshape(heads, 1)
    doc = doc_start.reshape(1, tokens)

    tok = pl.BlockSpec((tokens, wide), lambda i: (0, i))
    small = [
        whole((heads, tokens)),
        whole((heads, 1)),
        whole((1, tokens)),
        whole((tokens, state)),
        whole((tokens, state)),
    ]
    piece = pl.BlockSpec((per, state + META, LANES), lambda i: (i, 0, 0))
    weights = pltpu.VMEM((2, groups, tokens, group), F32)
    mine, send = pl.pallas_call(
        functools.partial(states_kernel, group, width),
        grid=(groups,),
        in_specs=[SMEM, tok, tok] + small,
        out_specs=[piece, piece],
        out_shape=[jax.ShapeDtypeStruct((chunks, state + META, LANES), F32)] * 2,
        scratch_shapes=[
            pltpu.VMEM((state, tokens), BF16),
            pltpu.VMEM((state, tokens), BF16),
            weights,
            pltpu.VMEM((groups, META, group), F32),
        ],
        compiler_params=PARAMS,
        name="states",
    )(flag, inputs, cotangent, step_size, decay, doc, b_in, c_in)

    theirs = swap_with(send, "context", 1)
    lower = core == 0
    own_f, own_b = mine[:, :half], mine[:, half:state]
    sib_f, sib_b = theirs[:, :half], theirs[:, half:state]
    own_l, own_mf, own_mb = [mine[:, state + k : state + k + 1] for k in range(3)]
    sib_l, sib_mf, sib_mb = [theirs[:, state + k : state + k + 1] for k in range(3)]
    own_e, sib_e = jnp.exp(own_l), jnp.exp(sib_l)
    f_own, f_sib = jnp.where(lower, sib_e, 1.0), jnp.where(lower, 1.0, own_e)
    b_own, b_sib = jnp.where(lower, 1.0, sib_e), jnp.where(lower, own_e, 1.0)
    chip_f = f_own * own_f + f_sib * sib_f
    chip_b = b_own * own_b + b_sib * sib_b
    chip_l = jnp.maximum(own_l + sib_l, NEVER)
    if context == 8:
        arrived = meet_chips(
            chip_f,
            chip_b,
            f_own * own_mf + f_sib * sib_mf,
            b_own * own_mb + b_sib * sib_mb,
            chip_l,
            "context",
        )
        before, after = join_chips(arrived, "context", chunks)
    else:
        before, after = scan_chips(chip_f, chip_b, chip_l, "context")

    full = jax.ShapeDtypeStruct((tokens, channels), F32)
    coded = jax.ShapeDtypeStruct((tokens, channels), BF16)
    mixed_loc, gx_loc, xh, xl, gh, gl, grads_loc = pl.pallas_call(
        functools.partial(local_kernel, group, width),
        grid=(groups,),
        in_specs=[
            SMEM,
            tok,
            tok,
            small[0],
            pl.BlockSpec((group, tokens), lambda i: (i, 0)),
        ]
        + small[1:],
        out_specs=[tok] * 6 + [whole((2, tokens, state))],
        out_shape=[full, full] + [coded] * 4 + [jax.ShapeDtypeStruct((2, tokens, state), F32)],
        scratch_shapes=[
            weights,
            pltpu.VMEM((2, groups, BLOCK, group), F32),
            pltpu.VMEM((2, groups, group, BLOCK), F32),
            pltpu.VMEM((3, BLOCK, BLOCK), F32),
            pltpu.VMEM((3, BLOCK, BLOCK), F32),
            pltpu.VMEM((3, BLOCK, BLOCK), F32),
        ],
        compiler_params=PARAMS,
        cost_estimate=pl.CostEstimate(
            flops=20 * tokens * tokens * channels,
            transcendentals=heads * tokens * tokens,
            bytes_accessed=20 * tokens * channels,
        ),
        name="local",
    )(skip, inputs, cotangent, step_size, step_size, decay, doc, b_in, c_in)

    entering = jnp.stack(
        [
            jnp.where(lower, before, sib_e * before + sib_f),
            jnp.where(lower, sib_b + sib_e * after, after),
        ]
    )
    passed = jnp.stack(
        [
            jnp.where(lower, own_e * before + own_f, before),
            jnp.where(lower, after, own_b + own_e * after),
        ]
    )
    other = swap_with(passed, "context", 1)

    parts = tensor if tokens % (8 * tensor) == 0 else 1
    state_spec = pl.BlockSpec((2, per, half, LANES), lambda i: (0, i, 0, 0))
    grads = pl.pallas_call(
        functools.partial(grads_kernel, parts),
        grid=(groups,),
        in_specs=[SMEM, state_spec, state_spec] + [tok] * 4 + [whole((2, tokens, state))],
        out_specs=whole((parts, 2, tokens // parts, state)),
        out_shape=jax.ShapeDtypeStruct((parts, 2, tokens // parts, state), F32),
        scratch_shapes=[
            pltpu.VMEM((2, state, wide), BF16),
            pltpu.VMEM((2, state, wide), BF16),
            pltpu.VMEM((2, tokens, state), F32),
        ],
        compiler_params=PARAMS,
        name="grads",
    )(flag, entering, other, xh, xl, gh, gl, grads_loc)

    mixed, grad_inputs = pl.pallas_call(
        functools.partial(outputs_kernel, group, width),
        grid=(groups,),
        in_specs=[SMEM, state_spec, state_spec, tok, tok] + small,
        out_specs=[tok, tok],
        out_shape=[coded, coded],
        scratch_shapes=[
            pltpu.VMEM((2, state, wide), BF16),
            pltpu.VMEM((2, state, wide), BF16),
            weights,
        ],
        compiler_params=PARAMS,
        cost_estimate=pl.CostEstimate(
            flops=8 * tokens * state * channels,
            transcendentals=2 * heads * tokens,
            bytes_accessed=16 * tokens * channels,
        ),
        name="outputs",
    )(flag, entering, other, mixed_loc, gx_loc, step_size, decay, doc, b_in, c_in)

    if tensor == 4 and parts == 4:
        place = lax.axis_index("tensor")
        pick = lambda at: lax.dynamic_index_in_dim(grads, at, 0, False)
        total = pick(place)
        for k in (2, 3, 1):
            total = total + swap_with(pick(place ^ k), "tensor", k)
        total = total.astype(BF16)
        summed = jnp.zeros((parts,) + total.shape, BF16)
        summed = lax.dynamic_update_index_in_dim(summed, total, place, 0)
        for k in (2, 3, 1):
            summed = lax.dynamic_update_index_in_dim(
                summed, swap_with(total, "tensor", k), place ^ k, 0
            )
    else:
        summed = lax.psum(grads, "tensor").astype(BF16)
    grad_b = summed[:, 0].reshape(tokens, state)
    grad_c = summed[:, 1].reshape(tokens, state)
    return (mixed, grad_inputs, grad_b, grad_c)


def solution(mesh):
    in_specs = (
        P("context", "tensor"),
        P("tensor", "context"),
        P("tensor"),
        P("tensor"),
        P("context", None),
        P("context", None),
        P("context"),
        P("context", "tensor"),
    )
    out_specs = (
        P("context", "tensor"),
        P("context", "tensor"),
        P("context", None),
        P("context", None),
    )
    return jax.shard_map(shards, mesh=mesh, in_specs=in_specs, out_specs=out_specs, check_vma=False)
```

```python
import functools

import jax
import jax.numpy as jnp
from jax import lax
from jax.experimental import pallas as pl
from jax.experimental.pallas import tpu as pltpu
from jax.sharding import PartitionSpec as P

BLOCK = 128
LANES = 128
F32 = jnp.float32
BF16 = jnp.bfloat16
NEVER = -200.0
MASKED = -1e30
BOUND = 6.0 * 1.796875
META = 8

NN = (((1,), (0,)), ((), ()))
NT = (((1,), (1,)), ((), ()))
TN = (((0,), (0,)), ((), ()))


def dot(a, b, dims):
    return lax.dot_general(a, b, dims, preferred_element_type=F32)


def split2(x):
    hi = x.astype(BF16)
    lo = (x - hi.astype(F32)).astype(BF16)
    return hi, lo


def split3(x):
    hi = x.astype(BF16)
    rest = x - hi.astype(F32)
    mid = rest.astype(BF16)
    lo = (rest - mid.astype(F32)).astype(BF16)
    return hi, mid, lo


def iota(shape, axis):
    return lax.broadcasted_iota(jnp.int32, shape, axis)


def block_sums(step, decay, doc):
    log_decay = -step * decay
    tri = jnp.where(iota((BLOCK, BLOCK), 0) >= iota((BLOCK, BLOCK), 1), 1.0, 0.0).astype(BF16)
    out = []
    for first in range(0, step.shape[1], BLOCK):
        cols = slice(first, first + BLOCK)
        parts = split3(log_decay[:, cols])
        starts = jnp.broadcast_to(doc[:, cols].astype(F32), (16, BLOCK)).astype(BF16)
        down = functools.reduce(jnp.add, [dot(tri, part, NT) for part in parts])
        across = functools.reduce(jnp.add, [dot(part, tri, NT) for part in parts])
        count_down = dot(tri, starts, NT)[:, :1]
        count_across = dot(starts, tri, NT)[:1]
        out.append((down, across, count_down, count_across))
    return out


def edge_weights(step, sums):
    eye = jnp.where(iota((BLOCK, BLOCK), 0) == iota((BLOCK, BLOCK), 1), 1.0, 0.0).astype(BF16)
    blocks = len(sums)
    ends = [s[0][BLOCK - 1 :] for s in sums]
    counts = [s[2][BLOCK - 1 :] for s in sums]
    keep, last = [], []
    for k in range(blocks):
        down, _, count_down, _ = sums[k]
        sum_before = down
        starts_before = count_down
        sum_after = ends[k] - down
        starts_after = counts[k] - count_down
        for j in range(k):
            sum_before = sum_before + ends[j]
            starts_before = starts_before + counts[j]
        for j in range(k + 1, blocks):
            sum_after = sum_after + ends[j]
            starts_after = starts_after + counts[j]
        parts = split3(step[:, k * BLOCK : (k + 1) * BLOCK])
        step_down = functools.reduce(jnp.add, [dot(eye, part, NT) for part in parts])
        keep.append(jnp.where(starts_before == 0.0, jnp.exp(sum_before), 0.0))
        last.append(jnp.where(starts_after == 0.0, jnp.exp(sum_after) * step_down, 0.0))
    total = functools.reduce(jnp.add, ends)
    starts = functools.reduce(jnp.add, counts)
    total = jnp.where(starts == 0.0, jnp.maximum(total, NEVER), NEVER)
    return jnp.concatenate(keep, 0), jnp.concatenate(last, 0), total


def expander(heads, width):
    shape = (heads, heads * width)
    return jnp.where(iota(shape, 0) == iota(shape, 1) // width, 1.0, 0.0).astype(BF16)


def fetch(pairs, sems):
    copies = [pltpu.make_async_copy(src, dst, sems.at[k]) for k, (src, dst) in enumerate(pairs)]
    for copy in copies:
        copy.start()
    return copies


def column(row):
    shape = (row.shape[1], row.shape[1])
    spot = iota(shape, 0) == iota(shape, 1)
    return jnp.sum(jnp.where(spot, row, 0.0), axis=1, keepdims=True)


def states_kernel(
    group, width, core_ref, x_hbm, g_hbm, step_hbm, decay_hbm, doc_hbm, b_hbm, c_hbm,
    mine_ref, send_ref, meta_ref, x_ref, g_ref, step_ref, decay_ref, doc_ref, b_ref, c_ref,
    b_t, c_t, weights, meta, small_sems, big_sems,
):
    step_id = pl.program_id(0)
    groups = weights.shape[1]
    half = b_t.shape[0] // 2
    wide = group * width
    chunks = wide // LANES

    def big(k):
        return [
            pltpu.make_async_copy(
                src.at[:, pl.ds(pl.multiple_of(k * wide, LANES), wide)], dst.at[k], big_sems.at[n, k]
            )
            for n, (src, dst) in enumerate(((x_hbm, x_ref), (g_hbm, g_ref)))
        ]

    @pl.when(step_id == 0)
    def _():
        small = fetch(
            (
                (step_hbm, step_ref),
                (decay_hbm, decay_ref),
                (doc_hbm, doc_ref),
                (b_hbm, b_ref),
                (c_hbm, c_ref),
            ),
            small_sems,
        )
        for k in range(groups):
            for copy in big(k):
                copy.start()
        for copy in small:
            copy.wait()
        swap = core_ref[0] == 1
        step = step_ref[...]
        sums = block_sums(step, column(decay_ref[...]), doc_ref[...])
        keep, last, total = edge_weights(step, sums)
        bound_f = BOUND * jnp.sum(last, axis=0, keepdims=True)
        bound_b = BOUND * jnp.sum(keep, axis=0, keepdims=True)
        rows = [total, jnp.exp(total), bound_f, bound_b]
        rows = jnp.concatenate(rows + [jnp.zeros((META - 4, total.shape[1]), F32)], 0)
        for k in range(groups):
            heads = slice(k * group, (k + 1) * group)
            weights[0, k] = last[:, heads]
            weights[1, k] = keep[:, heads]
            meta[k] = rows[:, heads]
        for ref, out in ((b_ref, b_t), (c_ref, c_t)):
            turned = ref[...].astype(F32).T
            swapped = jnp.concatenate([turned[half:], turned[:half]], 0)
            out[...] = jnp.where(swap, swapped, turned).astype(BF16)

    for copy in big(step_id):
        copy.wait()
    spread = expander(group, width)
    rows = functools.reduce(jnp.add, [dot(p, spread, NN) for p in split3(meta[step_id])])
    for k in range(chunks):
        for n in range(META):
            meta_ref[n, pl.ds(step_id * chunks + k, 1)] = rows[n : n + 1, k * LANES : (k + 1) * LANES]
    for kind, (ref, turned) in enumerate(((x_ref, b_t), (g_ref, c_t))):
        hi, lo = split2(weights[kind, step_id])
        turned = turned[...]
        for k in range(chunks):
            lanes = slice(k * LANES, (k + 1) * LANES)
            scale = dot(hi, spread[:, lanes], NN) + dot(lo, spread[:, lanes], NN)
            scaled = split2(ref[step_id, :, lanes].astype(F32) * scale)
            state = dot(turned, scaled[0], NN) + dot(turned, scaled[1], NN)
            mine_ref[k, kind * half : (kind + 1) * half] = state[:half]
            send_ref[k, kind * half : (kind + 1) * half] = state[half:]


def local_kernel(
    group, width, skip_ref, x_ref, g_ref, step_ref, step_blk, decay_ref, doc_ref, b_ref, c_ref,
    mixed_ref, gx_ref, xh_ref, xl_ref, gh_ref, gl_ref, coded_ref, grads_ref,
    weights, down_s, across_s, bias, inter, common,
):
    step_id = pl.program_id(0)
    groups = weights.shape[1]
    pairs = ((0, 0), (1, 0), (1, 1))

    @pl.when(step_id == 0)
    def _():
        step = step_ref[...]
        sums = block_sums(step, column(decay_ref[...]), doc_ref[...])
        keep, last, _ = edge_weights(step, sums)
        for k in range(groups):
            heads = slice(k * group, (k + 1) * group)
            weights[0, k] = last[:, heads]
            weights[1, k] = keep[:, heads]
            for j in range(2):
                down_s[j, k] = sums[j][0][:, heads]
                across_s[j, k] = sums[j][1][heads]
        for n, (t, s) in enumerate(pairs):
            if t == s:
                ok = sums[t][2] == sums[s][3]
                ok = ok & (iota((BLOCK, BLOCK), 0) >= iota((BLOCK, BLOCK), 1))
            else:
                ok = sums[t][2] == sums[s][3] - sums[s][3][:, BLOCK - 1 :]
            bias[n] = jnp.where(ok, 0.0, MASKED)
            inter[n] = dot(
                c_ref[t * BLOCK : (t + 1) * BLOCK], b_ref[s * BLOCK : (s + 1) * BLOCK], NT
            )
        common[...] = jnp.zeros_like(common)

    spread = expander(group, width)
    for ref, high, low, kind in ((x_ref, xh_ref, xl_ref, 0), (g_ref, gh_ref, gl_ref, 1)):
        hi, lo = split2(weights[kind, step_id])
        coded_ref[kind, 0, 0] = hi
        coded_ref[kind, 0, 1] = lo
        for k in range(group * width // LANES):
            lanes = slice(k * LANES, (k + 1) * LANES)
            scale = dot(hi, spread[:, lanes], NN) + dot(lo, spread[:, lanes], NN)
            scaled = split2(ref[:, lanes].astype(F32) * scale)
            high[:, lanes] = scaled[0]
            low[:, lanes] = scaled[1]

    down = [down_s[j, step_id] for j in range(2)]
    across = [across_s[j, step_id] for j in range(2)]
    left = iota((BLOCK, LANES), 1) < width
    left2 = iota((2 * BLOCK, LANES), 1) < width
    for k in range(group * width // LANES):
        lanes = slice(k * LANES, (k + 1) * LANES)
        xs = [x_ref[j * BLOCK : (j + 1) * BLOCK, lanes] for j in range(2)]
        gs = [g_ref[j * BLOCK : (j + 1) * BLOCK, lanes] for j in range(2)]
        zero = jnp.zeros_like(gs[0])
        halves = [
            jnp.concatenate([jnp.where(left, v, zero), jnp.where(left, zero, v)], 0) for v in gs
        ]
        inner = [dot(halves[t], xs[s], NT) for t, s in pairs]
        twice_x = [jnp.concatenate([v, v], 0) for v in xs]
        twice_g = [jnp.concatenate([v, v], 0) for v in gs]
        both_x = jnp.concatenate(twice_x, 0)
        both_g = jnp.concatenate(twice_g, 0)
        mixed_parts, gx_parts = [], []
        totals = [None] * 3
        for e in range(2):
            h = 2 * k + e
            parts = []
            for n, (t, s) in enumerate(pairs):
                row = across[s][h : h + 1]
                if t != s:
                    row = row - row[:, BLOCK - 1 :]
                weight = jnp.exp((down[t][:, h : h + 1] + bias[n]) - row)
                weight = weight * step_blk[h : h + 1, s * BLOCK : (s + 1) * BLOCK]
                term = weight * inner[n][e * BLOCK : (e + 1) * BLOCK]
                totals[n] = term if e == 0 else totals[n] + term
                parts.append(split2(weight * inter[n]))
            p00, p10, p11 = parts
            mixed_parts.append(
                (
                    dot(jnp.concatenate(p00, 1), twice_x[0], NN),
                    dot(jnp.concatenate(p10 + p11, 1), both_x, NN),
                )
            )
            gx_parts.append(
                (
                    dot(jnp.concatenate(p00 + p10, 0), both_g, TN),
                    dot(jnp.concatenate(p11, 0), twice_g[1], TN),
                )
            )
        for n in range(3):
            common[n] += totals[n]
        first = step_id * group + 2 * k
        skip = jnp.where(left, skip_ref[first], skip_ref[first + 1])
        for j in range(2):
            rows = slice(j * BLOCK, (j + 1) * BLOCK)
            mixed_ref[rows, lanes] = (
                jnp.where(left, mixed_parts[0][j], mixed_parts[1][j]) + skip * xs[j].astype(F32)
            )
            gx_ref[rows, lanes] = (
                jnp.where(left, gx_parts[0][j], gx_parts[1][j]) + skip * gs[j].astype(F32)
            )

    @pl.when(step_id == pl.num_programs(0) - 1)
    def _():
        c00, c10, c11 = [split2(common[n]) for n in range(3)]
        b0, b1 = b_ref[:BLOCK], b_ref[BLOCK:]
        c0, c1 = c_ref[:BLOCK], c_ref[BLOCK:]
        grads_ref[0, :BLOCK] = sum(dot(v, c0, TN) for v in c00) + sum(dot(v, c1, TN) for v in c10)
        grads_ref[0, BLOCK:] = sum(dot(v, c1, TN) for v in c11)
        grads_ref[1, :BLOCK] = sum(dot(v, b0, NN) for v in c00)
        grads_ref[1, BLOCK:] = sum(dot(v, b0, NN) for v in c10) + sum(dot(v, b1, NN) for v in c11)


def place_state(core, own, other, high, low):
    half = own.shape[1]
    for part, first in ((own, core), (other, 1 - core)):
        rows = pl.ds(pl.multiple_of(first * half, half), half)
        for k in range(own.shape[0]):
            lanes = slice(k * LANES, (k + 1) * LANES)
            hi, lo = split2(part[k])
            high[rows, lanes] = hi
            low[rows, lanes] = lo


def grads_kernel(
    parts, core_ref, own_f, other_f, own_b, other_b, xh_ref, xl_ref, gh_ref, gl_ref, local_ref,
    out_ref, high, low, total,
):
    step_id = pl.program_id(0)

    @pl.when(step_id == 0)
    def _():
        total[...] = local_ref[...]

    for slot, own, other, vh, vl in (
        (0, own_b, other_b, xh_ref, xl_ref),
        (1, own_f, other_f, gh_ref, gl_ref),
    ):
        place_state(core_ref[0], own, other, high.at[slot], low.at[slot])
        hi, lo = high[slot], low[slot]
        first = vh[...]
        total[slot] += dot(first, hi, NT) + dot(first, lo, NT) + dot(vl[...], hi, NT)

    @pl.when(step_id == pl.num_programs(0) - 1)
    def _():
        rows = total.shape[1] // parts
        for k in range(parts):
            for slot in range(2):
                out_ref[k, slot] = total[slot, k * rows : (k + 1) * rows]


def output_kernel(
    group, width, core_ref, own, other, base_ref, coded_ref, proj_ref, out_ref, high, low
):
    place_state(core_ref[0], own, other, high, low)
    spread = expander(group, width)
    hi, lo = coded_ref[0, 0, 0], coded_ref[0, 0, 1]
    proj = proj_ref[...]
    for k in range(group * width // LANES):
        lanes = slice(k * LANES, (k + 1) * LANES)
        scale = dot(hi, spread[:, lanes], NN) + dot(lo, spread[:, lanes], NN)
        carried = dot(proj, high[:, lanes], NN) + dot(proj, low[:, lanes], NN)
        out_ref[:, lanes] = (base_ref[:, lanes] + scale * carried).astype(BF16)


def whole(shape):
    return pl.BlockSpec(shape, lambda i: (0,) * len(shape))


SMEM = pl.BlockSpec(memory_space=pltpu.SMEM)
HBM = pl.BlockSpec(memory_space=pltpu.HBM)
PARAMS = pltpu.CompilerParams(vmem_limit_bytes=24 << 20)


def swap_with(value, axis, mask):
    size = lax.axis_size(axis)
    return lax.ppermute(value, axis, [(i, i ^ mask) for i in range(size)])


def scan_chips(total_f, total_b, total_l, axis):
    size, index = lax.axis_size(axis), lax.axis_index(axis)
    before, after = jnp.zeros_like(total_f), jnp.zeros_like(total_b)
    log_before, log_after = jnp.zeros_like(total_l), jnp.zeros_like(total_l)
    bit = 2
    while bit < size:
        other_f, other_b, other_l = [swap_with(v, axis, bit) for v in (total_f, total_b, total_l)]
        upper = (index & bit) != 0
        before = jnp.where(upper, jnp.exp(log_before) * other_f + before, before)
        after = jnp.where(upper, after, jnp.exp(log_after) * other_b + after)
        log_before = jnp.where(upper, log_before + other_l, log_before)
        log_after = jnp.where(upper, log_after, log_after + other_l)
        scale, other_scale = jnp.exp(total_l), jnp.exp(other_l)
        total_f = jnp.where(upper, scale * other_f + total_f, other_scale * total_f + other_f)
        total_b = jnp.where(upper, other_b + other_scale * total_b, total_b + scale * other_b)
        total_l = jnp.maximum(total_l + other_l, NEVER)
        bit *= 2
    return before, after


def encode(state, bound, log_decay):
    power = jnp.clip(jnp.ceil(jnp.log2(bound)), -100.0, 120.0)
    data = state * jnp.exp2(14.0 - power)[:, None]
    first = lax.reduce_precision(log_decay, 5, 10)
    second = lax.reduce_precision(log_decay - first, 5, 10)
    third = lax.reduce_precision(log_decay - first - second, 5, 10)
    rows = [data.reshape(-1, LANES), first, second, third, power]
    return jnp.concatenate([v.astype(jnp.float16) for v in rows], 0)


def decode(coded, chunks):
    size = coded.shape[0] - 4 * chunks
    rows = [coded[size + k * chunks : size + (k + 1) * chunks].astype(F32) for k in range(4)]
    state = coded[:size].reshape(chunks, -1, LANES).astype(F32)
    return state * jnp.exp2(rows[3] - 14.0)[:, None], jnp.exp(rows[0] + rows[1] + rows[2])[:, None]


def chip_place(axis):
    index = lax.axis_index(axis)
    return (index >> 1) & 1, (index >> 2) & 1


def pack_chip(total_f, total_b, bound_f, bound_b, log_decay, axis):
    return [
        encode(
            jnp.where(first, total_f, total_b), jnp.where(first, bound_f, bound_b), log_decay
        )
        for first in [bit == 0 for bit in chip_place(axis)]
    ]


def join_chips(arrived, axis, chunks):
    x, y = chip_place(axis)
    (one, decay_one), (two, decay_two), (three, decay_three) = [decode(v, chunks) for v in arrived]
    same = x == y
    close = jnp.where(same, two, three)
    decay_close = jnp.where(same, decay_two, decay_three)
    distant = jnp.where(same, three, two)
    beyond = close + decay_close * distant
    main = jnp.where(same, one + decay_one * beyond, beyond)
    side = jnp.where(same, 0.0, one)
    upper = y == 1
    return jnp.where(upper, main, side), jnp.where(upper, side, main)


def shards(inputs, step_size, decay_rate, skip, b_in, c_in, doc_start, cotangent):
    heads, tokens = step_size.shape
    channels = inputs.shape[1]
    width = channels // heads
    state = b_in.shape[1]
    half = state // 2
    group = min(8, heads)
    groups = heads // group
    wide = group * width
    per = wide // LANES
    chunks = channels // LANES
    context, tensor = lax.axis_size("context"), lax.axis_size("tensor")
    core = lax.axis_index("context") & 1
    flag = core.reshape(1).astype(jnp.int32)
    decay = decay_rate.reshape(1, heads)
    doc = doc_start.reshape(1, tokens)

    tok = pl.BlockSpec((tokens, wide), lambda i: (0, i))
    piece = pl.BlockSpec((per, state, LANES), lambda i: (i, 0, 0))
    weights = pltpu.VMEM((2, groups, tokens, group), F32)
    mine, send, meta = pl.pallas_call(
        functools.partial(states_kernel, group, width),
        grid=(groups,),
        in_specs=[SMEM] + [HBM] * 7,
        out_specs=[piece, piece, whole((META, chunks, LANES))],
        out_shape=[jax.ShapeDtypeStruct((chunks, state, LANES), F32)] * 2
        + [jax.ShapeDtypeStruct((META, chunks, LANES), F32)],
        scratch_shapes=[
            pltpu.VMEM((groups, tokens, wide), BF16),
            pltpu.VMEM((groups, tokens, wide), BF16),
            pltpu.VMEM((heads, tokens), F32),
            pltpu.VMEM((1, heads), F32),
            pltpu.VMEM((1, tokens), jnp.int32),
            pltpu.VMEM((tokens, state), BF16),
            pltpu.VMEM((tokens, state), BF16),
            pltpu.VMEM((state, tokens), BF16),
            pltpu.VMEM((state, tokens), BF16),
            weights,
            pltpu.VMEM((groups, META, group), F32),
            pltpu.SemaphoreType.DMA((5,)),
            pltpu.SemaphoreType.DMA((2, groups)),
        ],
        compiler_params=PARAMS,
        name="states",
    )(flag, inputs, cotangent, step_size, decay, doc, b_in, c_in)

    theirs = swap_with(send, "context", 1)
    sib_meta = swap_with(meta, "context", 1)
    lower = core == 0
    own_f, own_b = mine[:, :half], mine[:, half:]
    sib_f, sib_b = theirs[:, :half], theirs[:, half:]
    own_l, own_e, own_mf, own_mb = [meta[k] for k in range(4)]
    sib_l, sib_e, sib_mf, sib_mb = [sib_meta[k] for k in range(4)]
    f_own, f_sib = jnp.where(lower, sib_e, 1.0), jnp.where(lower, 1.0, own_e)
    b_own, b_sib = jnp.where(lower, 1.0, sib_e), jnp.where(lower, own_e, 1.0)
    chip_f = f_own[:, None] * own_f + f_sib[:, None] * sib_f
    chip_b = b_own[:, None] * own_b + b_sib[:, None] * sib_b
    chip_l = jnp.maximum(own_l + sib_l, NEVER)
    if context == 8:
        near, far = pack_chip(
            chip_f,
            chip_b,
            f_own * own_mf + f_sib * sib_mf,
            b_own * own_mb + b_sib * sib_mb,
            chip_l,
            "context",
        )
        near, far, skip = lax.optimization_barrier((near, far, skip))
        arrived = [
            swap_with(near, "context", 2),
            swap_with(far, "context", 4),
            swap_with(far, "context", 6),
        ]

    full = jax.ShapeDtypeStruct((tokens, channels), F32)
    coded = jax.ShapeDtypeStruct((tokens, channels), BF16)
    mixed_loc, gx_loc, xh, xl, gh, gl, scales, grads_loc = pl.pallas_call(
        functools.partial(local_kernel, group, width),
        grid=(groups,),
        in_specs=[
            SMEM,
            tok,
            tok,
            whole((heads, tokens)),
            pl.BlockSpec((group, tokens), lambda i: (i, 0)),
            whole((1, heads)),
            whole((1, tokens)),
            whole((tokens, state)),
            whole((tokens, state)),
        ],
        out_specs=[tok] * 6
        + [
            pl.BlockSpec((2, 1, 2, tokens, group), lambda i: (0, i, 0, 0, 0)),
            whole((2, tokens, state)),
        ],
        out_shape=[full, full]
        + [coded] * 4
        + [
            jax.ShapeDtypeStruct((2, groups, 2, tokens, group), BF16),
            jax.ShapeDtypeStruct((2, tokens, state), F32),
        ],
        scratch_shapes=[
            weights,
            pltpu.VMEM((2, groups, BLOCK, group), F32),
            pltpu.VMEM((2, groups, group, BLOCK), F32),
            pltpu.VMEM((3, BLOCK, BLOCK), F32),
            pltpu.VMEM((3, BLOCK, BLOCK), F32),
            pltpu.VMEM((3, BLOCK, BLOCK), F32),
        ],
        compiler_params=PARAMS,
        cost_estimate=pl.CostEstimate(
            flops=20 * tokens * tokens * channels,
            transcendentals=heads * tokens * tokens,
            bytes_accessed=20 * tokens * channels,
        ),
        name="local",
    )(skip, inputs, cotangent, step_size, step_size, decay, doc, b_in, c_in)

    if context == 8:
        arrived, grads_loc = lax.optimization_barrier((arrived, grads_loc))
        before, after = join_chips(arrived, "context", chunks)
    else:
        before, after = scan_chips(chip_f, chip_b, chip_l[:, None], "context")

    own_e, sib_e = own_e[:, None], sib_e[:, None]
    other_f = swap_with(jnp.where(lower, own_e * before + own_f, before), "context", 1)
    other_b = swap_with(jnp.where(lower, after, own_b + own_e * after), "context", 1)
    enter_f = jnp.where(lower, before, sib_e * before + sib_f)
    enter_b = jnp.where(lower, sib_b + sib_e * after, after)

    parts = tensor if tokens % (8 * tensor) == 0 else 1
    state_spec = pl.BlockSpec((per, half, LANES), lambda i: (i, 0, 0))
    slots = [pltpu.VMEM((2, state, wide), BF16)] * 2
    grads = pl.pallas_call(
        functools.partial(grads_kernel, parts),
        grid=(groups,),
        in_specs=[SMEM] + [state_spec] * 4 + [tok] * 4 + [whole((2, tokens, state))],
        out_specs=whole((parts, 2, tokens // parts, state)),
        out_shape=jax.ShapeDtypeStruct((parts, 2, tokens // parts, state), F32),
        scratch_shapes=slots + [pltpu.VMEM((2, tokens, state), F32)],
        compiler_params=PARAMS,
        name="grads",
    )(flag, enter_f, other_f, enter_b, other_b, xh, xl, gh, gl, grads_loc)

    def finish(kind, first, own, other, base, proj, name):
        return pl.pallas_call(
            functools.partial(output_kernel, group, width),
            grid=(groups,),
            in_specs=[
                SMEM,
                state_spec,
                state_spec,
                tok,
                pl.BlockSpec((1, 1, 2, tokens, group), lambda i: (kind, i, 0, 0, 0)),
                whole((tokens, state)),
            ],
            out_specs=tok,
            out_shape=coded,
            scratch_shapes=[pltpu.VMEM((state, wide), BF16)] * 2,
            compiler_params=PARAMS,
            cost_estimate=pl.CostEstimate(
                flops=4 * tokens * state * channels,
                transcendentals=0,
                bytes_accessed=8 * tokens * channels,
            ),
            name=name,
        )(first, own, other, base, scales, proj)

    if tensor == 4 and parts == 4:
        place = lax.axis_index("tensor")
        pick = lambda at: lax.dynamic_index_in_dim(grads, at, 0, False)
        own, leaving = pick(place), [pick(place ^ k) for k in (2, 3, 1)]
        own, leaving, first = lax.optimization_barrier((own, leaving, flag))
        landed = [swap_with(v, "tensor", k) for k, v in zip((2, 3, 1), leaving)]
        mixed = finish(1, first, enter_f, other_f, mixed_loc, c_in, "mixed")
        landed, mixed = lax.optimization_barrier((landed, mixed))
        total = (own + landed[0] + landed[1] + landed[2]).astype(BF16)
        total, first = lax.optimization_barrier((total, first))
        landed = [swap_with(total, "tensor", k) for k in (2, 3, 1)]
        grad_inputs = finish(0, first, enter_b, other_b, gx_loc, b_in, "grad_inputs")
        landed, grad_inputs = lax.optimization_barrier((landed, grad_inputs))
        summed = jnp.zeros((parts,) + total.shape, BF16)
        summed = lax.dynamic_update_index_in_dim(summed, total, place, 0)
        for k, v in zip((2, 3, 1), landed):
            summed = lax.dynamic_update_index_in_dim(summed, v, place ^ k, 0)
    else:
        mixed = finish(1, flag, enter_f, other_f, mixed_loc, c_in, "mixed")
        grad_inputs = finish(0, flag, enter_b, other_b, gx_loc, b_in, "grad_inputs")
        summed = lax.psum(grads, "tensor").astype(BF16)
    grad_b = summed[:, 0].reshape(tokens, state)
    grad_c = summed[:, 1].reshape(tokens, state)
    return (mixed, grad_inputs, grad_b, grad_c)


def solution(mesh):
    in_specs = (
        P("context", "tensor"),
        P("tensor", "context"),
        P("tensor"),
        P("tensor"),
        P("context", None),
        P("context", None),
        P("context"),
        P("context", "tensor"),
    )
    out_specs = (
        P("context", "tensor"),
        P("context", "tensor"),
        P("context", None),
        P("context", None),
    )
    return jax.shard_map(shards, mesh=mesh, in_specs=in_specs, out_specs=out_specs, check_vma=False)
```

```python
import functools

import jax
import jax.numpy as jnp
from jax import lax
from jax.experimental import pallas as pl
from jax.experimental.pallas import tpu as pltpu
from jax.sharding import PartitionSpec as P

BLOCK = 128
LANES = 128
F32 = jnp.float32
BF16 = jnp.bfloat16
NEVER = -200.0
MASKED = -1e30
BOUND = 6.0 * 1.796875
META = 8

NN = (((1,), (0,)), ((), ()))
NT = (((1,), (1,)), ((), ()))
TN = (((0,), (0,)), ((), ()))


def dot(a, b, dims):
    return lax.dot_general(a, b, dims, preferred_element_type=F32)


def split2(x):
    hi = x.astype(BF16)
    lo = (x - hi.astype(F32)).astype(BF16)
    return hi, lo


def split3(x):
    hi = x.astype(BF16)
    rest = x - hi.astype(F32)
    mid = rest.astype(BF16)
    lo = (rest - mid.astype(F32)).astype(BF16)
    return hi, mid, lo


def iota(shape, axis):
    return lax.broadcasted_iota(jnp.int32, shape, axis)


def block_sums(step, decay, doc):
    log_decay = -step * decay
    tri = jnp.where(iota((BLOCK, BLOCK), 0) >= iota((BLOCK, BLOCK), 1), 1.0, 0.0).astype(BF16)
    out = []
    for first in range(0, step.shape[1], BLOCK):
        cols = slice(first, first + BLOCK)
        parts = split3(log_decay[:, cols])
        starts = jnp.broadcast_to(doc[:, cols].astype(F32), (16, BLOCK)).astype(BF16)
        down = functools.reduce(jnp.add, [dot(tri, part, NT) for part in parts])
        across = functools.reduce(jnp.add, [dot(part, tri, NT) for part in parts])
        count_down = dot(tri, starts, NT)[:, :1]
        count_across = dot(starts, tri, NT)[:1]
        out.append((down, across, count_down, count_across))
    return out


def edge_weights(step, sums):
    eye = jnp.where(iota((BLOCK, BLOCK), 0) == iota((BLOCK, BLOCK), 1), 1.0, 0.0).astype(BF16)
    blocks = len(sums)
    ends = [s[0][BLOCK - 1 :] for s in sums]
    counts = [s[2][BLOCK - 1 :] for s in sums]
    keep, last = [], []
    for k in range(blocks):
        down, _, count_down, _ = sums[k]
        sum_before = down
        starts_before = count_down
        sum_after = ends[k] - down
        starts_after = counts[k] - count_down
        for j in range(k):
            sum_before = sum_before + ends[j]
            starts_before = starts_before + counts[j]
        for j in range(k + 1, blocks):
            sum_after = sum_after + ends[j]
            starts_after = starts_after + counts[j]
        parts = split3(step[:, k * BLOCK : (k + 1) * BLOCK])
        step_down = functools.reduce(jnp.add, [dot(eye, part, NT) for part in parts])
        keep.append(jnp.where(starts_before == 0.0, jnp.exp(sum_before), 0.0))
        last.append(jnp.where(starts_after == 0.0, jnp.exp(sum_after) * step_down, 0.0))
    total = functools.reduce(jnp.add, ends)
    starts = functools.reduce(jnp.add, counts)
    total = jnp.where(starts == 0.0, jnp.maximum(total, NEVER), NEVER)
    return jnp.concatenate(keep, 0), jnp.concatenate(last, 0), total


def expander(heads, width):
    shape = (heads, heads * width)
    return jnp.where(iota(shape, 0) == iota(shape, 1) // width, 1.0, 0.0).astype(BF16)


def fetch(pairs, sems):
    copies = [pltpu.make_async_copy(src, dst, sems.at[k]) for k, (src, dst) in enumerate(pairs)]
    for copy in copies:
        copy.start()
    return copies


def column(row):
    shape = (row.shape[1], row.shape[1])
    spot = iota(shape, 0) == iota(shape, 1)
    return jnp.sum(jnp.where(spot, row, 0.0), axis=1, keepdims=True)


def states_kernel(
    group, width, core_ref, x_hbm, g_hbm, step_hbm, decay_hbm, doc_hbm, b_hbm, c_hbm,
    mine_ref, send_ref, meta_ref, x_ref, g_ref, step_ref, decay_ref, doc_ref, b_ref, c_ref,
    b_t, c_t, weights, meta, small_sems, big_sems,
):
    step_id = pl.program_id(0)
    groups = weights.shape[1]
    half = b_t.shape[0] // 2
    wide = group * width
    chunks = wide // LANES

    def big(k):
        return [
            pltpu.make_async_copy(
                src.at[:, pl.ds(pl.multiple_of(k * wide, LANES), wide)], dst.at[k], big_sems.at[n, k]
            )
            for n, (src, dst) in enumerate(((x_hbm, x_ref), (g_hbm, g_ref)))
        ]

    @pl.when(step_id == 0)
    def _():
        small = fetch(
            (
                (step_hbm, step_ref),
                (decay_hbm, decay_ref),
                (doc_hbm, doc_ref),
                (b_hbm, b_ref),
                (c_hbm, c_ref),
            ),
            small_sems,
        )
        for k in range(groups):
            for copy in big(k):
                copy.start()
        for copy in small:
            copy.wait()
        swap = core_ref[0] == 1
        step = step_ref[...]
        sums = block_sums(step, column(decay_ref[...]), doc_ref[...])
        keep, last, total = edge_weights(step, sums)
        bound_f = BOUND * jnp.sum(last, axis=0, keepdims=True)
        bound_b = BOUND * jnp.sum(keep, axis=0, keepdims=True)
        rows = [total, jnp.exp(total), bound_f, bound_b]
        rows = jnp.concatenate(rows + [jnp.zeros((META - 4, total.shape[1]), F32)], 0)
        for k in range(groups):
            heads = slice(k * group, (k + 1) * group)
            weights[0, k] = last[:, heads]
            weights[1, k] = keep[:, heads]
            meta[k] = rows[:, heads]
        for ref, out in ((b_ref, b_t), (c_ref, c_t)):
            turned = ref[...].astype(F32).T
            swapped = jnp.concatenate([turned[half:], turned[:half]], 0)
            out[...] = jnp.where(swap, swapped, turned).astype(BF16)

    for copy in big(step_id):
        copy.wait()
    spread = expander(group, width)
    rows = functools.reduce(jnp.add, [dot(p, spread, NN) for p in split3(meta[step_id])])
    for k in range(chunks):
        for n in range(META):
            meta_ref[n, pl.ds(step_id * chunks + k, 1)] = rows[n : n + 1, k * LANES : (k + 1) * LANES]
    for kind, (ref, turned) in enumerate(((x_ref, b_t), (g_ref, c_t))):
        hi, lo = split2(weights[kind, step_id])
        turned = turned[...]
        for k in range(chunks):
            lanes = slice(k * LANES, (k + 1) * LANES)
            scale = dot(hi, spread[:, lanes], NN) + dot(lo, spread[:, lanes], NN)
            scaled = split2(ref[step_id, :, lanes].astype(F32) * scale)
            state = dot(turned, scaled[0], NN) + dot(turned, scaled[1], NN)
            mine_ref[k, kind * half : (kind + 1) * half] = state[:half]
            send_ref[k, kind * half : (kind + 1) * half] = state[half:]


def local_kernel(
    group, width, skip_ref, x_ref, g_ref, step_ref, step_blk, decay_ref, doc_ref, b_ref, c_ref,
    mixed_ref, gx_ref, xh_ref, xl_ref, gh_ref, gl_ref, coded_ref, grads_ref,
    weights, down_s, across_s, bias, inter, common,
):
    step_id = pl.program_id(0)
    groups = weights.shape[1]
    pairs = ((0, 0), (1, 0), (1, 1))

    @pl.when(step_id == 0)
    def _():
        step = step_ref[...]
        sums = block_sums(step, column(decay_ref[...]), doc_ref[...])
        keep, last, _ = edge_weights(step, sums)
        for k in range(groups):
            heads = slice(k * group, (k + 1) * group)
            weights[0, k] = last[:, heads]
            weights[1, k] = keep[:, heads]
            for j in range(2):
                down_s[j, k] = sums[j][0][:, heads]
                across_s[j, k] = sums[j][1][heads]
        for n, (t, s) in enumerate(pairs):
            if t == s:
                ok = sums[t][2] == sums[s][3]
                ok = ok & (iota((BLOCK, BLOCK), 0) >= iota((BLOCK, BLOCK), 1))
            else:
                ok = sums[t][2] == sums[s][3] - sums[s][3][:, BLOCK - 1 :]
            bias[n] = jnp.where(ok, 0.0, MASKED)
            inter[n] = dot(
                c_ref[t * BLOCK : (t + 1) * BLOCK], b_ref[s * BLOCK : (s + 1) * BLOCK], NT
            )
        common[...] = jnp.zeros_like(common)

    spread = expander(group, width)
    for ref, high, low, kind in ((x_ref, xh_ref, xl_ref, 0), (g_ref, gh_ref, gl_ref, 1)):
        hi, lo = split2(weights[kind, step_id])
        coded_ref[kind, 0, 0] = hi
        coded_ref[kind, 0, 1] = lo
        for k in range(group * width // LANES):
            lanes = slice(k * LANES, (k + 1) * LANES)
            scale = dot(hi, spread[:, lanes], NN) + dot(lo, spread[:, lanes], NN)
            scaled = split2(ref[:, lanes].astype(F32) * scale)
            high[:, lanes] = scaled[0]
            low[:, lanes] = scaled[1]

    down = [down_s[j, step_id] for j in range(2)]
    across = [across_s[j, step_id] for j in range(2)]
    left = iota((BLOCK, LANES), 1) < width
    left2 = iota((2 * BLOCK, LANES), 1) < width
    for k in range(group * width // LANES):
        lanes = slice(k * LANES, (k + 1) * LANES)
        xs = [x_ref[j * BLOCK : (j + 1) * BLOCK, lanes] for j in range(2)]
        gs = [g_ref[j * BLOCK : (j + 1) * BLOCK, lanes] for j in range(2)]
        zero = jnp.zeros_like(gs[0])
        halves = [
            jnp.concatenate([jnp.where(left, v, zero), jnp.where(left, zero, v)], 0) for v in gs
        ]
        inner = [dot(halves[t], xs[s], NT) for t, s in pairs]
        twice_x = [jnp.concatenate([v, v], 0) for v in xs]
        twice_g = [jnp.concatenate([v, v], 0) for v in gs]
        both_x = jnp.concatenate(twice_x, 0)
        both_g = jnp.concatenate(twice_g, 0)
        mixed_parts, gx_parts = [], []
        totals = [None] * 3
        for e in range(2):
            h = 2 * k + e
            parts = []
            for n, (t, s) in enumerate(pairs):
                row = across[s][h : h + 1]
                if t != s:
                    row = row - row[:, BLOCK - 1 :]
                weight = jnp.exp((down[t][:, h : h + 1] + bias[n]) - row)
                weight = weight * step_blk[h : h + 1, s * BLOCK : (s + 1) * BLOCK]
                term = weight * inner[n][e * BLOCK : (e + 1) * BLOCK]
                totals[n] = term if e == 0 else totals[n] + term
                parts.append(split2(weight * inter[n]))
            p00, p10, p11 = parts
            mixed_parts.append(
                (
                    dot(jnp.concatenate(p00, 1), twice_x[0], NN),
                    dot(jnp.concatenate(p10 + p11, 1), both_x, NN),
                )
            )
            gx_parts.append(
                (
                    dot(jnp.concatenate(p00 + p10, 0), both_g, TN),
                    dot(jnp.concatenate(p11, 0), twice_g[1], TN),
                )
            )
        for n in range(3):
            common[n] += totals[n]
        first = step_id * group + 2 * k
        skip = jnp.where(left, skip_ref[first], skip_ref[first + 1])
        for j in range(2):
            rows = slice(j * BLOCK, (j + 1) * BLOCK)
            mixed_ref[rows, lanes] = (
                jnp.where(left, mixed_parts[0][j], mixed_parts[1][j]) + skip * xs[j].astype(F32)
            )
            gx_ref[rows, lanes] = (
                jnp.where(left, gx_parts[0][j], gx_parts[1][j]) + skip * gs[j].astype(F32)
            )

    @pl.when(step_id == pl.num_programs(0) - 1)
    def _():
        c00, c10, c11 = [split2(common[n]) for n in range(3)]
        b0, b1 = b_ref[:BLOCK], b_ref[BLOCK:]
        c0, c1 = c_ref[:BLOCK], c_ref[BLOCK:]
        grads_ref[0, :BLOCK] = sum(dot(v, c0, TN) for v in c00) + sum(dot(v, c1, TN) for v in c10)
        grads_ref[0, BLOCK:] = sum(dot(v, c1, TN) for v in c11)
        grads_ref[1, :BLOCK] = sum(dot(v, b0, NN) for v in c00)
        grads_ref[1, BLOCK:] = sum(dot(v, b0, NN) for v in c10) + sum(dot(v, b1, NN) for v in c11)


def place_state(core, own, other, high, low):
    half = own.shape[1]
    for part, first in ((own, core), (other, 1 - core)):
        rows = pl.ds(pl.multiple_of(first * half, half), half)
        for k in range(own.shape[0]):
            lanes = slice(k * LANES, (k + 1) * LANES)
            hi, lo = split2(part[k])
            high[rows, lanes] = hi
            low[rows, lanes] = lo


def grads_kernel(
    parts, core_ref, own_f, other_f, own_b, other_b, xh_ref, xl_ref, gh_ref, gl_ref, local_ref,
    out_ref, high, low, total,
):
    step_id = pl.program_id(0)

    @pl.when(step_id == 0)
    def _():
        total[...] = local_ref[...]

    for slot, own, other, vh, vl in (
        (0, own_b, other_b, xh_ref, xl_ref),
        (1, own_f, other_f, gh_ref, gl_ref),
    ):
        place_state(core_ref[0], own, other, high.at[slot], low.at[slot])
        hi, lo = high[slot], low[slot]
        first = vh[...]
        total[slot] += dot(first, hi, NT) + dot(first, lo, NT) + dot(vl[...], hi, NT)

    @pl.when(step_id == pl.num_programs(0) - 1)
    def _():
        rows = total.shape[1] // parts
        for k in range(parts):
            for slot in range(2):
                out_ref[k, slot] = total[slot, k * rows : (k + 1) * rows]


def output_kernel(
    group, width, core_ref, own, other, base_ref, coded_ref, proj_ref, out_ref, high, low
):
    place_state(core_ref[0], own, other, high, low)
    spread = expander(group, width)
    hi, lo = coded_ref[0, 0, 0], coded_ref[0, 0, 1]
    proj = proj_ref[...]
    for k in range(group * width // LANES):
        lanes = slice(k * LANES, (k + 1) * LANES)
        scale = dot(hi, spread[:, lanes], NN) + dot(lo, spread[:, lanes], NN)
        carried = dot(proj, high[:, lanes], NN) + dot(proj, low[:, lanes], NN)
        out_ref[:, lanes] = (base_ref[:, lanes] + scale * carried).astype(BF16)


def whole(shape):
    return pl.BlockSpec(shape, lambda i: (0,) * len(shape))


SMEM = pl.BlockSpec(memory_space=pltpu.SMEM)
HBM = pl.BlockSpec(memory_space=pltpu.HBM)
PARAMS = pltpu.CompilerParams(vmem_limit_bytes=60 << 20)


def swap_with(value, axis, mask):
    size = lax.axis_size(axis)
    return lax.ppermute(value, axis, [(i, i ^ mask) for i in range(size)])


def scan_chips(total_f, total_b, total_l, axis):
    size, index = lax.axis_size(axis), lax.axis_index(axis)
    before, after = jnp.zeros_like(total_f), jnp.zeros_like(total_b)
    log_before, log_after = jnp.zeros_like(total_l), jnp.zeros_like(total_l)
    bit = 2
    while bit < size:
        other_f, other_b, other_l = [swap_with(v, axis, bit) for v in (total_f, total_b, total_l)]
        upper = (index & bit) != 0
        before = jnp.where(upper, jnp.exp(log_before) * other_f + before, before)
        after = jnp.where(upper, after, jnp.exp(log_after) * other_b + after)
        log_before = jnp.where(upper, log_before + other_l, log_before)
        log_after = jnp.where(upper, log_after, log_after + other_l)
        scale, other_scale = jnp.exp(total_l), jnp.exp(other_l)
        total_f = jnp.where(upper, scale * other_f + total_f, other_scale * total_f + other_f)
        total_b = jnp.where(upper, other_b + other_scale * total_b, total_b + scale * other_b)
        total_l = jnp.maximum(total_l + other_l, NEVER)
        bit *= 2
    return before, after


def encode(state, bound, log_decay):
    power = jnp.clip(jnp.ceil(jnp.log2(bound)), -100.0, 120.0)
    data = state * jnp.exp2(14.0 - power)[:, None]
    first = lax.reduce_precision(log_decay, 5, 10)
    second = lax.reduce_precision(log_decay - first, 5, 10)
    third = lax.reduce_precision(log_decay - first - second, 5, 10)
    rows = [data.reshape(-1, LANES), first, second, third, power]
    return jnp.concatenate([v.astype(jnp.float16) for v in rows], 0)


def decode(coded, chunks):
    size = coded.shape[0] - 4 * chunks
    rows = [coded[size + k * chunks : size + (k + 1) * chunks].astype(F32) for k in range(4)]
    state = coded[:size].reshape(chunks, -1, LANES)
    return state, jnp.exp2(rows[3] - 14.0), jnp.exp(rows[0] + rows[1] + rows[2])


def chip_place(axis):
    index = lax.axis_index(axis)
    return (index >> 1) & 1, (index >> 2) & 1


def pack_chip(total_f, total_b, bound_f, bound_b, log_decay, axis):
    return [
        encode(
            jnp.where(first, total_f, total_b), jnp.where(first, bound_f, bound_b), log_decay
        )
        for first in [bit == 0 for bit in chip_place(axis)]
    ]


def join_chips(arrived, axis, chunks):
    x, y = chip_place(axis)
    states, scales, decays = zip(*[decode(v, chunks) for v in arrived])
    _, two, three = decays
    same, upper = x == y, y == 1
    beyond = jnp.where(same, decays[0], 1.0)
    weights = [
        jnp.ones_like(two),
        beyond * jnp.where(same, 1.0, three),
        beyond * jnp.where(same, two, 1.0),
    ]
    weights = [w * scale for w, scale in zip(weights, scales)]
    main = [jnp.where(same, weights[0], 0.0)] + weights[1:]
    side = [jnp.where(same, 0.0, weights[0]), 0.0, 0.0]
    before = [jnp.where(upper, m, s) for m, s in zip(main, side)]
    after = [jnp.where(upper, s, m) for m, s in zip(main, side)]
    return states, before, after


def weigh(terms):
    return functools.reduce(jnp.add, [w[:, None] * v.astype(F32) for w, v in terms])


def shards(inputs, step_size, decay_rate, skip, b_in, c_in, doc_start, cotangent):
    heads, tokens = step_size.shape
    channels = inputs.shape[1]
    width = channels // heads
    state = b_in.shape[1]
    half = state // 2
    group = min(8, heads)
    groups = heads // group
    wide = group * width
    per = wide // LANES
    chunks = channels // LANES
    context, tensor = lax.axis_size("context"), lax.axis_size("tensor")
    core = lax.axis_index("context") & 1
    flag = core.reshape(1).astype(jnp.int32)
    decay = decay_rate.reshape(1, heads)
    doc = doc_start.reshape(1, tokens)

    tok = pl.BlockSpec((tokens, wide), lambda i: (0, i))
    piece = pl.BlockSpec((per, state, LANES), lambda i: (i, 0, 0))
    weights = pltpu.VMEM((2, groups, tokens, group), F32)
    mine, send, meta = pl.pallas_call(
        functools.partial(states_kernel, group, width),
        grid=(groups,),
        in_specs=[SMEM] + [HBM] * 7,
        out_specs=[piece, piece, whole((META, chunks, LANES))],
        out_shape=[jax.ShapeDtypeStruct((chunks, state, LANES), F32)] * 2
        + [jax.ShapeDtypeStruct((META, chunks, LANES), F32)],
        scratch_shapes=[
            pltpu.VMEM((groups, tokens, wide), BF16),
            pltpu.VMEM((groups, tokens, wide), BF16),
            pltpu.VMEM((heads, tokens), F32),
            pltpu.VMEM((1, heads), F32),
            pltpu.VMEM((1, tokens), jnp.int32),
            pltpu.VMEM((tokens, state), BF16),
            pltpu.VMEM((tokens, state), BF16),
            pltpu.VMEM((state, tokens), BF16),
            pltpu.VMEM((state, tokens), BF16),
            weights,
            pltpu.VMEM((groups, META, group), F32),
            pltpu.SemaphoreType.DMA((5,)),
            pltpu.SemaphoreType.DMA((2, groups)),
        ],
        compiler_params=PARAMS,
        name="states",
    )(flag, inputs, cotangent, step_size, decay, doc, b_in, c_in)

    theirs = swap_with(send, "context", 1)
    sib_meta = swap_with(meta, "context", 1)
    lower = core == 0
    own_f, own_b = mine[:, :half], mine[:, half:]
    sib_f, sib_b = theirs[:, :half], theirs[:, half:]
    own_l, own_e, own_mf, own_mb = [meta[k] for k in range(4)]
    sib_l, sib_e, sib_mf, sib_mb = [sib_meta[k] for k in range(4)]
    f_own, f_sib = jnp.where(lower, sib_e, 1.0), jnp.where(lower, 1.0, own_e)
    b_own, b_sib = jnp.where(lower, 1.0, sib_e), jnp.where(lower, own_e, 1.0)
    chip_f = f_own[:, None] * own_f + f_sib[:, None] * sib_f
    chip_b = b_own[:, None] * own_b + b_sib[:, None] * sib_b
    chip_l = jnp.maximum(own_l + sib_l, NEVER)
    if context == 8:
        near, far = pack_chip(
            chip_f,
            chip_b,
            f_own * own_mf + f_sib * sib_mf,
            b_own * own_mb + b_sib * sib_mb,
            chip_l,
            "context",
        )
        near, far, skip = lax.optimization_barrier((near, far, skip))
        arrived = [
            swap_with(near, "context", 2),
            swap_with(far, "context", 4),
            swap_with(far, "context", 6),
        ]

    full = jax.ShapeDtypeStruct((tokens, channels), F32)
    coded = jax.ShapeDtypeStruct((tokens, channels), BF16)
    mixed_loc, gx_loc, xh, xl, gh, gl, scales, grads_loc = pl.pallas_call(
        functools.partial(local_kernel, group, width),
        grid=(groups,),
        in_specs=[
            SMEM,
            tok,
            tok,
            whole((heads, tokens)),
            pl.BlockSpec((group, tokens), lambda i: (i, 0)),
            whole((1, heads)),
            whole((1, tokens)),
            whole((tokens, state)),
            whole((tokens, state)),
        ],
        out_specs=[tok] * 6
        + [
            pl.BlockSpec((2, 1, 2, tokens, group), lambda i: (0, i, 0, 0, 0)),
            whole((2, tokens, state)),
        ],
        out_shape=[full, full]
        + [coded] * 4
        + [
            jax.ShapeDtypeStruct((2, groups, 2, tokens, group), BF16),
            jax.ShapeDtypeStruct((2, tokens, state), F32),
        ],
        scratch_shapes=[
            weights,
            pltpu.VMEM((2, groups, BLOCK, group), F32),
            pltpu.VMEM((2, groups, group, BLOCK), F32),
            pltpu.VMEM((3, BLOCK, BLOCK), F32),
            pltpu.VMEM((3, BLOCK, BLOCK), F32),
            pltpu.VMEM((3, BLOCK, BLOCK), F32),
        ],
        compiler_params=PARAMS,
        cost_estimate=pl.CostEstimate(
            flops=20 * tokens * tokens * channels,
            transcendentals=heads * tokens * tokens,
            bytes_accessed=20 * tokens * channels,
        ),
        name="local",
    )(skip, inputs, cotangent, step_size, step_size, decay, doc, b_in, c_in)

    one, zero = jnp.ones_like(own_e), jnp.zeros_like(own_e)
    if context == 8:
        arrived, grads_loc = lax.optimization_barrier((arrived, grads_loc))
        states, before, after = join_chips(arrived, "context", chunks)
    else:
        states = scan_chips(chip_f, chip_b, chip_l[:, None], "context")
        before, after = [one, zero], [zero, one]
    pass_f = jnp.where(lower, own_e, 1.0)
    pass_b = jnp.where(lower, 1.0, own_e)
    keep_f = jnp.where(lower, 1.0, sib_e)
    keep_b = jnp.where(lower, sib_e, 1.0)
    at_lower = jnp.where(lower, one, zero)
    at_upper = jnp.where(lower, zero, one)
    weights = (
        [pass_f * w for w in before],
        [pass_b * w for w in after],
        [keep_f * w for w in before],
        [keep_b * w for w in after],
    )
    passed_f = weigh([*zip(weights[0], states), (at_lower, own_f)])
    passed_b = weigh([*zip(weights[1], states), (at_upper, own_b)])
    passed_f, passed_b, weights, states = lax.optimization_barrier(
        (passed_f, passed_b, weights, states)
    )
    other_f = swap_with(passed_f, "context", 1)
    other_b = swap_with(passed_b, "context", 1)
    enter_f = weigh([*zip(weights[2], states), (at_upper, sib_f)])
    enter_b = weigh([*zip(weights[3], states), (at_lower, sib_b)])

    parts = tensor if tokens % (8 * tensor) == 0 else 1
    state_spec = pl.BlockSpec((per, half, LANES), lambda i: (i, 0, 0))
    slots = [pltpu.VMEM((2, state, wide), BF16)] * 2
    grads = pl.pallas_call(
        functools.partial(grads_kernel, parts),
        grid=(groups,),
        in_specs=[SMEM] + [state_spec] * 4 + [tok] * 4 + [whole((2, tokens, state))],
        out_specs=whole((parts, 2, tokens // parts, state)),
        out_shape=jax.ShapeDtypeStruct((parts, 2, tokens // parts, state), F32),
        scratch_shapes=slots + [pltpu.VMEM((2, tokens, state), F32)],
        compiler_params=PARAMS,
        name="grads",
    )(flag, enter_f, other_f, enter_b, other_b, xh, xl, gh, gl, grads_loc)

    def finish(kind, first, own, other, base, proj, name):
        return pl.pallas_call(
            functools.partial(output_kernel, group, width),
            grid=(groups,),
            in_specs=[
                SMEM,
                state_spec,
                state_spec,
                tok,
                pl.BlockSpec((1, 1, 2, tokens, group), lambda i: (kind, i, 0, 0, 0)),
                whole((tokens, state)),
            ],
            out_specs=tok,
            out_shape=coded,
            scratch_shapes=[pltpu.VMEM((state, wide), BF16)] * 2,
            compiler_params=PARAMS,
            cost_estimate=pl.CostEstimate(
                flops=4 * tokens * state * channels,
                transcendentals=0,
                bytes_accessed=8 * tokens * channels,
            ),
            name=name,
        )(first, own, other, base, scales, proj)

    if tensor == 4 and parts == 4:
        place = lax.axis_index("tensor")
        pick = lambda at: lax.dynamic_index_in_dim(grads, at, 0, False)
        own, leaving = pick(place), [pick(place ^ k) for k in (2, 3, 1)]
        own, leaving, first = lax.optimization_barrier((own, leaving, flag))
        landed = [swap_with(v, "tensor", k) for k, v in zip((2, 3, 1), leaving)]
        mixed = finish(1, first, enter_f, other_f, mixed_loc, c_in, "mixed")
        landed, mixed = lax.optimization_barrier((landed, mixed))
        total = (own + landed[0] + landed[1] + landed[2]).astype(BF16)
        total, first = lax.optimization_barrier((total, first))
        landed = [swap_with(total, "tensor", k) for k in (2, 3, 1)]
        grad_inputs = finish(0, first, enter_b, other_b, gx_loc, b_in, "grad_inputs")
        landed, grad_inputs = lax.optimization_barrier((landed, grad_inputs))
        summed = jnp.zeros((parts,) + total.shape, BF16)
        summed = lax.dynamic_update_index_in_dim(summed, total, place, 0)
        for k, v in zip((2, 3, 1), landed):
            summed = lax.dynamic_update_index_in_dim(summed, v, place ^ k, 0)
    else:
        mixed = finish(1, flag, enter_f, other_f, mixed_loc, c_in, "mixed")
        grad_inputs = finish(0, flag, enter_b, other_b, gx_loc, b_in, "grad_inputs")
        summed = lax.psum(grads, "tensor").astype(BF16)
    grad_b = summed[:, 0].reshape(tokens, state)
    grad_c = summed[:, 1].reshape(tokens, state)
    return (mixed, grad_inputs, grad_b, grad_c)


def solution(mesh):
    in_specs = (
        P("context", "tensor"),
        P("tensor", "context"),
        P("tensor"),
        P("tensor"),
        P("context", None),
        P("context", None),
        P("context"),
        P("context", "tensor"),
    )
    out_specs = (
        P("context", "tensor"),
        P("context", "tensor"),
        P("context", None),
        P("context", None),
    )
    return jax.shard_map(shards, mesh=mesh, in_specs=in_specs, out_specs=out_specs, check_vma=False)
```

```python
import functools

import jax
import jax.numpy as jnp
from jax import lax
from jax.experimental import pallas as pl
from jax.experimental.pallas import tpu as pltpu
from jax.sharding import PartitionSpec as P

BLOCK = 128
LANES = 128
F32 = jnp.float32
BF16 = jnp.bfloat16
NEVER = -200.0
MASKED = -1e30
BOUND = 6.0 * 1.796875
META = 8
STATES_VMEM, LOCAL_VMEM, GRADS_VMEM, OUTPUT_VMEM = 62, 60, 48, 60

NN = (((1,), (0,)), ((), ()))
NT = (((1,), (1,)), ((), ()))
TN = (((0,), (0,)), ((), ()))


def dot(a, b, dims):
    return lax.dot_general(a, b, dims, preferred_element_type=F32)


def split2(x):
    hi = x.astype(BF16)
    lo = (x - hi.astype(F32)).astype(BF16)
    return hi, lo


def split3(x):
    hi = x.astype(BF16)
    rest = x - hi.astype(F32)
    mid = rest.astype(BF16)
    lo = (rest - mid.astype(F32)).astype(BF16)
    return hi, mid, lo


def iota(shape, axis):
    return lax.broadcasted_iota(jnp.int32, shape, axis)


def block_sums(step, decay, doc):
    log_decay = -step * decay
    tri = jnp.where(iota((BLOCK, BLOCK), 0) >= iota((BLOCK, BLOCK), 1), 1.0, 0.0).astype(BF16)
    out = []
    for first in range(0, step.shape[1], BLOCK):
        cols = slice(first, first + BLOCK)
        parts = split3(log_decay[:, cols])
        starts = jnp.broadcast_to(doc[:, cols].astype(F32), (16, BLOCK)).astype(BF16)
        down = functools.reduce(jnp.add, [dot(tri, part, NT) for part in parts])
        across = functools.reduce(jnp.add, [dot(part, tri, NT) for part in parts])
        count_down = dot(tri, starts, NT)[:, :1]
        count_across = dot(starts, tri, NT)[:1]
        out.append((down, across, count_down, count_across))
    return out


def edge_weights(step, sums):
    eye = jnp.where(iota((BLOCK, BLOCK), 0) == iota((BLOCK, BLOCK), 1), 1.0, 0.0).astype(BF16)
    blocks = len(sums)
    ends = [s[0][BLOCK - 1 :] for s in sums]
    counts = [s[2][BLOCK - 1 :] for s in sums]
    keep, last = [], []
    for k in range(blocks):
        down, _, count_down, _ = sums[k]
        sum_before = down
        starts_before = count_down
        sum_after = ends[k] - down
        starts_after = counts[k] - count_down
        for j in range(k):
            sum_before = sum_before + ends[j]
            starts_before = starts_before + counts[j]
        for j in range(k + 1, blocks):
            sum_after = sum_after + ends[j]
            starts_after = starts_after + counts[j]
        parts = split3(step[:, k * BLOCK : (k + 1) * BLOCK])
        step_down = functools.reduce(jnp.add, [dot(eye, part, NT) for part in parts])
        keep.append(jnp.where(starts_before == 0.0, jnp.exp(sum_before), 0.0))
        last.append(jnp.where(starts_after == 0.0, jnp.exp(sum_after) * step_down, 0.0))
    total = functools.reduce(jnp.add, ends)
    starts = functools.reduce(jnp.add, counts)
    total = jnp.where(starts == 0.0, jnp.maximum(total, NEVER), NEVER)
    return jnp.concatenate(keep, 0), jnp.concatenate(last, 0), total


def spread_rows(rows, first, width, columns, skipped):
    heads = rows // 4
    row = iota((rows, 1), 0) - skipped * heads
    head = jnp.where(row >= heads, row - heads, row)
    head = jnp.where((row >= 0) & (row < 2 * heads), head, -rows * rows)
    offset = iota((1, columns), 1) - (head - first) * width
    return jnp.where((offset >= 0) & (offset < width), 1.0, 0.0).astype(BF16)


def last_spread(rows, first, width, columns):
    return spread_rows(rows, first, width, columns, 0)


def keep_spread(rows, first, width, columns):
    return spread_rows(rows, first, width, columns, 2)


SPREADS = (last_spread, keep_spread)


def pieces(total, most=256):
    return [slice(k, min(k + most, total)) for k in range(0, total, most)]


def fetch(pairs, sems):
    copies = [pltpu.make_async_copy(src, dst, sems.at[k]) for k, (src, dst) in enumerate(pairs)]
    for copy in copies:
        copy.start()
    return copies


def column(row):
    shape = (row.shape[1], row.shape[1])
    spot = iota(shape, 0) == iota(shape, 1)
    return jnp.sum(jnp.where(spot, row, 0.0), axis=1, keepdims=True)


def states_kernel(
    group, width, core_ref, x_hbm, g_hbm, step_hbm, decay_hbm, doc_hbm, b_hbm, c_hbm,
    mine_ref, send_ref, meta_ref, edges_ref, x_ref, g_ref, step_ref, decay_ref, doc_ref, b_ref,
    c_ref, b_t, c_t, meta, small_sems, big_sems,
):
    step_id = pl.program_id(0)
    groups = x_ref.shape[0]
    half = b_t.shape[0] // 2
    wide = group * width
    chunks = wide // LANES

    def big(k):
        return [
            pltpu.make_async_copy(
                src.at[:, pl.ds(pl.multiple_of(k * wide, LANES), wide)], dst.at[k], big_sems.at[n, k]
            )
            for n, (src, dst) in enumerate(((x_hbm, x_ref), (g_hbm, g_ref)))
        ]

    @pl.when(step_id == 0)
    def _():
        small = fetch(
            (
                (step_hbm, step_ref),
                (decay_hbm, decay_ref),
                (doc_hbm, doc_ref),
                (b_hbm, b_ref),
                (c_hbm, c_ref),
            ),
            small_sems,
        )
        for k in range(groups):
            for copy in big(k):
                copy.start()
        for copy in small:
            copy.wait()
        swap = core_ref[0] == 1
        step = step_ref[...]
        sums = block_sums(step, column(decay_ref[...]), doc_ref[...])
        keep, last, total = edge_weights(step, sums)
        bound_f = BOUND * jnp.sum(last, axis=0, keepdims=True)
        bound_b = BOUND * jnp.sum(keep, axis=0, keepdims=True)
        rows = [total, jnp.exp(total), bound_f, bound_b]
        rows = jnp.concatenate(rows + [jnp.zeros((META - 4, total.shape[1]), F32)], 0)
        high, mid, low = split3(rows)
        meta[...] = jnp.concatenate([high, mid, low, jnp.zeros_like(high)], 1)
        edges_ref[...] = jnp.concatenate(split2(last) + split2(keep), 1)
        for ref, out in ((b_ref, b_t), (c_ref, c_t)):
            turned = ref[...].astype(F32).T
            swapped = jnp.concatenate([turned[half:], turned[:half]], 0)
            out[...] = jnp.where(swap, swapped, turned).astype(BF16)

    for copy in big(step_id):
        copy.wait()
    edges = edges_ref[...]
    spreads = [make(edges.shape[1], step_id * group, width, wide) for make in SPREADS]
    rows = dot(meta[...], spreads[0] + spreads[1], NN)
    for k in range(chunks):
        for n in range(META):
            meta_ref[n, pl.ds(step_id * chunks + k, 1)] = rows[n : n + 1, k * LANES : (k + 1) * LANES]
    for kind, (ref, turned) in enumerate(((x_ref, b_t), (g_ref, c_t))):
        turned = turned[...]
        for lanes in pieces(wide):
            scale = dot(edges, spreads[kind][:, lanes], NN)
            scaled = split2(ref[step_id, :, lanes].astype(F32) * scale)
            state = dot(turned, scaled[0], NN) + dot(turned, scaled[1], NN)
            for k in range(state.shape[1] // LANES):
                part = state[:, k * LANES : (k + 1) * LANES]
                at = lanes.start // LANES + k
                mine_ref[at, kind * half : (kind + 1) * half] = part[:half]
                send_ref[at, kind * half : (kind + 1) * half] = part[half:]


def local_kernel(
    group, width, skip_ref, x_ref, g_ref, step_ref, step_blk, decay_ref, doc_ref, b_ref, c_ref,
    mixed_ref, gx_ref, grads_ref, down_s, across_s, bias, inter, common,
):
    step_id = pl.program_id(0)
    groups = down_s.shape[1]
    pairs = ((0, 0), (1, 0), (1, 1))

    @pl.when(step_id == 0)
    def _():
        step = step_ref[...]
        sums = block_sums(step, column(decay_ref[...]), doc_ref[...])
        for k in range(groups):
            heads = slice(k * group, (k + 1) * group)
            for j in range(2):
                down_s[j, k] = sums[j][0][:, heads]
                across_s[j, k] = sums[j][1][heads]
        for n, (t, s) in enumerate(pairs):
            if t == s:
                ok = sums[t][2] == sums[s][3]
                ok = ok & (iota((BLOCK, BLOCK), 0) >= iota((BLOCK, BLOCK), 1))
            else:
                ok = sums[t][2] == sums[s][3] - sums[s][3][:, BLOCK - 1 :]
            bias[n] = jnp.where(ok, 0.0, MASKED)
            inter[n] = dot(
                c_ref[t * BLOCK : (t + 1) * BLOCK], b_ref[s * BLOCK : (s + 1) * BLOCK], NT
            )
        common[...] = jnp.zeros_like(common)

    down = [down_s[j, step_id] for j in range(2)]
    across = [across_s[j, step_id] for j in range(2)]
    left = iota((BLOCK, LANES), 1) < width
    left2 = iota((2 * BLOCK, LANES), 1) < width
    for k in range(group * width // LANES):
        lanes = slice(k * LANES, (k + 1) * LANES)
        xs = [x_ref[j * BLOCK : (j + 1) * BLOCK, lanes] for j in range(2)]
        gs = [g_ref[j * BLOCK : (j + 1) * BLOCK, lanes] for j in range(2)]
        zero = jnp.zeros_like(gs[0])
        halves = [
            jnp.concatenate([jnp.where(left, v, zero), jnp.where(left, zero, v)], 0) for v in gs
        ]
        inner = [dot(halves[t], xs[s], NT) for t, s in pairs]
        twice_x = [jnp.concatenate([v, v], 0) for v in xs]
        twice_g = [jnp.concatenate([v, v], 0) for v in gs]
        both_x = jnp.concatenate(twice_x, 0)
        both_g = jnp.concatenate(twice_g, 0)
        mixed_parts, gx_parts = [], []
        totals = [None] * 3
        for e in range(2):
            h = 2 * k + e
            parts = []
            for n, (t, s) in enumerate(pairs):
                row = across[s][h : h + 1]
                if t != s:
                    row = row - row[:, BLOCK - 1 :]
                weight = jnp.exp((down[t][:, h : h + 1] + bias[n]) - row)
                weight = weight * step_blk[h : h + 1, s * BLOCK : (s + 1) * BLOCK]
                term = weight * inner[n][e * BLOCK : (e + 1) * BLOCK]
                totals[n] = term if e == 0 else totals[n] + term
                parts.append(split2(weight * inter[n]))
            p00, p10, p11 = parts
            mixed_parts.append(
                (
                    dot(jnp.concatenate(p00, 1), twice_x[0], NN),
                    dot(jnp.concatenate(p10 + p11, 1), both_x, NN),
                )
            )
            gx_parts.append(
                (
                    dot(jnp.concatenate(p00 + p10, 0), both_g, TN),
                    dot(jnp.concatenate(p11, 0), twice_g[1], TN),
                )
            )
        for n in range(3):
            common[n] += totals[n]
        first = step_id * group + 2 * k
        skip = jnp.where(left, skip_ref[first], skip_ref[first + 1])
        for j in range(2):
            rows = slice(j * BLOCK, (j + 1) * BLOCK)
            mixed_ref[rows, lanes] = (
                jnp.where(left, mixed_parts[0][j], mixed_parts[1][j]) + skip * xs[j].astype(F32)
            )
            gx_ref[rows, lanes] = (
                jnp.where(left, gx_parts[0][j], gx_parts[1][j]) + skip * gs[j].astype(F32)
            )

    @pl.when(step_id == pl.num_programs(0) - 1)
    def _():
        c00, c10, c11 = [split2(common[n]) for n in range(3)]
        b0, b1 = b_ref[:BLOCK], b_ref[BLOCK:]
        c0, c1 = c_ref[:BLOCK], c_ref[BLOCK:]
        grads_ref[0, :BLOCK] = sum(dot(v, c0, TN) for v in c00) + sum(dot(v, c1, TN) for v in c10)
        grads_ref[0, BLOCK:] = sum(dot(v, c1, TN) for v in c11)
        grads_ref[1, :BLOCK] = sum(dot(v, b0, NN) for v in c00)
        grads_ref[1, BLOCK:] = sum(dot(v, b0, NN) for v in c10) + sum(dot(v, b1, NN) for v in c11)


def place_state(core, own, other, high, low):
    half = own.shape[1]
    for part, first in ((own, core), (other, 1 - core)):
        rows = pl.ds(pl.multiple_of(first * half, half), half)
        for k in range(own.shape[0]):
            lanes = slice(k * LANES, (k + 1) * LANES)
            hi, lo = split2(part[k])
            high[rows, lanes] = hi
            low[rows, lanes] = lo


def grads_kernel(
    group, width, masks, core_ref, place_ref, own_f, other_f, own_b, other_b, x_ref, g_ref, edges_ref,
    local_ref, *rest,
):
    outs, (both, total) = rest[:-2], rest[-2:]
    step_id = pl.program_id(0)
    state = local_ref.shape[2]

    @pl.when(step_id == 0)
    def _():
        total[...] = local_ref[...]

    edges = edges_ref[...]
    for slot, own, other, ref in ((0, own_b, other_b, x_ref), (1, own_f, other_f, g_ref)):
        place_state(core_ref[0], own, other, both.at[slot], both.at[slot, state:])
        spread = SPREADS[slot](edges.shape[1], step_id * group, width, group * width)
        high, low = split2(ref[...].astype(F32) * dot(edges, spread, NN))
        product = dot(high, both[slot], NT)
        product = product[:, :state] + product[:, state:]
        total[slot] += product + dot(low, both[slot, :state], NT)

    @pl.when(step_id == pl.num_programs(0) - 1)
    def _():
        rows = total.shape[1] // len(masks)
        for mask, out in zip(masks, outs):
            first = (place_ref[0] ^ mask) * rows
            for slot in range(2):
                out[slot] = total[slot, pl.ds(pl.multiple_of(first, rows), rows)]


def output_kernel(
    group, width, kind, core_ref, own, other, base_ref, edges_ref, proj_ref, out_ref, high, low
):
    place_state(core_ref[0], own, other, high, low)
    edges = edges_ref[...]
    wide = group * width
    spread = SPREADS[kind](edges.shape[1], pl.program_id(0) * group, width, wide)
    proj = proj_ref[...]
    for lanes in pieces(wide):
        scale = dot(edges, spread[:, lanes], NN)
        carried = dot(proj, high[:, lanes], NN) + dot(proj, low[:, lanes], NN)
        out_ref[:, lanes] = (base_ref[:, lanes] + scale * carried).astype(BF16)


def whole(shape):
    return pl.BlockSpec(shape, lambda i: (0,) * len(shape))


SMEM = pl.BlockSpec(memory_space=pltpu.SMEM)
HBM = pl.BlockSpec(memory_space=pltpu.HBM)


def grant(mib):
    return pltpu.CompilerParams(vmem_limit_bytes=mib << 20)


def swap_with(value, axis, mask):
    size = lax.axis_size(axis)
    return lax.ppermute(value, axis, [(i, i ^ mask) for i in range(size)])


def scan_chips(total_f, total_b, total_l, axis):
    size, index = lax.axis_size(axis), lax.axis_index(axis)
    before, after = jnp.zeros_like(total_f), jnp.zeros_like(total_b)
    log_before, log_after = jnp.zeros_like(total_l), jnp.zeros_like(total_l)
    bit = 2
    while bit < size:
        other_f, other_b, other_l = [swap_with(v, axis, bit) for v in (total_f, total_b, total_l)]
        upper = (index & bit) != 0
        before = jnp.where(upper, jnp.exp(log_before) * other_f + before, before)
        after = jnp.where(upper, after, jnp.exp(log_after) * other_b + after)
        log_before = jnp.where(upper, log_before + other_l, log_before)
        log_after = jnp.where(upper, log_after, log_after + other_l)
        scale, other_scale = jnp.exp(total_l), jnp.exp(other_l)
        total_f = jnp.where(upper, scale * other_f + total_f, other_scale * total_f + other_f)
        total_b = jnp.where(upper, other_b + other_scale * total_b, total_b + scale * other_b)
        total_l = jnp.maximum(total_l + other_l, NEVER)
        bit *= 2
    return before, after


def encode(state, bound, log_decay):
    power = jnp.clip(jnp.ceil(jnp.log2(bound)), -100.0, 120.0)
    data = state * jnp.exp2(14.0 - power)[:, None]
    first = lax.reduce_precision(log_decay, 5, 10)
    second = lax.reduce_precision(log_decay - first, 5, 10)
    third = lax.reduce_precision(log_decay - first - second, 5, 10)
    rows = [data.reshape(-1, LANES), first, second, third, power]
    return jnp.concatenate([v.astype(jnp.float16) for v in rows], 0)


def decode(coded, chunks):
    size = coded.shape[0] - 4 * chunks
    rows = [coded[size + k * chunks : size + (k + 1) * chunks].astype(F32) for k in range(4)]
    state = coded[:size].reshape(chunks, -1, LANES)
    return state, jnp.exp2(rows[3] - 14.0), jnp.exp(rows[0] + rows[1] + rows[2])


def chip_place(axis):
    index = lax.axis_index(axis)
    return (index >> 1) & 1, (index >> 2) & 1


def pack_chip(total_f, total_b, bound_f, bound_b, log_decay, axis):
    return [
        encode(
            jnp.where(first, total_f, total_b), jnp.where(first, bound_f, bound_b), log_decay
        )
        for first in [bit == 0 for bit in chip_place(axis)]
    ]


def join_chips(arrived, axis, chunks):
    x, y = chip_place(axis)
    states, scales, decays = zip(*[decode(v, chunks) for v in arrived])
    _, two, three = decays
    same, upper = x == y, y == 1
    beyond = jnp.where(same, decays[0], 1.0)
    weights = [
        jnp.ones_like(two),
        beyond * jnp.where(same, 1.0, three),
        beyond * jnp.where(same, two, 1.0),
    ]
    weights = [w * scale for w, scale in zip(weights, scales)]
    main = [jnp.where(same, weights[0], 0.0)] + weights[1:]
    side = [jnp.where(same, 0.0, weights[0]), 0.0, 0.0]
    before = [jnp.where(upper, m, s) for m, s in zip(main, side)]
    after = [jnp.where(upper, s, m) for m, s in zip(main, side)]
    return states, before, after


def weigh(terms):
    return functools.reduce(jnp.add, [w[:, None] * v.astype(F32) for w, v in terms])


def shards(inputs, step_size, decay_rate, skip, b_in, c_in, doc_start, cotangent):
    heads, tokens = step_size.shape
    channels = inputs.shape[1]
    width = channels // heads
    state = b_in.shape[1]
    half = state // 2
    group = min(8, heads)
    groups = heads // group
    wide = group * width
    per = wide // LANES
    chunks = channels // LANES
    context, tensor = lax.axis_size("context"), lax.axis_size("tensor")
    core = lax.axis_index("context") & 1
    flag = core.reshape(1).astype(jnp.int32)
    decay = decay_rate.reshape(1, heads)
    doc = doc_start.reshape(1, tokens)

    tok = pl.BlockSpec((tokens, wide), lambda i: (0, i))
    piece = pl.BlockSpec((per, state, LANES), lambda i: (i, 0, 0))
    mine, send, raw_meta, edges = pl.pallas_call(
        functools.partial(states_kernel, group, width),
        grid=(groups,),
        in_specs=[SMEM] + [HBM] * 7,
        out_specs=[piece, piece, whole((META, chunks, LANES)), whole((tokens, 4 * heads))],
        out_shape=[jax.ShapeDtypeStruct((chunks, state, LANES), F32)] * 2
        + [
            jax.ShapeDtypeStruct((META, chunks, LANES), F32),
            jax.ShapeDtypeStruct((tokens, 4 * heads), BF16),
        ],
        scratch_shapes=[
            pltpu.VMEM((groups, tokens, wide), BF16),
            pltpu.VMEM((groups, tokens, wide), BF16),
            pltpu.VMEM((heads, tokens), F32),
            pltpu.VMEM((1, heads), F32),
            pltpu.VMEM((1, tokens), jnp.int32),
            pltpu.VMEM((tokens, state), BF16),
            pltpu.VMEM((tokens, state), BF16),
            pltpu.VMEM((state, tokens), BF16),
            pltpu.VMEM((state, tokens), BF16),
            pltpu.VMEM((META, 4 * heads), BF16),
            pltpu.SemaphoreType.DMA((5,)),
            pltpu.SemaphoreType.DMA((2, groups)),
        ],
        compiler_params=grant(STATES_VMEM),
        name="states",
    )(flag, inputs, cotangent, step_size, decay, doc, b_in, c_in)

    meta = lax.optimization_barrier(jnp.maximum(raw_meta, NEVER))
    theirs = swap_with(send, "context", 1)
    sib_meta = swap_with(raw_meta, "context", 1)
    lower = core == 0
    own_f, own_b = mine[:, :half], mine[:, half:]
    sib_f, sib_b = theirs[:, :half], theirs[:, half:]
    own_l, own_e, own_mf, own_mb = [meta[k] for k in range(4)]
    sib_l, sib_e, sib_mf, sib_mb = [sib_meta[k] for k in range(4)]
    f_own, f_sib = jnp.where(lower, sib_e, 1.0), jnp.where(lower, 1.0, own_e)
    b_own, b_sib = jnp.where(lower, 1.0, sib_e), jnp.where(lower, own_e, 1.0)
    chip_f = f_own[:, None] * own_f + f_sib[:, None] * sib_f
    chip_b = b_own[:, None] * own_b + b_sib[:, None] * sib_b
    chip_l = jnp.maximum(own_l + sib_l, NEVER)
    if context == 8:
        near, far = pack_chip(
            chip_f,
            chip_b,
            f_own * own_mf + f_sib * sib_mf,
            b_own * own_mb + b_sib * sib_mb,
            chip_l,
            "context",
        )
        near, far, skip = lax.optimization_barrier((near, far, skip))
        arrived = [
            swap_with(near, "context", 2),
            swap_with(far, "context", 4),
            swap_with(far, "context", 6),
        ]

    full = jax.ShapeDtypeStruct((tokens, channels), F32)
    mixed_loc, gx_loc, grads_loc = pl.pallas_call(
        functools.partial(local_kernel, group, width),
        grid=(groups,),
        in_specs=[
            SMEM,
            tok,
            tok,
            whole((heads, tokens)),
            pl.BlockSpec((group, tokens), lambda i: (i, 0)),
            whole((1, heads)),
            whole((1, tokens)),
            whole((tokens, state)),
            whole((tokens, state)),
        ],
        out_specs=[tok, tok, whole((2, tokens, state))],
        out_shape=[full, full, jax.ShapeDtypeStruct((2, tokens, state), F32)],
        scratch_shapes=[
            pltpu.VMEM((2, groups, BLOCK, group), F32),
            pltpu.VMEM((2, groups, group, BLOCK), F32),
            pltpu.VMEM((3, BLOCK, BLOCK), F32),
            pltpu.VMEM((3, BLOCK, BLOCK), F32),
            pltpu.VMEM((3, BLOCK, BLOCK), F32),
        ],
        compiler_params=grant(LOCAL_VMEM),
        cost_estimate=pl.CostEstimate(
            flops=20 * tokens * tokens * channels,
            transcendentals=heads * tokens * tokens,
            bytes_accessed=12 * tokens * channels,
        ),
        name="local",
    )(skip, inputs, cotangent, step_size, step_size, decay, doc, b_in, c_in)

    one, zero = jnp.ones_like(own_e), jnp.zeros_like(own_e)
    if context == 8:
        arrived, grads_loc = lax.optimization_barrier((arrived, grads_loc))
        states, before, after = join_chips(arrived, "context", chunks)
    else:
        states = scan_chips(chip_f, chip_b, chip_l[:, None], "context")
        before, after = [one, zero], [zero, one]
    pass_f = jnp.where(lower, own_e, 1.0)
    pass_b = jnp.where(lower, 1.0, own_e)
    keep_f = jnp.where(lower, 1.0, sib_e)
    keep_b = jnp.where(lower, sib_e, 1.0)
    at_lower = jnp.where(lower, one, zero)
    at_upper = jnp.where(lower, zero, one)
    weights = (
        [pass_f * w for w in before],
        [pass_b * w for w in after],
        [keep_f * w for w in before],
        [keep_b * w for w in after],
    )
    passed_f = weigh([*zip(weights[0], states), (at_lower, own_f)])
    passed_b = weigh([*zip(weights[1], states), (at_upper, own_b)])
    passed_f, passed_b, weights, states = lax.optimization_barrier(
        (passed_f, passed_b, weights, states)
    )
    other_f = swap_with(passed_f, "context", 1)
    other_b = swap_with(passed_b, "context", 1)
    enter_f = weigh([*zip(weights[2], states), (at_upper, sib_f)])
    enter_b = weigh([*zip(weights[3], states), (at_lower, sib_b)])

    masks = (0, 2, 3, 1) if tensor == 4 else (0,)
    rows = tokens // len(masks)
    place = lax.axis_index("tensor")
    state_spec = pl.BlockSpec((per, half, LANES), lambda i: (i, 0, 0))
    parts = pl.pallas_call(
        functools.partial(grads_kernel, group, width, masks),
        grid=(groups,),
        in_specs=[SMEM, SMEM]
        + [state_spec] * 4
        + [tok, tok, whole((tokens, 4 * heads)), whole((2, tokens, state))],
        out_specs=[whole((2, rows, state))] * len(masks),
        out_shape=[jax.ShapeDtypeStruct((2, rows, state), F32)] * len(masks),
        scratch_shapes=[
            pltpu.VMEM((2, 2 * state, wide), BF16),
            pltpu.VMEM((2, tokens, state), F32),
        ],
        compiler_params=grant(GRADS_VMEM),
        name="grads",
    )(
        flag,
        place.reshape(1) if tensor == 4 else jnp.zeros((1,), jnp.int32),
        enter_f,
        other_f,
        enter_b,
        other_b,
        inputs,
        cotangent,
        edges,
        grads_loc,
    )

    def finish(kind, first, own, other, base, proj, name):
        return pl.pallas_call(
            functools.partial(output_kernel, group, width, kind),
            grid=(groups,),
            in_specs=[
                SMEM,
                state_spec,
                state_spec,
                tok,
                whole((tokens, 4 * heads)),
                whole((tokens, state)),
            ],
            out_specs=tok,
            out_shape=jax.ShapeDtypeStruct((tokens, channels), BF16),
            scratch_shapes=[pltpu.VMEM((state, wide), BF16)] * 2,
            compiler_params=grant(OUTPUT_VMEM),
            cost_estimate=pl.CostEstimate(
                flops=4 * tokens * state * channels,
                transcendentals=0,
                bytes_accessed=8 * tokens * channels,
            ),
            name=name,
        )(first, own, other, base, edges, proj)

    if tensor == 4:
        (own, *leaving), first = lax.optimization_barrier((parts, flag))
        landed = [swap_with(v, "tensor", k) for k, v in zip(masks[1:], leaving)]
        mixed = finish(1, first, enter_f, other_f, mixed_loc, c_in, "mixed")
        landed, mixed = lax.optimization_barrier((landed, mixed))
        total = (own + landed[0] + landed[1] + landed[2]).astype(BF16)
        total, first = lax.optimization_barrier((total, first))
        landed = [swap_with(total, "tensor", k) for k in masks[1:]]
        grad_inputs = finish(0, first, enter_b, other_b, gx_loc, b_in, "grad_inputs")
        landed, grad_inputs = lax.optimization_barrier((landed, grad_inputs))
        summed = jnp.zeros((4,) + total.shape, BF16)
        for k, v in zip(masks, [total] + landed):
            summed = lax.dynamic_update_index_in_dim(summed, v, place ^ k, 0)
        grad_b, grad_c = summed[:, 0], summed[:, 1]
    else:
        mixed = finish(1, flag, enter_f, other_f, mixed_loc, c_in, "mixed")
        grad_inputs = finish(0, flag, enter_b, other_b, gx_loc, b_in, "grad_inputs")
        grad_b, grad_c = lax.psum(parts[0], "tensor").astype(BF16)
    return (mixed, grad_inputs, grad_b.reshape(tokens, state), grad_c.reshape(tokens, state))


def solution(mesh):
    in_specs = (
        P("context", "tensor"),
        P("tensor", "context"),
        P("tensor"),
        P("tensor"),
        P("context", None),
        P("context", None),
        P("context"),
        P("context", "tensor"),
    )
    out_specs = (
        P("context", "tensor"),
        P("context", "tensor"),
        P("context", None),
        P("context", None),
    )
    return jax.shard_map(shards, mesh=mesh, in_specs=in_specs, out_specs=out_specs, check_vma=False)
```

```python
import functools

import jax
import jax.numpy as jnp
from jax import lax
from jax.experimental import pallas as pl
from jax.experimental.pallas import tpu as pltpu
from jax.sharding import PartitionSpec as P

BLOCK = 128
LANES = 128
F32 = jnp.float32
BF16 = jnp.bfloat16
NEVER = -200.0
MASKED = -1e30
BOUND = 6.0 * 1.796875
META = 8
STATES_VMEM, LOCAL_VMEM, GRADS_VMEM, OUTPUT_VMEM = 62, 60, 48, 60

NN = (((1,), (0,)), ((), ()))
NT = (((1,), (1,)), ((), ()))
TN = (((0,), (0,)), ((), ()))


def dot(a, b, dims):
    return lax.dot_general(a, b, dims, preferred_element_type=F32)


def split2(x):
    hi = x.astype(BF16)
    lo = (x - hi.astype(F32)).astype(BF16)
    return hi, lo


def split3(x):
    hi = x.astype(BF16)
    rest = x - hi.astype(F32)
    mid = rest.astype(BF16)
    lo = (rest - mid.astype(F32)).astype(BF16)
    return hi, mid, lo


def iota(shape, axis):
    return lax.broadcasted_iota(jnp.int32, shape, axis)


def block_sums(step, decay, doc):
    log_decay = -step * decay
    tri = jnp.where(iota((BLOCK, BLOCK), 0) >= iota((BLOCK, BLOCK), 1), 1.0, 0.0).astype(BF16)
    out = []
    for first in range(0, step.shape[1], BLOCK):
        cols = slice(first, first + BLOCK)
        parts = split3(log_decay[:, cols])
        starts = jnp.broadcast_to(doc[:, cols].astype(F32), (16, BLOCK)).astype(BF16)
        down = functools.reduce(jnp.add, [dot(tri, part, NT) for part in parts])
        across = functools.reduce(jnp.add, [dot(part, tri, NT) for part in parts])
        count_down = dot(tri, starts, NT)[:, :1]
        count_across = dot(starts, tri, NT)[:1]
        out.append((down, across, count_down, count_across))
    return out


def edge_weights(step, sums):
    eye = jnp.where(iota((BLOCK, BLOCK), 0) == iota((BLOCK, BLOCK), 1), 1.0, 0.0).astype(BF16)
    blocks = len(sums)
    ends = [s[0][BLOCK - 1 :] for s in sums]
    counts = [s[2][BLOCK - 1 :] for s in sums]
    keep, last = [], []
    for k in range(blocks):
        down, _, count_down, _ = sums[k]
        sum_before = down
        starts_before = count_down
        sum_after = ends[k] - down
        starts_after = counts[k] - count_down
        for j in range(k):
            sum_before = sum_before + ends[j]
            starts_before = starts_before + counts[j]
        for j in range(k + 1, blocks):
            sum_after = sum_after + ends[j]
            starts_after = starts_after + counts[j]
        parts = split3(step[:, k * BLOCK : (k + 1) * BLOCK])
        step_down = functools.reduce(jnp.add, [dot(eye, part, NT) for part in parts])
        keep.append(jnp.where(starts_before == 0.0, jnp.exp(sum_before), 0.0))
        last.append(jnp.where(starts_after == 0.0, jnp.exp(sum_after) * step_down, 0.0))
    total = functools.reduce(jnp.add, ends)
    starts = functools.reduce(jnp.add, counts)
    total = jnp.where(starts == 0.0, jnp.maximum(total, NEVER), NEVER)
    return jnp.concatenate(keep, 0), jnp.concatenate(last, 0), total


def spread_rows(rows, first, width, columns, skipped):
    heads = rows // 4
    row = iota((rows, 1), 0) - skipped * heads
    head = jnp.where(row >= heads, row - heads, row)
    head = jnp.where((row >= 0) & (row < 2 * heads), head, -rows * rows)
    offset = iota((1, columns), 1) - (head - first) * width
    return jnp.where((offset >= 0) & (offset < width), 1.0, 0.0).astype(BF16)


def last_spread(rows, first, width, columns):
    return spread_rows(rows, first, width, columns, 0)


def keep_spread(rows, first, width, columns):
    return spread_rows(rows, first, width, columns, 2)


SPREADS = (last_spread, keep_spread)


def pieces(total, most=256):
    return [slice(k, min(k + most, total)) for k in range(0, total, most)]


def fetch(pairs, sems):
    copies = [pltpu.make_async_copy(src, dst, sems.at[k]) for k, (src, dst) in enumerate(pairs)]
    for copy in copies:
        copy.start()
    return copies


def column(row):
    shape = (row.shape[1], row.shape[1])
    spot = iota(shape, 0) == iota(shape, 1)
    return jnp.sum(jnp.where(spot, row, 0.0), axis=1, keepdims=True)


def states_kernel(
    group, width, core_ref, x_hbm, g_hbm, step_hbm, decay_hbm, doc_hbm, b_hbm, c_hbm,
    mine_ref, send_ref, meta_ref, edges_ref, x_ref, g_ref, step_ref, decay_ref, doc_ref, b_ref,
    c_ref, b_t, c_t, meta, small_sems, big_sems,
):
    step_id = pl.program_id(0)
    groups = x_ref.shape[0]
    half = b_t.shape[0] // 2
    wide = group * width
    chunks = wide // LANES

    def big(k):
        return [
            pltpu.make_async_copy(
                src.at[:, pl.ds(pl.multiple_of(k * wide, LANES), wide)], dst.at[k], big_sems.at[n, k]
            )
            for n, (src, dst) in enumerate(((x_hbm, x_ref), (g_hbm, g_ref)))
        ]

    @pl.when(step_id == 0)
    def _():
        small = fetch(
            (
                (step_hbm, step_ref),
                (decay_hbm, decay_ref),
                (doc_hbm, doc_ref),
                (b_hbm, b_ref),
                (c_hbm, c_ref),
            ),
            small_sems,
        )
        for k in range(groups):
            for copy in big(k):
                copy.start()
        for copy in small:
            copy.wait()
        swap = core_ref[0] == 1
        step = step_ref[...]
        sums = block_sums(step, column(decay_ref[...]), doc_ref[...])
        keep, last, total = edge_weights(step, sums)
        bound_f = BOUND * jnp.sum(last, axis=0, keepdims=True)
        bound_b = BOUND * jnp.sum(keep, axis=0, keepdims=True)
        rows = [total, jnp.exp(total), bound_f, bound_b]
        rows = jnp.concatenate(rows + [jnp.zeros((META - 4, total.shape[1]), F32)], 0)
        high, mid, low = split3(rows)
        meta[...] = jnp.concatenate([high, mid, low, jnp.zeros_like(high)], 1)
        edges_ref[...] = jnp.concatenate(split2(last) + split2(keep), 1)
        for ref, out in ((b_ref, b_t), (c_ref, c_t)):
            turned = ref[...].astype(F32).T
            swapped = jnp.concatenate([turned[half:], turned[:half]], 0)
            out[...] = jnp.where(swap, swapped, turned).astype(BF16)

    for copy in big(step_id):
        copy.wait()
    edges = edges_ref[...]
    spreads = [make(edges.shape[1], step_id * group, width, wide) for make in SPREADS]
    rows = dot(meta[...], spreads[0] + spreads[1], NN)
    for k in range(chunks):
        for n in range(META):
            meta_ref[n, pl.ds(step_id * chunks + k, 1)] = rows[n : n + 1, k * LANES : (k + 1) * LANES]
    for kind, (ref, turned) in enumerate(((x_ref, b_t), (g_ref, c_t))):
        turned = turned[...]
        for lanes in pieces(wide):
            scale = dot(edges, spreads[kind][:, lanes], NN)
            scaled = split2(ref[step_id, :, lanes].astype(F32) * scale)
            state = dot(turned, scaled[0], NN) + dot(turned, scaled[1], NN)
            for k in range(state.shape[1] // LANES):
                part = state[:, k * LANES : (k + 1) * LANES]
                at = lanes.start // LANES + k
                mine_ref[at, kind * half : (kind + 1) * half] = part[:half]
                send_ref[at, kind * half : (kind + 1) * half] = part[half:]


def write_rows(masks, place_ref, total, out_ref):
    rows = total.shape[1] // len(masks)
    for k, mask in enumerate(masks):
        at = pl.ds(pl.multiple_of((place_ref[0] ^ mask) * rows, rows), rows)
        for slot in range(2):
            out_ref[k, slot] = total[slot, at]


def local_kernel(
    group, width, masks, skip_ref, place_ref, x_ref, g_ref, step_ref, step_blk, decay_ref, doc_ref, b_ref, c_ref,
    mixed_ref, gx_ref, grads_ref, down_s, across_s, bias, inter, common, sums_s,
):
    step_id = pl.program_id(0)
    groups = down_s.shape[1]
    pairs = ((0, 0), (1, 0), (1, 1))

    @pl.when(step_id == 0)
    def _():
        step = step_ref[...]
        sums = block_sums(step, column(decay_ref[...]), doc_ref[...])
        for k in range(groups):
            heads = slice(k * group, (k + 1) * group)
            for j in range(2):
                down_s[j, k] = sums[j][0][:, heads]
                across_s[j, k] = sums[j][1][heads]
        for n, (t, s) in enumerate(pairs):
            if t == s:
                ok = sums[t][2] == sums[s][3]
                ok = ok & (iota((BLOCK, BLOCK), 0) >= iota((BLOCK, BLOCK), 1))
            else:
                ok = sums[t][2] == sums[s][3] - sums[s][3][:, BLOCK - 1 :]
            bias[n] = jnp.where(ok, 0.0, MASKED)
            inter[n] = dot(
                c_ref[t * BLOCK : (t + 1) * BLOCK], b_ref[s * BLOCK : (s + 1) * BLOCK], NT
            )
        common[...] = jnp.zeros_like(common)

    down = [down_s[j, step_id] for j in range(2)]
    across = [across_s[j, step_id] for j in range(2)]
    left = iota((BLOCK, LANES), 1) < width
    left2 = iota((2 * BLOCK, LANES), 1) < width
    for k in range(group * width // LANES):
        lanes = slice(k * LANES, (k + 1) * LANES)
        xs = [x_ref[j * BLOCK : (j + 1) * BLOCK, lanes] for j in range(2)]
        gs = [g_ref[j * BLOCK : (j + 1) * BLOCK, lanes] for j in range(2)]
        zero = jnp.zeros_like(gs[0])
        halves = [
            jnp.concatenate([jnp.where(left, v, zero), jnp.where(left, zero, v)], 0) for v in gs
        ]
        inner = [dot(halves[t], xs[s], NT) for t, s in pairs]
        twice_x = [jnp.concatenate([v, v], 0) for v in xs]
        twice_g = [jnp.concatenate([v, v], 0) for v in gs]
        both_x = jnp.concatenate(twice_x, 0)
        both_g = jnp.concatenate(twice_g, 0)
        mixed_parts, gx_parts = [], []
        totals = [None] * 3
        for e in range(2):
            h = 2 * k + e
            parts = []
            for n, (t, s) in enumerate(pairs):
                row = across[s][h : h + 1]
                if t != s:
                    row = row - row[:, BLOCK - 1 :]
                weight = jnp.exp((down[t][:, h : h + 1] + bias[n]) - row)
                weight = weight * step_blk[h : h + 1, s * BLOCK : (s + 1) * BLOCK]
                term = weight * inner[n][e * BLOCK : (e + 1) * BLOCK]
                totals[n] = term if e == 0 else totals[n] + term
                parts.append(split2(weight * inter[n]))
            p00, p10, p11 = parts
            mixed_parts.append(
                (
                    dot(jnp.concatenate(p00, 1), twice_x[0], NN),
                    dot(jnp.concatenate(p10 + p11, 1), both_x, NN),
                )
            )
            gx_parts.append(
                (
                    dot(jnp.concatenate(p00 + p10, 0), both_g, TN),
                    dot(jnp.concatenate(p11, 0), twice_g[1], TN),
                )
            )
        for n in range(3):
            common[n] += totals[n]
        first = step_id * group + 2 * k
        skip = jnp.where(left, skip_ref[first], skip_ref[first + 1])
        for j in range(2):
            rows = slice(j * BLOCK, (j + 1) * BLOCK)
            mixed_ref[rows, lanes] = (
                jnp.where(left, mixed_parts[0][j], mixed_parts[1][j]) + skip * xs[j].astype(F32)
            )
            gx_ref[rows, lanes] = (
                jnp.where(left, gx_parts[0][j], gx_parts[1][j]) + skip * gs[j].astype(F32)
            )

    @pl.when(step_id == pl.num_programs(0) - 1)
    def _():
        c00, c10, c11 = [split2(common[n]) for n in range(3)]
        b0, b1 = b_ref[:BLOCK], b_ref[BLOCK:]
        c0, c1 = c_ref[:BLOCK], c_ref[BLOCK:]
        sums_s[0, :BLOCK] = sum(dot(v, c0, TN) for v in c00) + sum(dot(v, c1, TN) for v in c10)
        sums_s[0, BLOCK:] = sum(dot(v, c1, TN) for v in c11)
        sums_s[1, :BLOCK] = sum(dot(v, b0, NN) for v in c00)
        sums_s[1, BLOCK:] = sum(dot(v, b0, NN) for v in c10) + sum(dot(v, b1, NN) for v in c11)
        write_rows(masks, place_ref, sums_s, grads_ref)


def place_state(core, own, other, high, low):
    half = own.shape[1]
    for part, first in ((own, core), (other, 1 - core)):
        rows = pl.ds(pl.multiple_of(first * half, half), half)
        for k in range(own.shape[0]):
            lanes = slice(k * LANES, (k + 1) * LANES)
            hi, lo = split2(part[k])
            high[rows, lanes] = hi
            low[rows, lanes] = lo


def grads_kernel(
    group, width, masks, core_ref, place_ref, own_f, other_f, own_b, other_b, x_ref, g_ref, edges_ref,
    out_ref, both, total,
):
    step_id = pl.program_id(0)
    state = total.shape[2]

    @pl.when(step_id == 0)
    def _():
        total[...] = jnp.zeros_like(total)

    edges = edges_ref[...]
    for slot, own, other, ref in ((0, own_b, other_b, x_ref), (1, own_f, other_f, g_ref)):
        place_state(core_ref[0], own, other, both.at[slot], both.at[slot, state:])
        spread = SPREADS[slot](edges.shape[1], step_id * group, width, group * width)
        high, low = split2(ref[...].astype(F32) * dot(edges, spread, NN))
        product = dot(high, both[slot], NT)
        product = product[:, :state] + product[:, state:]
        total[slot] += product + dot(low, both[slot, :state], NT)

    @pl.when(step_id == pl.num_programs(0) - 1)
    def _():
        write_rows(masks, place_ref, total, out_ref)


def output_kernel(
    group, width, kind, core_ref, own, other, base_ref, edges_ref, proj_ref, out_ref, high, low
):
    place_state(core_ref[0], own, other, high, low)
    edges = edges_ref[...]
    wide = group * width
    spread = SPREADS[kind](edges.shape[1], pl.program_id(0) * group, width, wide)
    proj = proj_ref[...]
    for lanes in pieces(wide):
        scale = dot(edges, spread[:, lanes], NN)
        carried = dot(proj, high[:, lanes], NN) + dot(proj, low[:, lanes], NN)
        out_ref[:, lanes] = (base_ref[:, lanes] + scale * carried).astype(BF16)


def whole(shape):
    return pl.BlockSpec(shape, lambda i: (0,) * len(shape))


SMEM = pl.BlockSpec(memory_space=pltpu.SMEM)
HBM = pl.BlockSpec(memory_space=pltpu.HBM)


def grant(mib):
    return pltpu.CompilerParams(vmem_limit_bytes=mib << 20)


def swap_with(value, axis, mask):
    size = lax.axis_size(axis)
    return lax.ppermute(value, axis, [(i, i ^ mask) for i in range(size)])


def scan_chips(total_f, total_b, total_l, axis):
    size, index = lax.axis_size(axis), lax.axis_index(axis)
    before, after = jnp.zeros_like(total_f), jnp.zeros_like(total_b)
    log_before, log_after = jnp.zeros_like(total_l), jnp.zeros_like(total_l)
    bit = 2
    while bit < size:
        other_f, other_b, other_l = [swap_with(v, axis, bit) for v in (total_f, total_b, total_l)]
        upper = (index & bit) != 0
        before = jnp.where(upper, jnp.exp(log_before) * other_f + before, before)
        after = jnp.where(upper, after, jnp.exp(log_after) * other_b + after)
        log_before = jnp.where(upper, log_before + other_l, log_before)
        log_after = jnp.where(upper, log_after, log_after + other_l)
        scale, other_scale = jnp.exp(total_l), jnp.exp(other_l)
        total_f = jnp.where(upper, scale * other_f + total_f, other_scale * total_f + other_f)
        total_b = jnp.where(upper, other_b + other_scale * total_b, total_b + scale * other_b)
        total_l = jnp.maximum(total_l + other_l, NEVER)
        bit *= 2
    return before, after


def encode(state, bound, log_decay):
    power = jnp.clip(jnp.ceil(jnp.log2(bound)), -100.0, 120.0)
    data = state * jnp.exp2(14.0 - power)[:, None]
    first = lax.reduce_precision(log_decay, 5, 10)
    second = lax.reduce_precision(log_decay - first, 5, 10)
    third = lax.reduce_precision(log_decay - first - second, 5, 10)
    rows = [data.reshape(-1, LANES), first, second, third, power]
    return jnp.concatenate([v.astype(jnp.float16) for v in rows], 0)


def decode(coded, chunks):
    size = coded.shape[0] - 4 * chunks
    rows = [coded[size + k * chunks : size + (k + 1) * chunks].astype(F32) for k in range(4)]
    state = coded[:size].reshape(chunks, -1, LANES)
    return state, jnp.exp2(rows[3] - 14.0), jnp.exp(rows[0] + rows[1] + rows[2])


def chip_place(axis):
    index = lax.axis_index(axis)
    return (index >> 1) & 1, (index >> 2) & 1


def pack_chip(total_f, total_b, bound_f, bound_b, log_decay, axis):
    return [
        encode(
            jnp.where(first, total_f, total_b), jnp.where(first, bound_f, bound_b), log_decay
        )
        for first in [bit == 0 for bit in chip_place(axis)]
    ]


def join_chips(arrived, axis, chunks):
    x, y = chip_place(axis)
    states, scales, decays = zip(*[decode(v, chunks) for v in arrived])
    _, two, three = decays
    same, upper = x == y, y == 1
    beyond = jnp.where(same, decays[0], 1.0)
    weights = [
        jnp.ones_like(two),
        beyond * jnp.where(same, 1.0, three),
        beyond * jnp.where(same, two, 1.0),
    ]
    weights = [w * scale for w, scale in zip(weights, scales)]
    main = [jnp.where(same, weights[0], 0.0)] + weights[1:]
    side = [jnp.where(same, 0.0, weights[0]), 0.0, 0.0]
    before = [jnp.where(upper, m, s) for m, s in zip(main, side)]
    after = [jnp.where(upper, s, m) for m, s in zip(main, side)]
    return states, before, after


def weigh(terms):
    return functools.reduce(jnp.add, [w[:, None] * v.astype(F32) for w, v in terms])


def shards(inputs, step_size, decay_rate, skip, b_in, c_in, doc_start, cotangent):
    heads, tokens = step_size.shape
    channels = inputs.shape[1]
    width = channels // heads
    state = b_in.shape[1]
    half = state // 2
    group = min(8, heads)
    groups = heads // group
    wide = group * width
    per = wide // LANES
    chunks = channels // LANES
    context, tensor = lax.axis_size("context"), lax.axis_size("tensor")
    core = lax.axis_index("context") & 1
    flag = core.reshape(1).astype(jnp.int32)
    decay = decay_rate.reshape(1, heads)
    doc = doc_start.reshape(1, tokens)

    tok = pl.BlockSpec((tokens, wide), lambda i: (0, i))
    piece = pl.BlockSpec((per, state, LANES), lambda i: (i, 0, 0))
    mine, send, raw_meta, edges = pl.pallas_call(
        functools.partial(states_kernel, group, width),
        grid=(groups,),
        in_specs=[SMEM] + [HBM] * 7,
        out_specs=[piece, piece, whole((META, chunks, LANES)), whole((tokens, 4 * heads))],
        out_shape=[jax.ShapeDtypeStruct((chunks, state, LANES), F32)] * 2
        + [
            jax.ShapeDtypeStruct((META, chunks, LANES), F32),
            jax.ShapeDtypeStruct((tokens, 4 * heads), BF16),
        ],
        scratch_shapes=[
            pltpu.VMEM((groups, tokens, wide), BF16),
            pltpu.VMEM((groups, tokens, wide), BF16),
            pltpu.VMEM((heads, tokens), F32),
            pltpu.VMEM((1, heads), F32),
            pltpu.VMEM((1, tokens), jnp.int32),
            pltpu.VMEM((tokens, state), BF16),
            pltpu.VMEM((tokens, state), BF16),
            pltpu.VMEM((state, tokens), BF16),
            pltpu.VMEM((state, tokens), BF16),
            pltpu.VMEM((META, 4 * heads), BF16),
            pltpu.SemaphoreType.DMA((5,)),
            pltpu.SemaphoreType.DMA((2, groups)),
        ],
        compiler_params=grant(STATES_VMEM),
        name="states",
    )(flag, inputs, cotangent, step_size, decay, doc, b_in, c_in)

    meta = lax.optimization_barrier(jnp.maximum(raw_meta, NEVER))
    theirs = swap_with(send, "context", 1)
    sib_meta = swap_with(raw_meta, "context", 1)
    lower = core == 0
    own_f, own_b = mine[:, :half], mine[:, half:]
    sib_f, sib_b = theirs[:, :half], theirs[:, half:]
    own_l, own_e, own_mf, own_mb = [meta[k] for k in range(4)]
    sib_l, sib_e, sib_mf, sib_mb = [sib_meta[k] for k in range(4)]
    f_own, f_sib = jnp.where(lower, sib_e, 1.0), jnp.where(lower, 1.0, own_e)
    b_own, b_sib = jnp.where(lower, 1.0, sib_e), jnp.where(lower, own_e, 1.0)
    chip_f = f_own[:, None] * own_f + f_sib[:, None] * sib_f
    chip_b = b_own[:, None] * own_b + b_sib[:, None] * sib_b
    chip_l = jnp.maximum(own_l + sib_l, NEVER)
    if context == 8:
        near, far = pack_chip(
            chip_f,
            chip_b,
            f_own * own_mf + f_sib * sib_mf,
            b_own * own_mb + b_sib * sib_mb,
            chip_l,
            "context",
        )
        near, far, skip = lax.optimization_barrier((near, far, skip))
        arrived = [
            swap_with(near, "context", 2),
            swap_with(far, "context", 4),
            swap_with(far, "context", 6),
        ]

    full = jax.ShapeDtypeStruct((tokens, channels), F32)
    masks = (0, 2, 3, 1) if tensor == 4 else (0,)
    rows = tokens // len(masks)
    place = lax.axis_index("tensor")
    part = jax.ShapeDtypeStruct((len(masks), 2, rows, state), F32)
    spot = place.reshape(1) if tensor == 4 else jnp.zeros((1,), jnp.int32)
    mixed_loc, gx_loc, grads_loc = pl.pallas_call(
        functools.partial(local_kernel, group, width, masks),
        grid=(groups,),
        in_specs=[
            SMEM,
            SMEM,
            tok,
            tok,
            whole((heads, tokens)),
            pl.BlockSpec((group, tokens), lambda i: (i, 0)),
            whole((1, heads)),
            whole((1, tokens)),
            whole((tokens, state)),
            whole((tokens, state)),
        ],
        out_specs=[tok, tok, whole(part.shape)],
        out_shape=[full, full, part],
        scratch_shapes=[
            pltpu.VMEM((2, groups, BLOCK, group), F32),
            pltpu.VMEM((2, groups, group, BLOCK), F32),
            pltpu.VMEM((3, BLOCK, BLOCK), F32),
            pltpu.VMEM((3, BLOCK, BLOCK), F32),
            pltpu.VMEM((3, BLOCK, BLOCK), F32),
            pltpu.VMEM((2, tokens, state), F32),
        ],
        compiler_params=grant(LOCAL_VMEM),
        cost_estimate=pl.CostEstimate(
            flops=20 * tokens * tokens * channels,
            transcendentals=heads * tokens * tokens,
            bytes_accessed=12 * tokens * channels,
        ),
        name="local",
    )(skip, spot, inputs, cotangent, step_size, step_size, decay, doc, b_in, c_in)

    one, zero = jnp.ones_like(own_e), jnp.zeros_like(own_e)
    if context == 8:
        arrived, grads_loc = lax.optimization_barrier((arrived, grads_loc))
        states, before, after = join_chips(arrived, "context", chunks)
    else:
        states = scan_chips(chip_f, chip_b, chip_l[:, None], "context")
        before, after = [one, zero], [zero, one]
    pass_f = jnp.where(lower, own_e, 1.0)
    pass_b = jnp.where(lower, 1.0, own_e)
    keep_f = jnp.where(lower, 1.0, sib_e)
    keep_b = jnp.where(lower, sib_e, 1.0)
    at_lower = jnp.where(lower, one, zero)
    at_upper = jnp.where(lower, zero, one)
    weights = (
        [pass_f * w for w in before],
        [pass_b * w for w in after],
        [keep_f * w for w in before],
        [keep_b * w for w in after],
    )
    passed_f = weigh([*zip(weights[0], states), (at_lower, own_f)])
    passed_b = weigh([*zip(weights[1], states), (at_upper, own_b)])
    passed_f, passed_b, weights, states = lax.optimization_barrier(
        (passed_f, passed_b, weights, states)
    )
    other_f = swap_with(passed_f, "context", 1)
    other_b = swap_with(passed_b, "context", 1)
    enter_f = weigh([*zip(weights[2], states), (at_upper, sib_f)])
    enter_b = weigh([*zip(weights[3], states), (at_lower, sib_b)])

    state_spec = pl.BlockSpec((per, half, LANES), lambda i: (i, 0, 0))
    carried = pl.pallas_call(
        functools.partial(grads_kernel, group, width, masks),
        grid=(groups,),
        in_specs=[SMEM, SMEM] + [state_spec] * 4 + [tok, tok, whole((tokens, 4 * heads))],
        out_specs=whole(part.shape),
        out_shape=part,
        scratch_shapes=[
            pltpu.VMEM((2, 2 * state, wide), BF16),
            pltpu.VMEM((2, tokens, state), F32),
        ],
        compiler_params=grant(GRADS_VMEM),
        name="grads",
    )(
        flag, spot, enter_f, other_f, enter_b, other_b, inputs, cotangent, edges
    )
    parts = [carried[k] + grads_loc[k] for k in range(len(masks))]

    def finish(kind, first, own, other, base, proj, name):
        return pl.pallas_call(
            functools.partial(output_kernel, group, width, kind),
            grid=(groups,),
            in_specs=[
                SMEM,
                state_spec,
                state_spec,
                tok,
                whole((tokens, 4 * heads)),
                whole((tokens, state)),
            ],
            out_specs=tok,
            out_shape=jax.ShapeDtypeStruct((tokens, channels), BF16),
            scratch_shapes=[pltpu.VMEM((state, wide), BF16)] * 2,
            compiler_params=grant(OUTPUT_VMEM),
            cost_estimate=pl.CostEstimate(
                flops=4 * tokens * state * channels,
                transcendentals=0,
                bytes_accessed=8 * tokens * channels,
            ),
            name=name,
        )(first, own, other, base, edges, proj)

    if tensor == 4:
        (own, *leaving), first = lax.optimization_barrier((parts, flag))
        landed = [swap_with(v, "tensor", k) for k, v in zip(masks[1:], leaving)]
        mixed = finish(1, first, enter_f, other_f, mixed_loc, c_in, "mixed")
        landed, mixed = lax.optimization_barrier((landed, mixed))
        total = (own + landed[0] + landed[1] + landed[2]).astype(BF16)
        total, first = lax.optimization_barrier((total, first))
        landed = [swap_with(total, "tensor", k) for k in masks[1:]]
        grad_inputs = finish(0, first, enter_b, other_b, gx_loc, b_in, "grad_inputs")
        landed, grad_inputs = lax.optimization_barrier((landed, grad_inputs))
        summed = jnp.zeros((4,) + total.shape, BF16)
        for k, v in zip(masks, [total] + landed):
            summed = lax.dynamic_update_index_in_dim(summed, v, place ^ k, 0)
        grad_b, grad_c = summed[:, 0], summed[:, 1]
    else:
        mixed = finish(1, flag, enter_f, other_f, mixed_loc, c_in, "mixed")
        grad_inputs = finish(0, flag, enter_b, other_b, gx_loc, b_in, "grad_inputs")
        grad_b, grad_c = lax.psum(parts[0], "tensor").astype(BF16)
    return (mixed, grad_inputs, grad_b.reshape(tokens, state), grad_c.reshape(tokens, state))


def solution(mesh):
    in_specs = (
        P("context", "tensor"),
        P("tensor", "context"),
        P("tensor"),
        P("tensor"),
        P("context", None),
        P("context", None),
        P("context"),
        P("context", "tensor"),
    )
    out_specs = (
        P("context", "tensor"),
        P("context", "tensor"),
        P("context", None),
        P("context", None),
    )
    return jax.shard_map(shards, mesh=mesh, in_specs=in_specs, out_specs=out_specs, check_vma=False)
```

```python
import functools

import jax
import jax.numpy as jnp
from jax import lax
from jax.experimental import pallas as pl
from jax.experimental.pallas import tpu as pltpu
from jax.sharding import PartitionSpec as P

BLOCK = 128
LANES = 128
F32 = jnp.float32
BF16 = jnp.bfloat16
NEVER = -200.0
MASKED = -1e30
BOUND = 6.0 * 1.796875
META = 8
STATES_VMEM, LOCAL_VMEM, GRADS_VMEM, OUTPUT_VMEM = 62, 60, 48, 60

NN = (((1,), (0,)), ((), ()))
NT = (((1,), (1,)), ((), ()))
TN = (((0,), (0,)), ((), ()))


def dot(a, b, dims):
    return lax.dot_general(a, b, dims, preferred_element_type=F32)


def split2(x):
    hi = x.astype(BF16)
    lo = (x - hi.astype(F32)).astype(BF16)
    return hi, lo


def split3(x):
    hi = x.astype(BF16)
    rest = x - hi.astype(F32)
    mid = rest.astype(BF16)
    lo = (rest - mid.astype(F32)).astype(BF16)
    return hi, mid, lo


def iota(shape, axis):
    return lax.broadcasted_iota(jnp.int32, shape, axis)


def block_sums(step, decay, doc):
    log_decay = -step * decay
    tri = jnp.where(iota((BLOCK, BLOCK), 0) >= iota((BLOCK, BLOCK), 1), 1.0, 0.0).astype(BF16)
    out = []
    for first in range(0, step.shape[1], BLOCK):
        cols = slice(first, first + BLOCK)
        parts = split3(log_decay[:, cols])
        starts = jnp.broadcast_to(doc[:, cols].astype(F32), (16, BLOCK)).astype(BF16)
        down = functools.reduce(jnp.add, [dot(tri, part, NT) for part in parts])
        across = functools.reduce(jnp.add, [dot(part, tri, NT) for part in parts])
        count_down = dot(tri, starts, NT)[:, :1]
        count_across = dot(starts, tri, NT)[:1]
        out.append((down, across, count_down, count_across))
    return out


def edge_weights(step, sums):
    eye = jnp.where(iota((BLOCK, BLOCK), 0) == iota((BLOCK, BLOCK), 1), 1.0, 0.0).astype(BF16)
    blocks = len(sums)
    ends = [s[0][BLOCK - 1 :] for s in sums]
    counts = [s[2][BLOCK - 1 :] for s in sums]
    keep, last = [], []
    for k in range(blocks):
        down, _, count_down, _ = sums[k]
        sum_before = down
        starts_before = count_down
        sum_after = ends[k] - down
        starts_after = counts[k] - count_down
        for j in range(k):
            sum_before = sum_before + ends[j]
            starts_before = starts_before + counts[j]
        for j in range(k + 1, blocks):
            sum_after = sum_after + ends[j]
            starts_after = starts_after + counts[j]
        parts = split3(step[:, k * BLOCK : (k + 1) * BLOCK])
        step_down = functools.reduce(jnp.add, [dot(eye, part, NT) for part in parts])
        keep.append(jnp.where(starts_before == 0.0, jnp.exp(sum_before), 0.0))
        last.append(jnp.where(starts_after == 0.0, jnp.exp(sum_after) * step_down, 0.0))
    total = functools.reduce(jnp.add, ends)
    starts = functools.reduce(jnp.add, counts)
    total = jnp.where(starts == 0.0, jnp.maximum(total, NEVER), NEVER)
    return jnp.concatenate(keep, 0), jnp.concatenate(last, 0), total


def spread_rows(rows, first, width, columns, skipped):
    heads = rows // 4
    row = iota((rows, 1), 0) - skipped * heads
    head = jnp.where(row >= heads, row - heads, row)
    head = jnp.where((row >= 0) & (row < 2 * heads), head, -rows * rows)
    offset = iota((1, columns), 1) - (head - first) * width
    return jnp.where((offset >= 0) & (offset < width), 1.0, 0.0).astype(BF16)


def last_spread(rows, first, width, columns):
    return spread_rows(rows, first, width, columns, 0)


def keep_spread(rows, first, width, columns):
    return spread_rows(rows, first, width, columns, 2)


SPREADS = (last_spread, keep_spread)


def pieces(total, most=256):
    return [slice(k, min(k + most, total)) for k in range(0, total, most)]


def fetch(pairs, sems):
    copies = [pltpu.make_async_copy(src, dst, sems.at[k]) for k, (src, dst) in enumerate(pairs)]
    for copy in copies:
        copy.start()
    return copies


def column(row):
    shape = (row.shape[1], row.shape[1])
    spot = iota(shape, 0) == iota(shape, 1)
    return jnp.sum(jnp.where(spot, row, 0.0), axis=1, keepdims=True)


def states_kernel(
    group, width, core_ref, x_hbm, g_hbm, step_hbm, decay_hbm, doc_hbm, b_hbm, c_hbm,
    mine_ref, send_ref, meta_ref, edges_ref, x_ref, g_ref, step_ref, decay_ref, doc_ref, b_ref,
    c_ref, b_t, c_t, meta, small_sems, big_sems,
):
    step_id = pl.program_id(0)
    groups = x_ref.shape[0]
    half = b_t.shape[0] // 2
    wide = group * width
    chunks = wide // LANES

    def big(k):
        return [
            pltpu.make_async_copy(
                src.at[:, pl.ds(pl.multiple_of(k * wide, LANES), wide)], dst.at[k], big_sems.at[n, k]
            )
            for n, (src, dst) in enumerate(((x_hbm, x_ref), (g_hbm, g_ref)))
        ]

    @pl.when(step_id == 0)
    def _():
        small = fetch(
            (
                (step_hbm, step_ref),
                (decay_hbm, decay_ref),
                (doc_hbm, doc_ref),
                (b_hbm, b_ref),
                (c_hbm, c_ref),
            ),
            small_sems,
        )
        for k in range(groups):
            for copy in big(k):
                copy.start()
        for copy in small:
            copy.wait()
        swap = core_ref[0] == 1
        step = step_ref[...]
        sums = block_sums(step, column(decay_ref[...]), doc_ref[...])
        keep, last, total = edge_weights(step, sums)
        bound_f = BOUND * jnp.sum(last, axis=0, keepdims=True)
        bound_b = BOUND * jnp.sum(keep, axis=0, keepdims=True)
        rows = [total, jnp.exp(total), bound_f, bound_b]
        rows = jnp.concatenate(rows + [jnp.zeros((META - 4, total.shape[1]), F32)], 0)
        high, mid, low = split3(rows)
        meta[...] = jnp.concatenate([high, mid, low, jnp.zeros_like(high)], 1)
        edges_ref[...] = jnp.concatenate(split2(last) + split2(keep), 1)
        for ref, out in ((b_ref, b_t), (c_ref, c_t)):
            turned = ref[...].astype(F32).T
            swapped = jnp.concatenate([turned[half:], turned[:half]], 0)
            out[...] = jnp.where(swap, swapped, turned).astype(BF16)

    for copy in big(step_id):
        copy.wait()
    edges = edges_ref[...]
    spreads = [make(edges.shape[1], step_id * group, width, wide) for make in SPREADS]
    rows = dot(meta[...], spreads[0] + spreads[1], NN)
    for k in range(chunks):
        for n in range(META):
            meta_ref[n, pl.ds(step_id * chunks + k, 1)] = rows[n : n + 1, k * LANES : (k + 1) * LANES]
    for kind, (ref, turned) in enumerate(((x_ref, b_t), (g_ref, c_t))):
        turned = turned[...]
        for lanes in pieces(wide):
            scale = dot(edges, spreads[kind][:, lanes], NN)
            scaled = split2(ref[step_id, :, lanes].astype(F32) * scale)
            state = dot(turned, scaled[0], NN) + dot(turned, scaled[1], NN)
            for k in range(state.shape[1] // LANES):
                part = state[:, k * LANES : (k + 1) * LANES]
                at = lanes.start // LANES + k
                mine_ref[at, kind * half : (kind + 1) * half] = part[:half]
                send_ref[at, kind * half : (kind + 1) * half] = part[half:]


def write_rows(masks, place_ref, total, out_ref):
    rows = total.shape[1] // len(masks)
    for k, mask in enumerate(masks):
        at = pl.ds(pl.multiple_of((place_ref[0] ^ mask) * rows, rows), rows)
        for slot in range(2):
            out_ref[k, slot] = total[slot, at]


def local_kernel(
    group, width, masks, skip_ref, place_ref, x_ref, g_ref, step_ref, step_blk, decay_ref, doc_ref, b_ref, c_ref,
    mixed_ref, gx_ref, grads_ref, down_s, across_s, bias, inter, common, sums_s,
):
    step_id = pl.program_id(0)
    groups = down_s.shape[1]
    pairs = ((0, 0), (1, 0), (1, 1))

    @pl.when(step_id == 0)
    def _():
        step = step_ref[...]
        sums = block_sums(step, column(decay_ref[...]), doc_ref[...])
        for k in range(groups):
            heads = slice(k * group, (k + 1) * group)
            for j in range(2):
                down_s[j, k] = sums[j][0][:, heads]
                across_s[j, k] = sums[j][1][heads]
        for n, (t, s) in enumerate(pairs):
            if t == s:
                ok = sums[t][2] == sums[s][3]
                ok = ok & (iota((BLOCK, BLOCK), 0) >= iota((BLOCK, BLOCK), 1))
            else:
                ok = sums[t][2] == sums[s][3] - sums[s][3][:, BLOCK - 1 :]
            bias[n] = jnp.where(ok, 0.0, MASKED)
            inter[n] = dot(
                c_ref[t * BLOCK : (t + 1) * BLOCK], b_ref[s * BLOCK : (s + 1) * BLOCK], NT
            )
        common[...] = jnp.zeros_like(common)

    down = [down_s[j, step_id] for j in range(2)]
    across = [across_s[j, step_id] for j in range(2)]
    left = iota((BLOCK, LANES), 1) < width
    left2 = iota((2 * BLOCK, LANES), 1) < width
    for k in range(group * width // LANES):
        lanes = slice(k * LANES, (k + 1) * LANES)
        xs = [x_ref[j * BLOCK : (j + 1) * BLOCK, lanes] for j in range(2)]
        gs = [g_ref[j * BLOCK : (j + 1) * BLOCK, lanes] for j in range(2)]
        zero = jnp.zeros_like(gs[0])
        halves = [
            jnp.concatenate([jnp.where(left, v, zero), jnp.where(left, zero, v)], 0) for v in gs
        ]
        inner = [dot(halves[t], xs[s], NT) for t, s in pairs]
        twice_x = [jnp.concatenate([v, v], 0) for v in xs]
        twice_g = [jnp.concatenate([v, v], 0) for v in gs]
        both_x = jnp.concatenate(twice_x, 0)
        both_g = jnp.concatenate(twice_g, 0)
        mixed_parts, gx_parts = [], []
        totals = [None] * 3
        for e in range(2):
            h = 2 * k + e
            parts = []
            for n, (t, s) in enumerate(pairs):
                row = across[s][h : h + 1]
                if t != s:
                    row = row - row[:, BLOCK - 1 :]
                weight = jnp.exp((down[t][:, h : h + 1] + bias[n]) - row)
                weight = weight * step_blk[h : h + 1, s * BLOCK : (s + 1) * BLOCK]
                term = weight * inner[n][e * BLOCK : (e + 1) * BLOCK]
                totals[n] = term if e == 0 else totals[n] + term
                parts.append(split2(weight * inter[n]))
            p00, p10, p11 = parts
            mixed_parts.append(
                (
                    dot(jnp.concatenate(p00, 1), twice_x[0], NN),
                    dot(jnp.concatenate(p10 + p11, 1), both_x, NN),
                )
            )
            gx_parts.append(
                (
                    dot(jnp.concatenate(p00 + p10, 0), both_g, TN),
                    dot(jnp.concatenate(p11, 0), twice_g[1], TN),
                )
            )
        for n in range(3):
            common[n] += totals[n]
        first = step_id * group + 2 * k
        skip = jnp.where(left, skip_ref[first], skip_ref[first + 1])
        for j in range(2):
            rows = slice(j * BLOCK, (j + 1) * BLOCK)
            mixed_ref[rows, lanes] = (
                jnp.where(left, mixed_parts[0][j], mixed_parts[1][j]) + skip * xs[j].astype(F32)
            )
            gx_ref[rows, lanes] = (
                jnp.where(left, gx_parts[0][j], gx_parts[1][j]) + skip * gs[j].astype(F32)
            )

    @pl.when(step_id == pl.num_programs(0) - 1)
    def _():
        c00, c10, c11 = [split2(common[n]) for n in range(3)]
        b0, b1 = b_ref[:BLOCK], b_ref[BLOCK:]
        c0, c1 = c_ref[:BLOCK], c_ref[BLOCK:]
        sums_s[0, :BLOCK] = sum(dot(v, c0, TN) for v in c00) + sum(dot(v, c1, TN) for v in c10)
        sums_s[0, BLOCK:] = sum(dot(v, c1, TN) for v in c11)
        sums_s[1, :BLOCK] = sum(dot(v, b0, NN) for v in c00)
        sums_s[1, BLOCK:] = sum(dot(v, b0, NN) for v in c10) + sum(dot(v, b1, NN) for v in c11)
        write_rows(masks, place_ref, sums_s, grads_ref)


def place_state(core, own, other, high, low):
    half = own.shape[1]
    for part, first in ((own, core), (other, 1 - core)):
        rows = pl.ds(pl.multiple_of(first * half, half), half)
        for k in range(own.shape[0]):
            lanes = slice(k * LANES, (k + 1) * LANES)
            hi, lo = split2(part[k])
            high[rows, lanes] = hi
            low[rows, lanes] = lo


def grads_kernel(
    group, width, masks, core_ref, place_ref, own_f, other_f, own_b, other_b, x_ref, g_ref, edges_ref,
    out_ref, both, total,
):
    step_id = pl.program_id(0)
    state = total.shape[2]

    @pl.when(step_id == 0)
    def _():
        total[...] = jnp.zeros_like(total)

    edges = edges_ref[...]
    for slot, own, other, ref in ((0, own_b, other_b, x_ref), (1, own_f, other_f, g_ref)):
        place_state(core_ref[0], own, other, both.at[slot], both.at[slot, state:])
        spread = SPREADS[slot](edges.shape[1], step_id * group, width, group * width)
        high, low = split2(ref[...].astype(F32) * dot(edges, spread, NN))
        product = dot(high, both[slot], NT)
        product = product[:, :state] + product[:, state:]
        total[slot] += product + dot(low, both[slot, :state], NT)

    @pl.when(step_id == pl.num_programs(0) - 1)
    def _():
        write_rows(masks, place_ref, total, out_ref)


def output_kernel(
    group, width, kind, core_ref, own, other, base_ref, edges_ref, proj_ref, out_ref, high, low
):
    place_state(core_ref[0], own, other, high, low)
    edges = edges_ref[...]
    wide = group * width
    spread = SPREADS[kind](edges.shape[1], pl.program_id(0) * group, width, wide)
    proj = proj_ref[...]
    for lanes in pieces(wide):
        scale = dot(edges, spread[:, lanes], NN)
        carried = dot(proj, high[:, lanes], NN) + dot(proj, low[:, lanes], NN)
        out_ref[:, lanes] = (base_ref[:, lanes] + scale * carried).astype(BF16)


def whole(shape):
    return pl.BlockSpec(shape, lambda i: (0,) * len(shape))


SMEM = pl.BlockSpec(memory_space=pltpu.SMEM)
HBM = pl.BlockSpec(memory_space=pltpu.HBM)


def grant(mib):
    return pltpu.CompilerParams(vmem_limit_bytes=mib << 20)


def swap_with(value, axis, mask):
    size = lax.axis_size(axis)
    return lax.ppermute(value, axis, [(i, i ^ mask) for i in range(size)])


def scan_chips(total_f, total_b, total_l, axis):
    size, index = lax.axis_size(axis), lax.axis_index(axis)
    before, after = jnp.zeros_like(total_f), jnp.zeros_like(total_b)
    log_before, log_after = jnp.zeros_like(total_l), jnp.zeros_like(total_l)
    bit = 2
    while bit < size:
        other_f, other_b, other_l = [swap_with(v, axis, bit) for v in (total_f, total_b, total_l)]
        upper = (index & bit) != 0
        before = jnp.where(upper, jnp.exp(log_before) * other_f + before, before)
        after = jnp.where(upper, after, jnp.exp(log_after) * other_b + after)
        log_before = jnp.where(upper, log_before + other_l, log_before)
        log_after = jnp.where(upper, log_after, log_after + other_l)
        scale, other_scale = jnp.exp(total_l), jnp.exp(other_l)
        total_f = jnp.where(upper, scale * other_f + total_f, other_scale * total_f + other_f)
        total_b = jnp.where(upper, other_b + other_scale * total_b, total_b + scale * other_b)
        total_l = jnp.maximum(total_l + other_l, NEVER)
        bit *= 2
    return before, after


def encode(state, bound, log_decay):
    power = jnp.clip(jnp.ceil(jnp.log2(bound)), -100.0, 120.0)
    data = state * jnp.exp2(14.0 - power)[:, None]
    first = lax.reduce_precision(log_decay, 5, 10)
    second = lax.reduce_precision(log_decay - first, 5, 10)
    third = lax.reduce_precision(log_decay - first - second, 5, 10)
    rows = [data.reshape(-1, LANES), first, second, third, power]
    return jnp.concatenate([v.astype(jnp.float16) for v in rows], 0)


def decode(coded, chunks):
    size = coded.shape[0] - 4 * chunks
    rows = [coded[size + k * chunks : size + (k + 1) * chunks].astype(F32) for k in range(4)]
    state = coded[:size].reshape(chunks, -1, LANES)
    return state, jnp.exp2(rows[3] - 14.0), jnp.exp(rows[0] + rows[1] + rows[2])


def chip_place(axis):
    index = lax.axis_index(axis)
    return (index >> 1) & 1, (index >> 2) & 1


def pack_chip(total_f, total_b, bound_f, bound_b, log_decay, axis):
    return [
        encode(
            jnp.where(first, total_f, total_b), jnp.where(first, bound_f, bound_b), log_decay
        )
        for first in [bit == 0 for bit in chip_place(axis)]
    ]


def join_chips(arrived, axis, chunks):
    x, y = chip_place(axis)
    states, scales, decays = zip(*[decode(v, chunks) for v in arrived])
    _, two, three = decays
    same, upper = x == y, y == 1
    beyond = jnp.where(same, decays[0], 1.0)
    weights = [
        jnp.ones_like(two),
        beyond * jnp.where(same, 1.0, three),
        beyond * jnp.where(same, two, 1.0),
    ]
    weights = [w * scale for w, scale in zip(weights, scales)]
    main = [jnp.where(same, weights[0], 0.0)] + weights[1:]
    side = [jnp.where(same, 0.0, weights[0]), 0.0, 0.0]
    before = [jnp.where(upper, m, s) for m, s in zip(main, side)]
    after = [jnp.where(upper, s, m) for m, s in zip(main, side)]
    return states, before, after


def weigh(terms):
    return functools.reduce(jnp.add, [w[:, None] * v.astype(F32) for w, v in terms])


def shards(inputs, step_size, decay_rate, skip, b_in, c_in, doc_start, cotangent):
    heads, tokens = step_size.shape
    channels = inputs.shape[1]
    width = channels // heads
    state = b_in.shape[1]
    half = state // 2
    group = min(8, heads)
    groups = heads // group
    wide = group * width
    per = wide // LANES
    chunks = channels // LANES
    context, tensor = lax.axis_size("context"), lax.axis_size("tensor")
    core = lax.axis_index("context") & 1
    flag = core.reshape(1).astype(jnp.int32)
    decay = decay_rate.reshape(1, heads)
    doc = doc_start.reshape(1, tokens)

    tok = pl.BlockSpec((tokens, wide), lambda i: (0, i))
    piece = pl.BlockSpec((per, state, LANES), lambda i: (i, 0, 0))
    sgroup = min(32, heads)
    sgroups = heads // sgroup
    swide = sgroup * width
    piece = pl.BlockSpec((swide // LANES, state, LANES), lambda i: (i, 0, 0))
    mine, send, raw_meta, edges = pl.pallas_call(
        functools.partial(states_kernel, sgroup, width),
        grid=(sgroups,),
        in_specs=[SMEM] + [HBM] * 7,
        out_specs=[piece, piece, whole((META, chunks, LANES)), whole((tokens, 4 * heads))],
        out_shape=[jax.ShapeDtypeStruct((chunks, state, LANES), F32)] * 2
        + [
            jax.ShapeDtypeStruct((META, chunks, LANES), F32),
            jax.ShapeDtypeStruct((tokens, 4 * heads), BF16),
        ],
        scratch_shapes=[
            pltpu.VMEM((sgroups, tokens, swide), BF16),
            pltpu.VMEM((sgroups, tokens, swide), BF16),
            pltpu.VMEM((heads, tokens), F32),
            pltpu.VMEM((1, heads), F32),
            pltpu.VMEM((1, tokens), jnp.int32),
            pltpu.VMEM((tokens, state), BF16),
            pltpu.VMEM((tokens, state), BF16),
            pltpu.VMEM((state, tokens), BF16),
            pltpu.VMEM((state, tokens), BF16),
            pltpu.VMEM((META, 4 * heads), BF16),
            pltpu.SemaphoreType.DMA((5,)),
            pltpu.SemaphoreType.DMA((2, sgroups)),
        ],
        compiler_params=grant(STATES_VMEM),
        name="states",
    )(flag, inputs, cotangent, step_size, decay, doc, b_in, c_in)

    least = float(jnp.finfo(F32).min)
    meta, mine = lax.optimization_barrier((jnp.maximum(raw_meta, NEVER), jnp.maximum(mine, least)))
    theirs = swap_with(send, "context", 1)
    sib_meta = swap_with(raw_meta, "context", 1)
    lower = core == 0
    own_f, own_b = mine[:, :half], mine[:, half:]
    sib_f, sib_b = theirs[:, :half], theirs[:, half:]
    own_l, own_e, own_mf, own_mb = [meta[k] for k in range(4)]
    sib_l, sib_e, sib_mf, sib_mb = [sib_meta[k] for k in range(4)]
    f_own, f_sib = jnp.where(lower, sib_e, 1.0), jnp.where(lower, 1.0, own_e)
    b_own, b_sib = jnp.where(lower, 1.0, sib_e), jnp.where(lower, own_e, 1.0)
    chip_f = f_own[:, None] * own_f + f_sib[:, None] * sib_f
    chip_b = b_own[:, None] * own_b + b_sib[:, None] * sib_b
    chip_l = jnp.maximum(own_l + sib_l, NEVER)
    if context == 8:
        near, far = pack_chip(
            chip_f,
            chip_b,
            f_own * own_mf + f_sib * sib_mf,
            b_own * own_mb + b_sib * sib_mb,
            chip_l,
            "context",
        )
        near, far, skip = lax.optimization_barrier((near, far, skip))
        arrived = [
            swap_with(near, "context", 2),
            swap_with(far, "context", 4),
            swap_with(far, "context", 6),
        ]

    full = jax.ShapeDtypeStruct((tokens, channels), F32)
    masks = (0, 2, 3, 1) if tensor == 4 else (0,)
    rows = tokens // len(masks)
    place = lax.axis_index("tensor")
    part = jax.ShapeDtypeStruct((len(masks), 2, rows, state), F32)
    spot = place.reshape(1) if tensor == 4 else jnp.zeros((1,), jnp.int32)
    mixed_loc, gx_loc, grads_loc = pl.pallas_call(
        functools.partial(local_kernel, group, width, masks),
        grid=(groups,),
        in_specs=[
            SMEM,
            SMEM,
            tok,
            tok,
            whole((heads, tokens)),
            pl.BlockSpec((group, tokens), lambda i: (i, 0)),
            whole((1, heads)),
            whole((1, tokens)),
            whole((tokens, state)),
            whole((tokens, state)),
        ],
        out_specs=[tok, tok, whole(part.shape)],
        out_shape=[full, full, part],
        scratch_shapes=[
            pltpu.VMEM((2, groups, BLOCK, group), F32),
            pltpu.VMEM((2, groups, group, BLOCK), F32),
            pltpu.VMEM((3, BLOCK, BLOCK), F32),
            pltpu.VMEM((3, BLOCK, BLOCK), F32),
            pltpu.VMEM((3, BLOCK, BLOCK), F32),
            pltpu.VMEM((2, tokens, state), F32),
        ],
        compiler_params=grant(LOCAL_VMEM),
        cost_estimate=pl.CostEstimate(
            flops=20 * tokens * tokens * channels,
            transcendentals=heads * tokens * tokens,
            bytes_accessed=12 * tokens * channels,
        ),
        name="local",
    )(skip, spot, inputs, cotangent, step_size, step_size, decay, doc, b_in, c_in)

    one, zero = jnp.ones_like(own_e), jnp.zeros_like(own_e)
    if context == 8:
        arrived, grads_loc = lax.optimization_barrier((arrived, grads_loc))
        states, before, after = join_chips(arrived, "context", chunks)
    else:
        states = scan_chips(chip_f, chip_b, chip_l[:, None], "context")
        before, after = [one, zero], [zero, one]
    pass_f = jnp.where(lower, own_e, 1.0)
    pass_b = jnp.where(lower, 1.0, own_e)
    keep_f = jnp.where(lower, 1.0, sib_e)
    keep_b = jnp.where(lower, sib_e, 1.0)
    at_lower = jnp.where(lower, one, zero)
    at_upper = jnp.where(lower, zero, one)
    weights = (
        [pass_f * w for w in before],
        [pass_b * w for w in after],
        [keep_f * w for w in before],
        [keep_b * w for w in after],
    )
    passed_f = weigh([*zip(weights[0], states), (at_lower, own_f)])
    passed_b = weigh([*zip(weights[1], states), (at_upper, own_b)])
    passed_f, passed_b, weights, states = lax.optimization_barrier(
        (passed_f, passed_b, weights, states)
    )
    other_f = swap_with(passed_f, "context", 1)
    other_b = swap_with(passed_b, "context", 1)
    enter_f = weigh([*zip(weights[2], states), (at_upper, sib_f)])
    enter_b = weigh([*zip(weights[3], states), (at_lower, sib_b)])

    ggroup = min(32, heads)
    gwide = ggroup * width
    gtok = pl.BlockSpec((tokens, gwide), lambda i: (0, i))
    gstate = pl.BlockSpec((gwide // LANES, half, LANES), lambda i: (i, 0, 0))
    carried = pl.pallas_call(
        functools.partial(grads_kernel, ggroup, width, masks),
        grid=(heads // ggroup,),
        in_specs=[SMEM, SMEM] + [gstate] * 4 + [gtok, gtok, whole((tokens, 4 * heads))],
        out_specs=whole(part.shape),
        out_shape=part,
        scratch_shapes=[
            pltpu.VMEM((2, 2 * state, gwide), BF16),
            pltpu.VMEM((2, tokens, state), F32),
        ],
        compiler_params=grant(GRADS_VMEM),
        name="grads",
    )(
        flag, spot, enter_f, other_f, enter_b, other_b, inputs, cotangent, edges
    )
    parts = [carried[k] + grads_loc[k] for k in range(len(masks))]

    state_spec = pl.BlockSpec((per, half, LANES), lambda i: (i, 0, 0))

    def finish(kind, first, own, other, base, proj, name):
        return pl.pallas_call(
            functools.partial(output_kernel, group, width, kind),
            grid=(groups,),
            in_specs=[
                SMEM,
                state_spec,
                state_spec,
                tok,
                whole((tokens, 4 * heads)),
                whole((tokens, state)),
            ],
            out_specs=tok,
            out_shape=jax.ShapeDtypeStruct((tokens, channels), BF16),
            scratch_shapes=[pltpu.VMEM((state, wide), BF16)] * 2,
            compiler_params=grant(OUTPUT_VMEM),
            cost_estimate=pl.CostEstimate(
                flops=4 * tokens * state * channels,
                transcendentals=0,
                bytes_accessed=8 * tokens * channels,
            ),
            name=name,
        )(first, own, other, base, edges, proj)

    if tensor == 4:
        (own, *leaving), first = lax.optimization_barrier((parts, flag))
        landed = [swap_with(v, "tensor", k) for k, v in zip(masks[1:], leaving)]
        mixed = finish(1, first, enter_f, other_f, mixed_loc, c_in, "mixed")
        landed, mixed = lax.optimization_barrier((landed, mixed))
        total = (own + landed[0] + landed[1] + landed[2]).astype(BF16)
        total, first = lax.optimization_barrier((total, first))
        landed = [swap_with(total, "tensor", k) for k in masks[1:]]
        grad_inputs = finish(0, first, enter_b, other_b, gx_loc, b_in, "grad_inputs")
        landed, grad_inputs = lax.optimization_barrier((landed, grad_inputs))
        summed = jnp.zeros((4,) + total.shape, BF16)
        for k, v in zip(masks, [total] + landed):
            summed = lax.dynamic_update_index_in_dim(summed, v, place ^ k, 0)
        grad_b, grad_c = summed[:, 0], summed[:, 1]
    else:
        mixed = finish(1, flag, enter_f, other_f, mixed_loc, c_in, "mixed")
        grad_inputs = finish(0, flag, enter_b, other_b, gx_loc, b_in, "grad_inputs")
        grad_b, grad_c = lax.psum(parts[0], "tensor").astype(BF16)
    return (mixed, grad_inputs, grad_b.reshape(tokens, state), grad_c.reshape(tokens, state))


def solution(mesh):
    in_specs = (
        P("context", "tensor"),
        P("tensor", "context"),
        P("tensor"),
        P("tensor"),
        P("context", None),
        P("context", None),
        P("context"),
        P("context", "tensor"),
    )
    out_specs = (
        P("context", "tensor"),
        P("context", "tensor"),
        P("context", None),
        P("context", None),
    )
    return jax.shard_map(shards, mesh=mesh, in_specs=in_specs, out_specs=out_specs, check_vma=False)
```

```python
import functools

import jax
import jax.numpy as jnp
from jax import lax
from jax.experimental import pallas as pl
from jax.experimental.pallas import tpu as pltpu
from jax.sharding import PartitionSpec as P

BLOCK = 128
LANES = 128
F32 = jnp.float32
BF16 = jnp.bfloat16
NEVER = -200.0
MASKED = -1e30
BOUND = 6.0 * 1.796875
STEP = 1024.0
META = 8
STATES_VMEM, LOCAL_VMEM, GRADS_VMEM, OUTPUT_VMEM = 62, 60, 48, 60

NN = (((1,), (0,)), ((), ()))
NT = (((1,), (1,)), ((), ()))
TN = (((0,), (0,)), ((), ()))


def dot(a, b, dims):
    return lax.dot_general(a, b, dims, preferred_element_type=F32)


def split2(x):
    hi = x.astype(BF16)
    lo = (x - hi.astype(F32)).astype(BF16)
    return hi, lo


def split3(x):
    hi = x.astype(BF16)
    rest = x - hi.astype(F32)
    mid = rest.astype(BF16)
    lo = (rest - mid.astype(F32)).astype(BF16)
    return hi, mid, lo


def iota(shape, axis):
    return lax.broadcasted_iota(jnp.int32, shape, axis)


def block_sums(step, decay, doc):
    log_decay = -step * decay
    tri = jnp.where(iota((BLOCK, BLOCK), 0) >= iota((BLOCK, BLOCK), 1), 1.0, 0.0).astype(BF16)
    out = []
    for first in range(0, step.shape[1], BLOCK):
        cols = slice(first, first + BLOCK)
        parts = split3(log_decay[:, cols])
        starts = jnp.broadcast_to(doc[:, cols].astype(F32), (16, BLOCK)).astype(BF16)
        down = functools.reduce(jnp.add, [dot(tri, part, NT) for part in parts])
        across = functools.reduce(jnp.add, [dot(part, tri, NT) for part in parts])
        count_down = dot(tri, starts, NT)[:, :1]
        count_across = dot(starts, tri, NT)[:1]
        out.append((down, across, count_down, count_across))
    return out


def edge_weights(step, sums):
    eye = jnp.where(iota((BLOCK, BLOCK), 0) == iota((BLOCK, BLOCK), 1), 1.0, 0.0).astype(BF16)
    blocks = len(sums)
    ends = [s[0][BLOCK - 1 :] for s in sums]
    counts = [s[2][BLOCK - 1 :] for s in sums]
    keep, last = [], []
    for k in range(blocks):
        down, _, count_down, _ = sums[k]
        sum_before = down
        starts_before = count_down
        sum_after = ends[k] - down
        starts_after = counts[k] - count_down
        for j in range(k):
            sum_before = sum_before + ends[j]
            starts_before = starts_before + counts[j]
        for j in range(k + 1, blocks):
            sum_after = sum_after + ends[j]
            starts_after = starts_after + counts[j]
        parts = split3(step[:, k * BLOCK : (k + 1) * BLOCK])
        step_down = functools.reduce(jnp.add, [dot(eye, part, NT) for part in parts])
        keep.append(jnp.where(starts_before == 0.0, jnp.exp(sum_before), 0.0))
        last.append(jnp.where(starts_after == 0.0, jnp.exp(sum_after) * step_down, 0.0))
    total = functools.reduce(jnp.add, ends)
    starts = functools.reduce(jnp.add, counts)
    total = jnp.where(starts == 0.0, jnp.maximum(total, NEVER), NEVER)
    return jnp.concatenate(keep, 0), jnp.concatenate(last, 0), total


def spread_rows(rows, first, width, columns, skipped):
    heads = rows // 4
    row = iota((rows, 1), 0) - skipped * heads
    head = jnp.where(row >= heads, row - heads, row)
    head = jnp.where((row >= 0) & (row < 2 * heads), head, -rows * rows)
    offset = iota((1, columns), 1) - (head - first) * width
    return jnp.where((offset >= 0) & (offset < width), 1.0, 0.0).astype(BF16)


def last_spread(rows, first, width, columns):
    return spread_rows(rows, first, width, columns, 0)


def keep_spread(rows, first, width, columns):
    return spread_rows(rows, first, width, columns, 2)


SPREADS = (last_spread, keep_spread)


def pieces(total, most=256):
    return [slice(k, min(k + most, total)) for k in range(0, total, most)]


def fetch(pairs, sems):
    copies = [pltpu.make_async_copy(src, dst, sems.at[k]) for k, (src, dst) in enumerate(pairs)]
    for copy in copies:
        copy.start()
    return copies


def column(row):
    shape = (row.shape[1], row.shape[1])
    spot = iota(shape, 0) == iota(shape, 1)
    return jnp.sum(jnp.where(spot, row, 0.0), axis=1, keepdims=True)


def states_kernel(
    group, width, core_ref, x_hbm, g_hbm, step_hbm, decay_hbm, doc_hbm, b_hbm, c_hbm,
    mine_ref, send_ref, meta_ref, edges_ref, x_ref, g_ref, step_ref, decay_ref, doc_ref, b_ref,
    c_ref, b_t, c_t, meta, small_sems, big_sems,
):
    step_id = pl.program_id(0)
    groups = x_ref.shape[0]
    half = b_t.shape[0] // 2
    wide = group * width
    chunks = wide // LANES

    def big(k):
        return [
            pltpu.make_async_copy(
                src.at[:, pl.ds(pl.multiple_of(k * wide, LANES), wide)], dst.at[k], big_sems.at[n, k]
            )
            for n, (src, dst) in enumerate(((x_hbm, x_ref), (g_hbm, g_ref)))
        ]

    @pl.when(step_id == 0)
    def _():
        small = fetch(
            (
                (step_hbm, step_ref),
                (decay_hbm, decay_ref),
                (doc_hbm, doc_ref),
                (b_hbm, b_ref),
                (c_hbm, c_ref),
            ),
            small_sems,
        )
        for k in range(groups):
            for copy in big(k):
                copy.start()
        for copy in small:
            copy.wait()
        swap = core_ref[0] == 1
        step = step_ref[...]
        sums = block_sums(step, column(decay_ref[...]), doc_ref[...])
        keep, last, total = edge_weights(step, sums)
        bound_f = BOUND * jnp.sum(last, axis=0, keepdims=True)
        bound_b = BOUND * jnp.sum(keep, axis=0, keepdims=True)
        rows = [total, jnp.exp(total), bound_f, bound_b]
        rows = jnp.concatenate(rows + [jnp.zeros((META - 4, total.shape[1]), F32)], 0)
        high, mid, low = split3(rows)
        meta[...] = jnp.concatenate([high, mid, low, jnp.zeros_like(high)], 1)
        edges_ref[...] = jnp.concatenate(split2(last) + split2(keep), 1)
        for ref, out in ((b_ref, b_t), (c_ref, c_t)):
            turned = ref[...].astype(F32).T
            swapped = jnp.concatenate([turned[half:], turned[:half]], 0)
            out[...] = jnp.where(swap, swapped, turned).astype(BF16)

    for copy in big(step_id):
        copy.wait()
    edges = edges_ref[...]
    spreads = [make(edges.shape[1], step_id * group, width, wide) for make in SPREADS]
    rows = dot(meta[...], spreads[0] + spreads[1], NN)
    for k in range(chunks):
        for n in range(META):
            meta_ref[n, pl.ds(step_id * chunks + k, 1)] = rows[n : n + 1, k * LANES : (k + 1) * LANES]
    for kind, (ref, turned) in enumerate(((x_ref, b_t), (g_ref, c_t))):
        turned = turned[...]
        for lanes in pieces(wide):
            scale = dot(edges, spreads[kind][:, lanes], NN)
            scaled = split2(ref[step_id, :, lanes].astype(F32) * scale)
            state = dot(turned, scaled[0], NN) + dot(turned, scaled[1], NN)
            for k in range(state.shape[1] // LANES):
                part = state[:, k * LANES : (k + 1) * LANES]
                at = lanes.start // LANES + k
                mine_ref[at, kind * half : (kind + 1) * half] = part[:half]
                send_ref[at, kind * half : (kind + 1) * half] = part[half:]


def write_rows(masks, place_ref, total, out_ref):
    rows = total.shape[1] // len(masks)
    for k, mask in enumerate(masks):
        at = pl.ds(pl.multiple_of((place_ref[0] ^ mask) * rows, rows), rows)
        for slot in range(2):
            out_ref[k, slot] = total[slot, at]


def local_kernel(
    group, width, masks, skip_ref, place_ref, x_ref, g_ref, step_ref, step_blk, decay_ref, doc_ref, b_ref, c_ref,
    mixed_ref, gx_ref, grads_ref, down_s, across_s, bias, inter, common, sums_s,
):
    step_id = pl.program_id(0)
    groups = down_s.shape[1]
    pairs = ((0, 0), (1, 0), (1, 1))

    @pl.when(step_id == 0)
    def _():
        step = step_ref[...]
        sums = block_sums(step, column(decay_ref[...]), doc_ref[...])
        for k in range(groups):
            heads = slice(k * group, (k + 1) * group)
            for j in range(2):
                down_s[j, k] = sums[j][0][:, heads]
                across_s[j, k] = sums[j][1][heads]
        for n, (t, s) in enumerate(pairs):
            if t == s:
                ok = sums[t][2] == sums[s][3]
                ok = ok & (iota((BLOCK, BLOCK), 0) >= iota((BLOCK, BLOCK), 1))
            else:
                ok = sums[t][2] == sums[s][3] - sums[s][3][:, BLOCK - 1 :]
            bias[n] = jnp.where(ok, 0.0, MASKED)
            inter[n] = dot(
                c_ref[t * BLOCK : (t + 1) * BLOCK], b_ref[s * BLOCK : (s + 1) * BLOCK], NT
            )
        common[...] = jnp.zeros_like(common)

    down = [down_s[j, step_id] for j in range(2)]
    across = [across_s[j, step_id] for j in range(2)]
    left = iota((BLOCK, LANES), 1) < width
    left2 = iota((2 * BLOCK, LANES), 1) < width
    for k in range(group * width // LANES):
        lanes = slice(k * LANES, (k + 1) * LANES)
        xs = [x_ref[j * BLOCK : (j + 1) * BLOCK, lanes] for j in range(2)]
        gs = [g_ref[j * BLOCK : (j + 1) * BLOCK, lanes] for j in range(2)]
        zero = jnp.zeros_like(gs[0])
        halves = [
            jnp.concatenate([jnp.where(left, v, zero), jnp.where(left, zero, v)], 0) for v in gs
        ]
        inner = [dot(halves[t], xs[s], NT) for t, s in pairs]
        twice_x = [jnp.concatenate([v, v], 0) for v in xs]
        twice_g = [jnp.concatenate([v, v], 0) for v in gs]
        both_x = jnp.concatenate(twice_x, 0)
        both_g = jnp.concatenate(twice_g, 0)
        mixed_parts, gx_parts = [], []
        totals = [None] * 3
        for e in range(2):
            h = 2 * k + e
            parts = []
            for n, (t, s) in enumerate(pairs):
                row = across[s][h : h + 1]
                if t != s:
                    row = row - row[:, BLOCK - 1 :]
                weight = jnp.exp(jnp.minimum(down[t][:, h : h + 1] - row, 0.0) + bias[n])
                weight = weight * step_blk[h : h + 1, s * BLOCK : (s + 1) * BLOCK]
                term = weight * inner[n][e * BLOCK : (e + 1) * BLOCK]
                totals[n] = term if e == 0 else totals[n] + term
                parts.append(split2(weight * inter[n]))
            p00, p10, p11 = parts
            mixed_parts.append(
                (
                    dot(jnp.concatenate(p00, 1), twice_x[0], NN),
                    dot(jnp.concatenate(p10 + p11, 1), both_x, NN),
                )
            )
            gx_parts.append(
                (
                    dot(jnp.concatenate(p00 + p10, 0), both_g, TN),
                    dot(jnp.concatenate(p11, 0), twice_g[1], TN),
                )
            )
        for n in range(3):
            common[n] += totals[n]
        first = step_id * group + 2 * k
        skip = jnp.where(left, skip_ref[first], skip_ref[first + 1])
        for j in range(2):
            rows = slice(j * BLOCK, (j + 1) * BLOCK)
            mixed_ref[rows, lanes] = (
                jnp.where(left, mixed_parts[0][j], mixed_parts[1][j]) + skip * xs[j].astype(F32)
            )
            gx_ref[rows, lanes] = (
                jnp.where(left, gx_parts[0][j], gx_parts[1][j]) + skip * gs[j].astype(F32)
            )

    @pl.when(step_id == pl.num_programs(0) - 1)
    def _():
        c00, c10, c11 = [split2(common[n]) for n in range(3)]
        b0, b1 = b_ref[:BLOCK], b_ref[BLOCK:]
        c0, c1 = c_ref[:BLOCK], c_ref[BLOCK:]
        sums_s[0, :BLOCK] = sum(dot(v, c0, TN) for v in c00) + sum(dot(v, c1, TN) for v in c10)
        sums_s[0, BLOCK:] = sum(dot(v, c1, TN) for v in c11)
        sums_s[1, :BLOCK] = sum(dot(v, b0, NN) for v in c00)
        sums_s[1, BLOCK:] = sum(dot(v, b0, NN) for v in c10) + sum(dot(v, b1, NN) for v in c11)
        write_rows(masks, place_ref, sums_s, grads_ref)


def place_state(core, own, other, high, low):
    half = own.shape[1]
    for part, first in ((own, core), (other, 1 - core)):
        rows = pl.ds(pl.multiple_of(first * half, half), half)
        for k in range(own.shape[0]):
            lanes = slice(k * LANES, (k + 1) * LANES)
            hi, lo = split2(part[k])
            high[rows, lanes] = hi
            low[rows, lanes] = lo


def grads_kernel(
    group, width, masks, core_ref, place_ref, own_f, other_f, own_b, other_b, x_ref, g_ref, edges_ref,
    out_ref, both, total,
):
    step_id = pl.program_id(0)
    state = total.shape[2]

    @pl.when(step_id == 0)
    def _():
        total[...] = jnp.zeros_like(total)

    edges = edges_ref[...]
    for slot, own, other, ref in ((0, own_b, other_b, x_ref), (1, own_f, other_f, g_ref)):
        place_state(core_ref[0], own, other, both.at[slot], both.at[slot, state:])
        spread = SPREADS[slot](edges.shape[1], step_id * group, width, group * width)
        high, low = split2(ref[...].astype(F32) * dot(edges, spread, NN))
        product = dot(high, both[slot], NT)
        product = product[:, :state] + product[:, state:]
        total[slot] += product + dot(low, both[slot, :state], NT)

    @pl.when(step_id == pl.num_programs(0) - 1)
    def _():
        write_rows(masks, place_ref, total, out_ref)


def output_kernel(
    group, width, kind, core_ref, own, other, base_ref, edges_ref, proj_ref, out_ref, high, low
):
    place_state(core_ref[0], own, other, high, low)
    edges = edges_ref[...]
    wide = group * width
    spread = SPREADS[kind](edges.shape[1], pl.program_id(0) * group, width, wide)
    proj = proj_ref[...]
    for lanes in pieces(wide):
        scale = dot(edges, spread[:, lanes], NN)
        carried = dot(proj, high[:, lanes], NN) + dot(proj, low[:, lanes], NN)
        out_ref[:, lanes] = (base_ref[:, lanes] + scale * carried).astype(BF16)


def whole(shape):
    return pl.BlockSpec(shape, lambda i: (0,) * len(shape))


SMEM = pl.BlockSpec(memory_space=pltpu.SMEM)
HBM = pl.BlockSpec(memory_space=pltpu.HBM)


def grant(mib):
    return pltpu.CompilerParams(vmem_limit_bytes=mib << 20)


def swap_with(value, axis, mask):
    size = lax.axis_size(axis)
    return lax.ppermute(value, axis, [(i, i ^ mask) for i in range(size)])


def scan_chips(total_f, total_b, total_l, axis):
    size, index = lax.axis_size(axis), lax.axis_index(axis)
    before, after = jnp.zeros_like(total_f), jnp.zeros_like(total_b)
    log_before, log_after = jnp.zeros_like(total_l), jnp.zeros_like(total_l)
    bit = 2
    while bit < size:
        other_f, other_b, other_l = [swap_with(v, axis, bit) for v in (total_f, total_b, total_l)]
        upper = (index & bit) != 0
        before = jnp.where(upper, jnp.exp(log_before) * other_f + before, before)
        after = jnp.where(upper, after, jnp.exp(log_after) * other_b + after)
        log_before = jnp.where(upper, log_before + other_l, log_before)
        log_after = jnp.where(upper, log_after, log_after + other_l)
        scale, other_scale = jnp.exp(total_l), jnp.exp(other_l)
        total_f = jnp.where(upper, scale * other_f + total_f, other_scale * total_f + other_f)
        total_b = jnp.where(upper, other_b + other_scale * total_b, total_b + scale * other_b)
        total_l = jnp.maximum(total_l + other_l, NEVER)
        bit *= 2
    return before, after


def encode(state, bound, log_decay):
    power = jnp.clip(jnp.ceil(jnp.log2(bound)), -100.0, 120.0)
    data = state * jnp.exp2(14.0 - power)[:, None]
    first = lax.reduce_precision(log_decay, 5, 10)
    second = lax.reduce_precision(log_decay - first, 8, 10)
    third = lax.reduce_precision(log_decay - first - second, 8, 10)
    rows = [data.reshape(-1, LANES), first, second * STEP, third * STEP**2, power]
    return jnp.concatenate([v.astype(jnp.float16) for v in rows], 0)


def decode(coded, chunks):
    size = coded.shape[0] - 4 * chunks
    rows = [coded[size + k * chunks : size + (k + 1) * chunks].astype(F32) for k in range(4)]
    state = coded[:size].reshape(chunks, -1, LANES)
    return state, jnp.exp2(rows[3] - 14.0), jnp.exp(rows[0] + (rows[1] + rows[2] / STEP) / STEP)


def chip_place(axis):
    index = lax.axis_index(axis)
    return (index >> 1) & 1, (index >> 2) & 1


def pack_chip(total_f, total_b, bound_f, bound_b, log_decay, axis):
    return [
        encode(
            jnp.where(first, total_f, total_b), jnp.where(first, bound_f, bound_b), log_decay
        )
        for first in [bit == 0 for bit in chip_place(axis)]
    ]


def join_chips(arrived, axis, chunks):
    x, y = chip_place(axis)
    states, scales, decays = zip(*[decode(v, chunks) for v in arrived])
    _, two, three = decays
    same, upper = x == y, y == 1
    beyond = jnp.where(same, decays[0], 1.0)
    weights = [
        jnp.ones_like(two),
        beyond * jnp.where(same, 1.0, three),
        beyond * jnp.where(same, two, 1.0),
    ]
    weights = [w * scale for w, scale in zip(weights, scales)]
    main = [jnp.where(same, weights[0], 0.0)] + weights[1:]
    side = [jnp.where(same, 0.0, weights[0]), 0.0, 0.0]
    before = [jnp.where(upper, m, s) for m, s in zip(main, side)]
    after = [jnp.where(upper, s, m) for m, s in zip(main, side)]
    return states, before, after


def weigh(terms):
    return functools.reduce(jnp.add, [w[:, None] * v.astype(F32) for w, v in terms])


def shards(inputs, step_size, decay_rate, skip, b_in, c_in, doc_start, cotangent):
    heads, tokens = step_size.shape
    channels = inputs.shape[1]
    width = channels // heads
    state = b_in.shape[1]
    half = state // 2
    group = min(8, heads)
    groups = heads // group
    wide = group * width
    per = wide // LANES
    chunks = channels // LANES
    context, tensor = lax.axis_size("context"), lax.axis_size("tensor")
    core = lax.axis_index("context") & 1
    flag = core.reshape(1).astype(jnp.int32)
    decay = decay_rate.reshape(1, heads)
    doc = doc_start.reshape(1, tokens)

    tok = pl.BlockSpec((tokens, wide), lambda i: (0, i))
    piece = pl.BlockSpec((per, state, LANES), lambda i: (i, 0, 0))
    sgroup = min(32, heads)
    sgroups = heads // sgroup
    swide = sgroup * width
    piece = pl.BlockSpec((swide // LANES, state, LANES), lambda i: (i, 0, 0))
    mine, send, raw_meta, edges = pl.pallas_call(
        functools.partial(states_kernel, sgroup, width),
        grid=(sgroups,),
        in_specs=[SMEM] + [HBM] * 7,
        out_specs=[piece, piece, whole((META, chunks, LANES)), whole((tokens, 4 * heads))],
        out_shape=[jax.ShapeDtypeStruct((chunks, state, LANES), F32)] * 2
        + [
            jax.ShapeDtypeStruct((META, chunks, LANES), F32),
            jax.ShapeDtypeStruct((tokens, 4 * heads), BF16),
        ],
        scratch_shapes=[
            pltpu.VMEM((sgroups, tokens, swide), BF16),
            pltpu.VMEM((sgroups, tokens, swide), BF16),
            pltpu.VMEM((heads, tokens), F32),
            pltpu.VMEM((1, heads), F32),
            pltpu.VMEM((1, tokens), jnp.int32),
            pltpu.VMEM((tokens, state), BF16),
            pltpu.VMEM((tokens, state), BF16),
            pltpu.VMEM((state, tokens), BF16),
            pltpu.VMEM((state, tokens), BF16),
            pltpu.VMEM((META, 4 * heads), BF16),
            pltpu.SemaphoreType.DMA((5,)),
            pltpu.SemaphoreType.DMA((2, sgroups)),
        ],
        compiler_params=grant(STATES_VMEM),
        name="states",
    )(flag, inputs, cotangent, step_size, decay, doc, b_in, c_in)

    least = float(jnp.finfo(F32).min)
    meta, mine = lax.optimization_barrier((jnp.maximum(raw_meta, NEVER), jnp.maximum(mine, least)))
    theirs = swap_with(send, "context", 1)
    sib_meta = swap_with(raw_meta, "context", 1)
    lower = core == 0
    own_f, own_b = mine[:, :half], mine[:, half:]
    sib_f, sib_b = theirs[:, :half], theirs[:, half:]
    own_l, own_e, own_mf, own_mb = [meta[k] for k in range(4)]
    sib_l, sib_e, sib_mf, sib_mb = [sib_meta[k] for k in range(4)]
    f_own, f_sib = jnp.where(lower, sib_e, 1.0), jnp.where(lower, 1.0, own_e)
    b_own, b_sib = jnp.where(lower, 1.0, sib_e), jnp.where(lower, own_e, 1.0)
    chip_f = f_own[:, None] * own_f + f_sib[:, None] * sib_f
    chip_b = b_own[:, None] * own_b + b_sib[:, None] * sib_b
    chip_l = jnp.maximum(own_l + sib_l, NEVER)
    if context == 8:
        near, far = pack_chip(
            chip_f,
            chip_b,
            f_own * own_mf + f_sib * sib_mf,
            b_own * own_mb + b_sib * sib_mb,
            chip_l,
            "context",
        )
        near, far, skip = lax.optimization_barrier((near, far, skip))
        arrived = [
            swap_with(near, "context", 2),
            swap_with(far, "context", 4),
            swap_with(far, "context", 6),
        ]

    full = jax.ShapeDtypeStruct((tokens, channels), F32)
    masks = (0, 2, 3, 1) if tensor == 4 else (0,)
    rows = tokens // len(masks)
    place = lax.axis_index("tensor")
    part = jax.ShapeDtypeStruct((len(masks), 2, rows, state), F32)
    spot = place.reshape(1) if tensor == 4 else jnp.zeros((1,), jnp.int32)
    mixed_loc, gx_loc, grads_loc = pl.pallas_call(
        functools.partial(local_kernel, group, width, masks),
        grid=(groups,),
        in_specs=[
            SMEM,
            SMEM,
            tok,
            tok,
            whole((heads, tokens)),
            pl.BlockSpec((group, tokens), lambda i: (i, 0)),
            whole((1, heads)),
            whole((1, tokens)),
            whole((tokens, state)),
            whole((tokens, state)),
        ],
        out_specs=[tok, tok, whole(part.shape)],
        out_shape=[full, full, part],
        scratch_shapes=[
            pltpu.VMEM((2, groups, BLOCK, group), F32),
            pltpu.VMEM((2, groups, group, BLOCK), F32),
            pltpu.VMEM((3, BLOCK, BLOCK), F32),
            pltpu.VMEM((3, BLOCK, BLOCK), F32),
            pltpu.VMEM((3, BLOCK, BLOCK), F32),
            pltpu.VMEM((2, tokens, state), F32),
        ],
        compiler_params=grant(LOCAL_VMEM),
        cost_estimate=pl.CostEstimate(
            flops=20 * tokens * tokens * channels,
            transcendentals=heads * tokens * tokens,
            bytes_accessed=12 * tokens * channels,
        ),
        name="local",
    )(skip, spot, inputs, cotangent, step_size, step_size, decay, doc, b_in, c_in)

    one, zero = jnp.ones_like(own_e), jnp.zeros_like(own_e)
    if context == 8:
        arrived, grads_loc = lax.optimization_barrier((arrived, grads_loc))
        states, before, after = join_chips(arrived, "context", chunks)
    else:
        states = scan_chips(chip_f, chip_b, chip_l[:, None], "context")
        before, after = [one, zero], [zero, one]
    pass_f = jnp.where(lower, own_e, 1.0)
    pass_b = jnp.where(lower, 1.0, own_e)
    keep_f = jnp.where(lower, 1.0, sib_e)
    keep_b = jnp.where(lower, sib_e, 1.0)
    at_lower = jnp.where(lower, one, zero)
    at_upper = jnp.where(lower, zero, one)
    weights = (
        [pass_f * w for w in before],
        [pass_b * w for w in after],
        [keep_f * w for w in before],
        [keep_b * w for w in after],
    )
    passed_f = weigh([*zip(weights[0], states), (at_lower, own_f)])
    passed_b = weigh([*zip(weights[1], states), (at_upper, own_b)])
    passed_f, passed_b, weights, states = lax.optimization_barrier(
        (passed_f, passed_b, weights, states)
    )
    other_f = swap_with(passed_f, "context", 1)
    other_b = swap_with(passed_b, "context", 1)
    enter_f = weigh([*zip(weights[2], states), (at_upper, sib_f)])
    enter_b = weigh([*zip(weights[3], states), (at_lower, sib_b)])

    ggroup = min(32, heads)
    gwide = ggroup * width
    gtok = pl.BlockSpec((tokens, gwide), lambda i: (0, i))
    gstate = pl.BlockSpec((gwide // LANES, half, LANES), lambda i: (i, 0, 0))
    carried = pl.pallas_call(
        functools.partial(grads_kernel, ggroup, width, masks),
        grid=(heads // ggroup,),
        in_specs=[SMEM, SMEM] + [gstate] * 4 + [gtok, gtok, whole((tokens, 4 * heads))],
        out_specs=whole(part.shape),
        out_shape=part,
        scratch_shapes=[
            pltpu.VMEM((2, 2 * state, gwide), BF16),
            pltpu.VMEM((2, tokens, state), F32),
        ],
        compiler_params=grant(GRADS_VMEM),
        name="grads",
    )(
        flag, spot, enter_f, other_f, enter_b, other_b, inputs, cotangent, edges
    )
    parts = [carried[k] + grads_loc[k] for k in range(len(masks))]

    state_spec = pl.BlockSpec((per, half, LANES), lambda i: (i, 0, 0))

    def finish(kind, first, own, other, base, proj, name):
        return pl.pallas_call(
            functools.partial(output_kernel, group, width, kind),
            grid=(groups,),
            in_specs=[
                SMEM,
                state_spec,
                state_spec,
                tok,
                whole((tokens, 4 * heads)),
                whole((tokens, state)),
            ],
            out_specs=tok,
            out_shape=jax.ShapeDtypeStruct((tokens, channels), BF16),
            scratch_shapes=[pltpu.VMEM((state, wide), BF16)] * 2,
            compiler_params=grant(OUTPUT_VMEM),
            cost_estimate=pl.CostEstimate(
                flops=4 * tokens * state * channels,
                transcendentals=0,
                bytes_accessed=8 * tokens * channels,
            ),
            name=name,
        )(first, own, other, base, edges, proj)

    if tensor == 4:
        (own, *leaving), first = lax.optimization_barrier((parts, flag))
        landed = [swap_with(v, "tensor", k) for k, v in zip(masks[1:], leaving)]
        mixed = finish(1, first, enter_f, other_f, mixed_loc, c_in, "mixed")
        landed, mixed = lax.optimization_barrier((landed, mixed))
        total = (own + landed[0] + landed[1] + landed[2]).astype(BF16)
        total, first = lax.optimization_barrier((total, first))
        landed = [swap_with(total, "tensor", k) for k in masks[1:]]
        grad_inputs = finish(0, first, enter_b, other_b, gx_loc, b_in, "grad_inputs")
        landed, grad_inputs = lax.optimization_barrier((landed, grad_inputs))
        summed = jnp.zeros((4,) + total.shape, BF16)
        for k, v in zip(masks, [total] + landed):
            summed = lax.dynamic_update_index_in_dim(summed, v, place ^ k, 0)
        grad_b, grad_c = summed[:, 0], summed[:, 1]
    else:
        mixed = finish(1, flag, enter_f, other_f, mixed_loc, c_in, "mixed")
        grad_inputs = finish(0, flag, enter_b, other_b, gx_loc, b_in, "grad_inputs")
        grad_b, grad_c = lax.psum(parts[0], "tensor").astype(BF16)
    return (mixed, grad_inputs, grad_b.reshape(tokens, state), grad_c.reshape(tokens, state))


def solution(mesh):
    in_specs = (
        P("context", "tensor"),
        P("tensor", "context"),
        P("tensor"),
        P("tensor"),
        P("context", None),
        P("context", None),
        P("context"),
        P("context", "tensor"),
    )
    out_specs = (
        P("context", "tensor"),
        P("context", "tensor"),
        P("context", None),
        P("context", None),
    )
    return jax.shard_map(shards, mesh=mesh, in_specs=in_specs, out_specs=out_specs, check_vma=False)
```

```python
import functools

import jax
import jax.numpy as jnp
from jax import lax
from jax.experimental import pallas as pl
from jax.experimental.pallas import tpu as pltpu
from jax.sharding import PartitionSpec as P

BLOCK = 128
LANES = 128
F32 = jnp.float32
BF16 = jnp.bfloat16
NEVER = -200.0
MASKED = -1e30
BOUND = 6.0 * 1.796875
STEP = 1024.0
META = 8
STATES_VMEM, LOCAL_VMEM, GRADS_VMEM, OUTPUT_VMEM = 62, 60, 48, 60

NN = (((1,), (0,)), ((), ()))
NT = (((1,), (1,)), ((), ()))
TN = (((0,), (0,)), ((), ()))


def dot(a, b, dims):
    return lax.dot_general(a, b, dims, preferred_element_type=F32)


def split2(x):
    hi = x.astype(BF16)
    lo = (x - hi.astype(F32)).astype(BF16)
    return hi, lo


def split3(x):
    hi = x.astype(BF16)
    rest = x - hi.astype(F32)
    mid = rest.astype(BF16)
    lo = (rest - mid.astype(F32)).astype(BF16)
    return hi, mid, lo


def iota(shape, axis):
    return lax.broadcasted_iota(jnp.int32, shape, axis)


def block_sums(step, decay, doc):
    log_decay = -step * decay
    tri = jnp.where(iota((BLOCK, BLOCK), 0) >= iota((BLOCK, BLOCK), 1), 1.0, 0.0).astype(BF16)
    out = []
    for first in range(0, step.shape[1], BLOCK):
        cols = slice(first, first + BLOCK)
        parts = split3(log_decay[:, cols])
        starts = jnp.broadcast_to(doc[:, cols].astype(F32), (16, BLOCK)).astype(BF16)
        down = functools.reduce(jnp.add, [dot(tri, part, NT) for part in parts])
        across = functools.reduce(jnp.add, [dot(part, tri, NT) for part in parts])
        count_down = dot(tri, starts, NT)[:, :1]
        count_across = dot(starts, tri, NT)[:1]
        out.append((down, across, count_down, count_across))
    return out


def edge_weights(step, sums):
    eye = jnp.where(iota((BLOCK, BLOCK), 0) == iota((BLOCK, BLOCK), 1), 1.0, 0.0).astype(BF16)
    blocks = len(sums)
    ends = [s[0][BLOCK - 1 :] for s in sums]
    counts = [s[2][BLOCK - 1 :] for s in sums]
    keep, last = [], []
    for k in range(blocks):
        down, _, count_down, _ = sums[k]
        sum_before = down
        starts_before = count_down
        sum_after = ends[k] - down
        starts_after = counts[k] - count_down
        for j in range(k):
            sum_before = sum_before + ends[j]
            starts_before = starts_before + counts[j]
        for j in range(k + 1, blocks):
            sum_after = sum_after + ends[j]
            starts_after = starts_after + counts[j]
        parts = split3(step[:, k * BLOCK : (k + 1) * BLOCK])
        step_down = functools.reduce(jnp.add, [dot(eye, part, NT) for part in parts])
        keep.append(jnp.where(starts_before == 0.0, jnp.exp(sum_before), 0.0))
        last.append(jnp.where(starts_after == 0.0, jnp.exp(sum_after) * step_down, 0.0))
    total = functools.reduce(jnp.add, ends)
    starts = functools.reduce(jnp.add, counts)
    total = jnp.where(starts == 0.0, jnp.maximum(total, NEVER), NEVER)
    return jnp.concatenate(keep, 0), jnp.concatenate(last, 0), total


def spread_rows(rows, first, width, columns, skipped):
    heads = rows // 4
    row = iota((rows, 1), 0) - skipped * heads
    head = jnp.where(row >= heads, row - heads, row)
    head = jnp.where((row >= 0) & (row < 2 * heads), head, -rows * rows)
    offset = iota((1, columns), 1) - (head - first) * width
    return jnp.where((offset >= 0) & (offset < width), 1.0, 0.0).astype(BF16)


def last_spread(rows, first, width, columns):
    return spread_rows(rows, first, width, columns, 0)


def keep_spread(rows, first, width, columns):
    return spread_rows(rows, first, width, columns, 2)


SPREADS = (last_spread, keep_spread)


def pieces(total, most=256):
    return [slice(k, min(k + most, total)) for k in range(0, total, most)]


def fetch(pairs, sems):
    copies = [pltpu.make_async_copy(src, dst, sems.at[k]) for k, (src, dst) in enumerate(pairs)]
    for copy in copies:
        copy.start()
    return copies


def column(row):
    shape = (row.shape[1], row.shape[1])
    spot = iota(shape, 0) == iota(shape, 1)
    return jnp.sum(jnp.where(spot, row, 0.0), axis=1, keepdims=True)


def states_kernel(
    group, width, core_ref, x_hbm, g_hbm, step_hbm, decay_hbm, doc_hbm, b_hbm, c_hbm,
    mine_ref, send_ref, meta_ref, edges_ref, x_ref, g_ref, step_ref, decay_ref, doc_ref, b_ref,
    c_ref, b_t, c_t, meta, small_sems, big_sems,
):
    step_id = pl.program_id(0)
    groups = x_ref.shape[0]
    half = b_t.shape[0] // 2
    wide = group * width
    chunks = wide // LANES

    def big(k):
        return [
            pltpu.make_async_copy(
                src.at[:, pl.ds(pl.multiple_of(k * wide, LANES), wide)], dst.at[k], big_sems.at[n, k]
            )
            for n, (src, dst) in enumerate(((x_hbm, x_ref), (g_hbm, g_ref)))
        ]

    @pl.when(step_id == 0)
    def _():
        small = fetch(
            (
                (step_hbm, step_ref),
                (decay_hbm, decay_ref),
                (doc_hbm, doc_ref),
                (b_hbm, b_ref),
                (c_hbm, c_ref),
            ),
            small_sems,
        )
        for k in range(groups):
            for copy in big(k):
                copy.start()
        for copy in small:
            copy.wait()
        swap = core_ref[0] == 1
        step = step_ref[...]
        sums = block_sums(step, column(decay_ref[...]), doc_ref[...])
        keep, last, total = edge_weights(step, sums)
        bound_f = BOUND * jnp.sum(last, axis=0, keepdims=True)
        bound_b = BOUND * jnp.sum(keep, axis=0, keepdims=True)
        rows = [total, jnp.exp(total), bound_f, bound_b]
        rows = jnp.concatenate(rows + [jnp.zeros((META - 4, total.shape[1]), F32)], 0)
        high, mid, low = split3(rows)
        meta[...] = jnp.concatenate([high, mid, low, jnp.zeros_like(high)], 1)
        edges_ref[...] = jnp.concatenate(split2(last) + split2(keep), 1)
        for ref, out in ((b_ref, b_t), (c_ref, c_t)):
            turned = ref[...].astype(F32).T
            swapped = jnp.concatenate([turned[half:], turned[:half]], 0)
            out[...] = jnp.where(swap, swapped, turned).astype(BF16)

    for copy in big(step_id):
        copy.wait()
    edges = edges_ref[...]
    spreads = [make(edges.shape[1], step_id * group, width, wide) for make in SPREADS]
    rows = dot(meta[...], spreads[0] + spreads[1], NN)
    for k in range(chunks):
        for n in range(META):
            meta_ref[n, pl.ds(step_id * chunks + k, 1)] = rows[n : n + 1, k * LANES : (k + 1) * LANES]
    for kind, (ref, turned) in enumerate(((x_ref, b_t), (g_ref, c_t))):
        turned = turned[...]
        for lanes in pieces(wide):
            scale = dot(edges, spreads[kind][:, lanes], NN)
            scaled = split2(ref[step_id, :, lanes].astype(F32) * scale)
            state = dot(turned, scaled[0], NN) + dot(turned, scaled[1], NN)
            for k in range(state.shape[1] // LANES):
                part = state[:, k * LANES : (k + 1) * LANES]
                at = lanes.start // LANES + k
                mine_ref[at, kind * half : (kind + 1) * half] = part[:half]
                send_ref[at, kind * half : (kind + 1) * half] = part[half:]


def write_rows(masks, place_ref, total, out_ref):
    rows = total.shape[1] // len(masks)
    for k, mask in enumerate(masks):
        at = pl.ds(pl.multiple_of((place_ref[0] ^ mask) * rows, rows), rows)
        for slot in range(2):
            out_ref[k, slot] = total[slot, at]


def local_kernel(
    group, width, masks, skip_ref, place_ref, x_ref, g_ref, step_ref, step_blk, decay_ref, doc_ref, b_ref, c_ref,
    mixed_ref, gx_ref, grads_ref, down_s, across_s, bias, inter, common, sums_s,
):
    step_id = pl.program_id(0)
    groups = down_s.shape[1]
    pairs = ((0, 0), (1, 0), (1, 1))

    @pl.when(step_id == 0)
    def _():
        step = step_ref[...]
        sums = block_sums(step, column(decay_ref[...]), doc_ref[...])
        for k in range(groups):
            heads = slice(k * group, (k + 1) * group)
            for j in range(2):
                down_s[j, k] = sums[j][0][:, heads]
                across_s[j, k] = sums[j][1][heads]
        for n, (t, s) in enumerate(pairs):
            if t == s:
                ok = sums[t][2] == sums[s][3]
                ok = ok & (iota((BLOCK, BLOCK), 0) >= iota((BLOCK, BLOCK), 1))
            else:
                ok = sums[t][2] == sums[s][3] - sums[s][3][:, BLOCK - 1 :]
            bias[n] = jnp.where(ok, 0.0, MASKED)
            inter[n] = dot(
                c_ref[t * BLOCK : (t + 1) * BLOCK], b_ref[s * BLOCK : (s + 1) * BLOCK], NT
            )
        common[...] = jnp.zeros_like(common)

    down = [down_s[j, step_id] for j in range(2)]
    across = [across_s[j, step_id] for j in range(2)]
    left = iota((BLOCK, LANES), 1) < width
    left2 = iota((2 * BLOCK, LANES), 1) < width
    for k in range(group * width // LANES):
        lanes = slice(k * LANES, (k + 1) * LANES)
        xs = [x_ref[j * BLOCK : (j + 1) * BLOCK, lanes] for j in range(2)]
        gs = [g_ref[j * BLOCK : (j + 1) * BLOCK, lanes] for j in range(2)]
        zero = jnp.zeros_like(gs[0])
        halves = [
            jnp.concatenate([jnp.where(left, v, zero), jnp.where(left, zero, v)], 0) for v in gs
        ]
        inner = [dot(halves[t], xs[s], NT) for t, s in pairs]
        twice_x = [jnp.concatenate([v, v], 0) for v in xs]
        twice_g = [jnp.concatenate([v, v], 0) for v in gs]
        both_x = jnp.concatenate(twice_x, 0)
        both_g = jnp.concatenate(twice_g, 0)
        mixed_parts, gx_parts = [], []
        totals = [None] * 3
        for e in range(2):
            h = 2 * k + e
            parts = []
            for n, (t, s) in enumerate(pairs):
                row = across[s][h : h + 1]
                if t != s:
                    row = row - row[:, BLOCK - 1 :]
                weight = jnp.exp(jnp.minimum(down[t][:, h : h + 1] - row, 0.0) + bias[n])
                weight = weight * step_blk[h : h + 1, s * BLOCK : (s + 1) * BLOCK]
                term = weight * inner[n][e * BLOCK : (e + 1) * BLOCK]
                totals[n] = term if e == 0 else totals[n] + term
                parts.append(split2(weight * inter[n]))
            p00, p10, p11 = parts
            mixed_parts.append(
                (
                    dot(jnp.concatenate(p00, 1), twice_x[0], NN),
                    dot(jnp.concatenate(p10 + p11, 1), both_x, NN),
                )
            )
            gx_parts.append(
                (
                    dot(jnp.concatenate(p00 + p10, 0), both_g, TN),
                    dot(jnp.concatenate(p11, 0), twice_g[1], TN),
                )
            )
        for n in range(3):
            common[n] += totals[n]
        first = step_id * group + 2 * k
        skip = jnp.where(left, skip_ref[first], skip_ref[first + 1])
        for j in range(2):
            rows = slice(j * BLOCK, (j + 1) * BLOCK)
            mixed_ref[rows, lanes] = (
                jnp.where(left, mixed_parts[0][j], mixed_parts[1][j]) + skip * xs[j].astype(F32)
            )
            gx_ref[rows, lanes] = (
                jnp.where(left, gx_parts[0][j], gx_parts[1][j]) + skip * gs[j].astype(F32)
            )

    @pl.when(step_id == pl.num_programs(0) - 1)
    def _():
        c00, c10, c11 = [split2(common[n]) for n in range(3)]
        b0, b1 = b_ref[:BLOCK], b_ref[BLOCK:]
        c0, c1 = c_ref[:BLOCK], c_ref[BLOCK:]
        sums_s[0, :BLOCK] = sum(dot(v, c0, TN) for v in c00) + sum(dot(v, c1, TN) for v in c10)
        sums_s[0, BLOCK:] = sum(dot(v, c1, TN) for v in c11)
        sums_s[1, :BLOCK] = sum(dot(v, b0, NN) for v in c00)
        sums_s[1, BLOCK:] = sum(dot(v, b0, NN) for v in c10) + sum(dot(v, b1, NN) for v in c11)
        write_rows(masks, place_ref, sums_s, grads_ref)


def place_state(core, own, other, high, low):
    half = own.shape[1]
    for part, first in ((own, core), (other, 1 - core)):
        rows = pl.ds(pl.multiple_of(first * half, half), half)
        for k in range(own.shape[0]):
            lanes = slice(k * LANES, (k + 1) * LANES)
            hi, lo = split2(part[k])
            high[rows, lanes] = hi
            low[rows, lanes] = lo


def grads_kernel(
    group, width, masks, core_ref, place_ref, own_f, other_f, own_b, other_b, x_ref, g_ref, edges_ref,
    out_ref, both, total,
):
    step_id = pl.program_id(0)
    state = total.shape[2]

    @pl.when(step_id == 0)
    def _():
        total[...] = jnp.zeros_like(total)

    edges = edges_ref[...]
    for slot, own, other, ref in ((0, own_b, other_b, x_ref), (1, own_f, other_f, g_ref)):
        place_state(core_ref[0], own, other, both.at[slot], both.at[slot, state:])
        spread = SPREADS[slot](edges.shape[1], step_id * group, width, group * width)
        high, low = split2(ref[...].astype(F32) * dot(edges, spread, NN))
        product = dot(high, both[slot], NT)
        product = product[:, :state] + product[:, state:]
        total[slot] += product + dot(low, both[slot, :state], NT)

    @pl.when(step_id == pl.num_programs(0) - 1)
    def _():
        write_rows(masks, place_ref, total, out_ref)


def output_kernel(
    group, width, kind, core_ref, own, other, base_ref, edges_ref, proj_ref, out_ref, high, low
):
    place_state(core_ref[0], own, other, high, low)
    edges = edges_ref[...]
    wide = group * width
    spread = SPREADS[kind](edges.shape[1], pl.program_id(0) * group, width, wide)
    proj = proj_ref[...]
    for lanes in pieces(wide):
        scale = dot(edges, spread[:, lanes], NN)
        carried = dot(proj, high[:, lanes], NN) + dot(proj, low[:, lanes], NN)
        out_ref[:, lanes] = (base_ref[:, lanes] + scale * carried).astype(BF16)


def whole(shape):
    return pl.BlockSpec(shape, lambda i: (0,) * len(shape))


SMEM = pl.BlockSpec(memory_space=pltpu.SMEM)
HBM = pl.BlockSpec(memory_space=pltpu.HBM)


def grant(mib):
    return pltpu.CompilerParams(vmem_limit_bytes=mib << 20)


def swap_with(value, axis, mask):
    size = lax.axis_size(axis)
    return lax.ppermute(value, axis, [(i, i ^ mask) for i in range(size)])


def scan_chips(total_f, total_b, total_l, axis):
    size, index = lax.axis_size(axis), lax.axis_index(axis)
    before, after = jnp.zeros_like(total_f), jnp.zeros_like(total_b)
    log_before, log_after = jnp.zeros_like(total_l), jnp.zeros_like(total_l)
    bit = 2
    while bit < size:
        other_f, other_b, other_l = [swap_with(v, axis, bit) for v in (total_f, total_b, total_l)]
        upper = (index & bit) != 0
        before = jnp.where(upper, jnp.exp(log_before) * other_f + before, before)
        after = jnp.where(upper, after, jnp.exp(log_after) * other_b + after)
        log_before = jnp.where(upper, log_before + other_l, log_before)
        log_after = jnp.where(upper, log_after, log_after + other_l)
        scale, other_scale = jnp.exp(total_l), jnp.exp(other_l)
        total_f = jnp.where(upper, scale * other_f + total_f, other_scale * total_f + other_f)
        total_b = jnp.where(upper, other_b + other_scale * total_b, total_b + scale * other_b)
        total_l = jnp.maximum(total_l + other_l, NEVER)
        bit *= 2
    return before, after


def encode(state, bound, log_decay):
    power = jnp.clip(jnp.ceil(jnp.log2(bound)), -100.0, 120.0)
    data = state * jnp.exp2(14.0 - power)[:, None]
    first = lax.reduce_precision(log_decay, 5, 10)
    second = lax.reduce_precision(log_decay - first, 8, 10)
    rows = [data.reshape(-1, LANES), first, second * STEP, power]
    return jnp.concatenate([v.astype(jnp.float16) for v in rows], 0)


def decode(coded, chunks):
    size = coded.shape[0] - 3 * chunks
    rows = [coded[size + k * chunks : size + (k + 1) * chunks].astype(F32) for k in range(3)]
    state = coded[:size].reshape(chunks, -1, LANES)
    return state, jnp.exp2(rows[2] - 14.0), jnp.exp(rows[0] + rows[1] / STEP)


def chip_place(axis):
    index = lax.axis_index(axis)
    return (index >> 1) & 1, (index >> 2) & 1


def pack_chip(total_f, total_b, bound_f, bound_b, log_decay, axis):
    return [
        encode(
            jnp.where(first, total_f, total_b), jnp.where(first, bound_f, bound_b), log_decay
        )
        for first in [bit == 0 for bit in chip_place(axis)]
    ]


def join_chips(arrived, axis, chunks):
    x, y = chip_place(axis)
    states, scales, decays = zip(*[decode(v, chunks) for v in arrived])
    _, two, three = decays
    same, upper = x == y, y == 1
    beyond = jnp.where(same, decays[0], 1.0)
    weights = [
        jnp.ones_like(two),
        beyond * jnp.where(same, 1.0, three),
        beyond * jnp.where(same, two, 1.0),
    ]
    weights = [w * scale for w, scale in zip(weights, scales)]
    main = [jnp.where(same, weights[0], 0.0)] + weights[1:]
    side = [jnp.where(same, 0.0, weights[0]), 0.0, 0.0]
    before = [jnp.where(upper, m, s) for m, s in zip(main, side)]
    after = [jnp.where(upper, s, m) for m, s in zip(main, side)]
    return states, before, after


def weigh(terms):
    return functools.reduce(jnp.add, [w[:, None] * v.astype(F32) for w, v in terms])


def shards(inputs, step_size, decay_rate, skip, b_in, c_in, doc_start, cotangent):
    heads, tokens = step_size.shape
    channels = inputs.shape[1]
    width = channels // heads
    state = b_in.shape[1]
    half = state // 2
    group = min(8, heads)
    groups = heads // group
    wide = group * width
    per = wide // LANES
    chunks = channels // LANES
    context, tensor = lax.axis_size("context"), lax.axis_size("tensor")
    core = lax.axis_index("context") & 1
    flag = core.reshape(1).astype(jnp.int32)
    decay = decay_rate.reshape(1, heads)
    doc = doc_start.reshape(1, tokens)

    tok = pl.BlockSpec((tokens, wide), lambda i: (0, i))
    piece = pl.BlockSpec((per, state, LANES), lambda i: (i, 0, 0))
    sgroup = min(32, heads)
    sgroups = heads // sgroup
    swide = sgroup * width
    piece = pl.BlockSpec((swide // LANES, state, LANES), lambda i: (i, 0, 0))
    mine, send, raw_meta, edges = pl.pallas_call(
        functools.partial(states_kernel, sgroup, width),
        grid=(sgroups,),
        in_specs=[SMEM] + [HBM] * 7,
        out_specs=[piece, piece, whole((META, chunks, LANES)), whole((tokens, 4 * heads))],
        out_shape=[jax.ShapeDtypeStruct((chunks, state, LANES), F32)] * 2
        + [
            jax.ShapeDtypeStruct((META, chunks, LANES), F32),
            jax.ShapeDtypeStruct((tokens, 4 * heads), BF16),
        ],
        scratch_shapes=[
            pltpu.VMEM((sgroups, tokens, swide), BF16),
            pltpu.VMEM((sgroups, tokens, swide), BF16),
            pltpu.VMEM((heads, tokens), F32),
            pltpu.VMEM((1, heads), F32),
            pltpu.VMEM((1, tokens), jnp.int32),
            pltpu.VMEM((tokens, state), BF16),
            pltpu.VMEM((tokens, state), BF16),
            pltpu.VMEM((state, tokens), BF16),
            pltpu.VMEM((state, tokens), BF16),
            pltpu.VMEM((META, 4 * heads), BF16),
            pltpu.SemaphoreType.DMA((5,)),
            pltpu.SemaphoreType.DMA((2, sgroups)),
        ],
        compiler_params=grant(STATES_VMEM),
        name="states",
    )(flag, inputs, cotangent, step_size, decay, doc, b_in, c_in)

    least = float(jnp.finfo(F32).min)
    meta, mine = lax.optimization_barrier((jnp.maximum(raw_meta, NEVER), jnp.maximum(mine, least)))
    theirs = swap_with(send, "context", 1)
    sib_meta = swap_with(raw_meta, "context", 1)
    lower = core == 0
    own_f, own_b = mine[:, :half], mine[:, half:]
    sib_f, sib_b = theirs[:, :half], theirs[:, half:]
    own_l, own_e, own_mf, own_mb = [meta[k] for k in range(4)]
    sib_l, sib_e, sib_mf, sib_mb = [sib_meta[k] for k in range(4)]
    f_own, f_sib = jnp.where(lower, sib_e, 1.0), jnp.where(lower, 1.0, own_e)
    b_own, b_sib = jnp.where(lower, 1.0, sib_e), jnp.where(lower, own_e, 1.0)
    chip_f = f_own[:, None] * own_f + f_sib[:, None] * sib_f
    chip_b = b_own[:, None] * own_b + b_sib[:, None] * sib_b
    chip_l = jnp.maximum(own_l + sib_l, NEVER)
    if context == 8:
        near, far = pack_chip(
            chip_f,
            chip_b,
            f_own * own_mf + f_sib * sib_mf,
            b_own * own_mb + b_sib * sib_mb,
            chip_l,
            "context",
        )
        near, far, skip = lax.optimization_barrier((near, far, skip))
        arrived = [
            swap_with(near, "context", 2),
            swap_with(far, "context", 4),
            swap_with(far, "context", 6),
        ]

    full = jax.ShapeDtypeStruct((tokens, channels), F32)
    masks = (0, 2, 3, 1) if tensor == 4 else (0,)
    rows = tokens // len(masks)
    place = lax.axis_index("tensor")
    part = jax.ShapeDtypeStruct((len(masks), 2, rows, state), F32)
    spot = place.reshape(1) if tensor == 4 else jnp.zeros((1,), jnp.int32)
    mixed_loc, gx_loc, grads_loc = pl.pallas_call(
        functools.partial(local_kernel, group, width, masks),
        grid=(groups,),
        in_specs=[
            SMEM,
            SMEM,
            tok,
            tok,
            whole((heads, tokens)),
            pl.BlockSpec((group, tokens), lambda i: (i, 0)),
            whole((1, heads)),
            whole((1, tokens)),
            whole((tokens, state)),
            whole((tokens, state)),
        ],
        out_specs=[tok, tok, whole(part.shape)],
        out_shape=[full, full, part],
        scratch_shapes=[
            pltpu.VMEM((2, groups, BLOCK, group), F32),
            pltpu.VMEM((2, groups, group, BLOCK), F32),
            pltpu.VMEM((3, BLOCK, BLOCK), F32),
            pltpu.VMEM((3, BLOCK, BLOCK), F32),
            pltpu.VMEM((3, BLOCK, BLOCK), F32),
            pltpu.VMEM((2, tokens, state), F32),
        ],
        compiler_params=grant(LOCAL_VMEM),
        cost_estimate=pl.CostEstimate(
            flops=20 * tokens * tokens * channels,
            transcendentals=heads * tokens * tokens,
            bytes_accessed=12 * tokens * channels,
        ),
        name="local",
    )(skip, spot, inputs, cotangent, step_size, step_size, decay, doc, b_in, c_in)

    one, zero = jnp.ones_like(own_e), jnp.zeros_like(own_e)
    if context == 8:
        arrived, grads_loc = lax.optimization_barrier((arrived, grads_loc))
        states, before, after = join_chips(arrived, "context", chunks)
    else:
        states = scan_chips(chip_f, chip_b, chip_l[:, None], "context")
        before, after = [one, zero], [zero, one]
    pass_f = jnp.where(lower, own_e, 1.0)
    pass_b = jnp.where(lower, 1.0, own_e)
    keep_f = jnp.where(lower, 1.0, sib_e)
    keep_b = jnp.where(lower, sib_e, 1.0)
    at_lower = jnp.where(lower, one, zero)
    at_upper = jnp.where(lower, zero, one)
    weights = (
        [pass_f * w for w in before],
        [pass_b * w for w in after],
        [keep_f * w for w in before],
        [keep_b * w for w in after],
    )
    passed_f = weigh([*zip(weights[0], states), (at_lower, own_f)])
    passed_b = weigh([*zip(weights[1], states), (at_upper, own_b)])
    passed_f, passed_b, weights, states = lax.optimization_barrier(
        (passed_f, passed_b, weights, states)
    )
    other_f = swap_with(passed_f, "context", 1)
    other_b = swap_with(passed_b, "context", 1)
    enter_f = weigh([*zip(weights[2], states), (at_upper, sib_f)])
    enter_b = weigh([*zip(weights[3], states), (at_lower, sib_b)])

    ggroup = min(32, heads)
    gwide = ggroup * width
    gtok = pl.BlockSpec((tokens, gwide), lambda i: (0, i))
    gstate = pl.BlockSpec((gwide // LANES, half, LANES), lambda i: (i, 0, 0))
    carried = pl.pallas_call(
        functools.partial(grads_kernel, ggroup, width, masks),
        grid=(heads // ggroup,),
        in_specs=[SMEM, SMEM] + [gstate] * 4 + [gtok, gtok, whole((tokens, 4 * heads))],
        out_specs=whole(part.shape),
        out_shape=part,
        scratch_shapes=[
            pltpu.VMEM((2, 2 * state, gwide), BF16),
            pltpu.VMEM((2, tokens, state), F32),
        ],
        compiler_params=grant(GRADS_VMEM),
        name="grads",
    )(
        flag, spot, enter_f, other_f, enter_b, other_b, inputs, cotangent, edges
    )
    parts = [carried[k] + grads_loc[k] for k in range(len(masks))]

    state_spec = pl.BlockSpec((per, half, LANES), lambda i: (i, 0, 0))

    def finish(kind, first, own, other, base, proj, name):
        return pl.pallas_call(
            functools.partial(output_kernel, group, width, kind),
            grid=(groups,),
            in_specs=[
                SMEM,
                state_spec,
                state_spec,
                tok,
                whole((tokens, 4 * heads)),
                whole((tokens, state)),
            ],
            out_specs=tok,
            out_shape=jax.ShapeDtypeStruct((tokens, channels), BF16),
            scratch_shapes=[pltpu.VMEM((state, wide), BF16)] * 2,
            compiler_params=grant(OUTPUT_VMEM),
            cost_estimate=pl.CostEstimate(
                flops=4 * tokens * state * channels,
                transcendentals=0,
                bytes_accessed=8 * tokens * channels,
            ),
            name=name,
        )(first, own, other, base, edges, proj)

    if tensor == 4:
        (own, *leaving), first = lax.optimization_barrier((parts, flag))
        landed = [swap_with(v, "tensor", k) for k, v in zip(masks[1:], leaving)]
        mixed = finish(1, first, enter_f, other_f, mixed_loc, c_in, "mixed")
        landed, mixed = lax.optimization_barrier((landed, mixed))
        total = (own + landed[0] + landed[1] + landed[2]).astype(BF16)
        total, first = lax.optimization_barrier((total, first))
        landed = [swap_with(total, "tensor", k) for k in masks[1:]]
        grad_inputs = finish(0, first, enter_b, other_b, gx_loc, b_in, "grad_inputs")
        landed, grad_inputs = lax.optimization_barrier((landed, grad_inputs))
        summed = jnp.zeros((4,) + total.shape, BF16)
        for k, v in zip(masks, [total] + landed):
            summed = lax.dynamic_update_index_in_dim(summed, v, place ^ k, 0)
        grad_b, grad_c = summed[:, 0], summed[:, 1]
    else:
        mixed = finish(1, flag, enter_f, other_f, mixed_loc, c_in, "mixed")
        grad_inputs = finish(0, flag, enter_b, other_b, gx_loc, b_in, "grad_inputs")
        grad_b, grad_c = lax.psum(parts[0], "tensor").astype(BF16)
    return (mixed, grad_inputs, grad_b.reshape(tokens, state), grad_c.reshape(tokens, state))


def solution(mesh):
    in_specs = (
        P("context", "tensor"),
        P("tensor", "context"),
        P("tensor"),
        P("tensor"),
        P("context", None),
        P("context", None),
        P("context"),
        P("context", "tensor"),
    )
    out_specs = (
        P("context", "tensor"),
        P("context", "tensor"),
        P("context", None),
        P("context", None),
    )
    return jax.shard_map(shards, mesh=mesh, in_specs=in_specs, out_specs=out_specs, check_vma=False)
```

```python
import functools

import jax
import jax.numpy as jnp
from jax import lax
from jax.experimental import pallas as pl
from jax.experimental.pallas import tpu as pltpu
from jax.sharding import PartitionSpec as P

BLOCK = 128
LANES = 128
F32 = jnp.float32
BF16 = jnp.bfloat16
NEVER = -200.0
MASKED = -1e30
BOUND = 6.0 * 1.796875
STEP = 1024.0
META = 8
STATES_VMEM, LOCAL_VMEM, GRADS_VMEM, OUTPUT_VMEM = 62, 60, 48, 60

NN = (((1,), (0,)), ((), ()))
NT = (((1,), (1,)), ((), ()))
TN = (((0,), (0,)), ((), ()))


def dot(a, b, dims):
    return lax.dot_general(a, b, dims, preferred_element_type=F32)


def split2(x):
    hi = x.astype(BF16)
    lo = (x - hi.astype(F32)).astype(BF16)
    return hi, lo


def split3(x):
    hi = x.astype(BF16)
    rest = x - hi.astype(F32)
    mid = rest.astype(BF16)
    lo = (rest - mid.astype(F32)).astype(BF16)
    return hi, mid, lo


def iota(shape, axis):
    return lax.broadcasted_iota(jnp.int32, shape, axis)


def block_sums(step, decay, doc):
    log_decay = -step * decay
    tri = jnp.where(iota((BLOCK, BLOCK), 0) >= iota((BLOCK, BLOCK), 1), 1.0, 0.0).astype(BF16)
    out = []
    for first in range(0, step.shape[1], BLOCK):
        cols = slice(first, first + BLOCK)
        parts = split3(log_decay[:, cols])
        starts = jnp.broadcast_to(doc[:, cols].astype(F32), (16, BLOCK)).astype(BF16)
        down = functools.reduce(jnp.add, [dot(tri, part, NT) for part in parts])
        across = functools.reduce(jnp.add, [dot(part, tri, NT) for part in parts])
        count_down = dot(tri, starts, NT)[:, :1]
        count_across = dot(starts, tri, NT)[:1]
        out.append((down, across, count_down, count_across))
    return out


def edge_weights(step, sums):
    eye = jnp.where(iota((BLOCK, BLOCK), 0) == iota((BLOCK, BLOCK), 1), 1.0, 0.0).astype(BF16)
    blocks = len(sums)
    ends = [s[0][BLOCK - 1 :] for s in sums]
    counts = [s[2][BLOCK - 1 :] for s in sums]
    keep, last = [], []
    for k in range(blocks):
        down, _, count_down, _ = sums[k]
        sum_before = down
        starts_before = count_down
        sum_after = ends[k] - down
        starts_after = counts[k] - count_down
        for j in range(k):
            sum_before = sum_before + ends[j]
            starts_before = starts_before + counts[j]
        for j in range(k + 1, blocks):
            sum_after = sum_after + ends[j]
            starts_after = starts_after + counts[j]
        parts = split3(step[:, k * BLOCK : (k + 1) * BLOCK])
        step_down = functools.reduce(jnp.add, [dot(eye, part, NT) for part in parts])
        keep.append(jnp.where(starts_before == 0.0, jnp.exp(sum_before), 0.0))
        last.append(jnp.where(starts_after == 0.0, jnp.exp(sum_after) * step_down, 0.0))
    total = functools.reduce(jnp.add, ends)
    starts = functools.reduce(jnp.add, counts)
    total = jnp.where(starts == 0.0, jnp.maximum(total, NEVER), NEVER)
    return jnp.concatenate(keep, 0), jnp.concatenate(last, 0), total


def spread_rows(rows, first, width, columns, skipped):
    heads = rows // 4
    row = iota((rows, 1), 0) - skipped * heads
    head = jnp.where(row >= heads, row - heads, row)
    head = jnp.where((row >= 0) & (row < 2 * heads), head, -rows * rows)
    offset = iota((1, columns), 1) - (head - first) * width
    return jnp.where((offset >= 0) & (offset < width), 1.0, 0.0).astype(BF16)


def last_spread(rows, first, width, columns):
    return spread_rows(rows, first, width, columns, 0)


def keep_spread(rows, first, width, columns):
    return spread_rows(rows, first, width, columns, 2)


SPREADS = (last_spread, keep_spread)


def pieces(total, most=256):
    return [slice(k, min(k + most, total)) for k in range(0, total, most)]


def fetch(pairs, sems):
    copies = [pltpu.make_async_copy(src, dst, sems.at[k]) for k, (src, dst) in enumerate(pairs)]
    for copy in copies:
        copy.start()
    return copies


def column(row):
    shape = (row.shape[1], row.shape[1])
    spot = iota(shape, 0) == iota(shape, 1)
    return jnp.sum(jnp.where(spot, row, 0.0), axis=1, keepdims=True)


def states_kernel(
    group, width, core_ref, x_hbm, g_hbm, step_hbm, decay_hbm, doc_hbm, b_hbm, c_hbm,
    mine_ref, send_ref, meta_ref, edges_ref, x_ref, g_ref, step_ref, decay_ref, doc_ref, b_ref,
    c_ref, b_t, c_t, meta, small_sems, big_sems,
):
    step_id = pl.program_id(0)
    groups = x_ref.shape[0]
    half = b_t.shape[0] // 2
    wide = group * width
    chunks = wide // LANES

    def big(k):
        return [
            pltpu.make_async_copy(
                src.at[:, pl.ds(pl.multiple_of(k * wide, LANES), wide)], dst.at[k], big_sems.at[n, k]
            )
            for n, (src, dst) in enumerate(((x_hbm, x_ref), (g_hbm, g_ref)))
        ]

    @pl.when(step_id == 0)
    def _():
        small = fetch(
            (
                (step_hbm, step_ref),
                (decay_hbm, decay_ref),
                (doc_hbm, doc_ref),
                (b_hbm, b_ref),
                (c_hbm, c_ref),
            ),
            small_sems,
        )
        for k in range(groups):
            for copy in big(k):
                copy.start()
        for copy in small:
            copy.wait()
        swap = core_ref[0] == 1
        step = step_ref[...]
        sums = block_sums(step, column(decay_ref[...]), doc_ref[...])
        keep, last, total = edge_weights(step, sums)
        bound_f = BOUND * jnp.sum(last, axis=0, keepdims=True)
        bound_b = BOUND * jnp.sum(keep, axis=0, keepdims=True)
        rows = [total, jnp.exp(total), bound_f, bound_b]
        rows = jnp.concatenate(rows + [jnp.zeros((META - 4, total.shape[1]), F32)], 0)
        high, mid, low = split3(rows)
        meta[...] = jnp.concatenate([high, mid, low, jnp.zeros_like(high)], 1)
        edges_ref[...] = jnp.concatenate(split2(last) + split2(keep), 1)
        for ref, out in ((b_ref, b_t), (c_ref, c_t)):
            turned = ref[...].astype(F32).T
            swapped = jnp.concatenate([turned[half:], turned[:half]], 0)
            out[...] = jnp.where(swap, swapped, turned).astype(BF16)

    arriving = big(step_id)
    edges = edges_ref[...]
    spreads = [make(edges.shape[1], step_id * group, width, wide) for make in SPREADS]
    rows = dot(meta[...], spreads[0] + spreads[1], NN)
    for k in range(chunks):
        for n in range(META):
            meta_ref[n, pl.ds(step_id * chunks + k, 1)] = rows[n : n + 1, k * LANES : (k + 1) * LANES]
    for kind, (ref, turned) in enumerate(((x_ref, b_t), (g_ref, c_t))):
        arriving[kind].wait()
        turned = turned[...]
        for lanes in pieces(wide):
            scale = dot(edges, spreads[kind][:, lanes], NN)
            scaled = split2(ref[step_id, :, lanes].astype(F32) * scale)
            state = dot(turned, scaled[0], NN) + dot(turned, scaled[1], NN)
            for k in range(state.shape[1] // LANES):
                part = state[:, k * LANES : (k + 1) * LANES]
                at = lanes.start // LANES + k
                mine_ref[at, kind * half : (kind + 1) * half] = part[:half]
                send_ref[at, kind * half : (kind + 1) * half] = part[half:]


def write_rows(masks, place_ref, total, out_ref):
    rows = total.shape[1] // len(masks)
    for k, mask in enumerate(masks):
        at = pl.ds(pl.multiple_of((place_ref[0] ^ mask) * rows, rows), rows)
        for slot in range(2):
            out_ref[k, slot] = total[slot, at]


def local_kernel(
    group, width, masks, skip_ref, place_ref, x_ref, g_ref, step_ref, step_blk, decay_ref, doc_ref, b_ref, c_ref,
    mixed_ref, gx_ref, grads_ref, down_s, across_s, bias, inter, common, sums_s,
):
    step_id = pl.program_id(0)
    groups = down_s.shape[1]
    pairs = ((0, 0), (1, 0), (1, 1))

    @pl.when(step_id == 0)
    def _():
        step = step_ref[...]
        sums = block_sums(step, column(decay_ref[...]), doc_ref[...])
        for k in range(groups):
            heads = slice(k * group, (k + 1) * group)
            for j in range(2):
                down_s[j, k] = sums[j][0][:, heads]
                across_s[j, k] = sums[j][1][heads]
        for n, (t, s) in enumerate(pairs):
            if t == s:
                ok = sums[t][2] == sums[s][3]
                ok = ok & (iota((BLOCK, BLOCK), 0) >= iota((BLOCK, BLOCK), 1))
            else:
                ok = sums[t][2] == sums[s][3] - sums[s][3][:, BLOCK - 1 :]
            bias[n] = jnp.where(ok, 0.0, MASKED)
            inter[n] = dot(
                c_ref[t * BLOCK : (t + 1) * BLOCK], b_ref[s * BLOCK : (s + 1) * BLOCK], NT
            )
        common[...] = jnp.zeros_like(common)

    down = [down_s[j, step_id] for j in range(2)]
    across = [across_s[j, step_id] for j in range(2)]
    left = iota((BLOCK, LANES), 1) < width
    left2 = iota((2 * BLOCK, LANES), 1) < width
    for k in range(group * width // LANES):
        lanes = slice(k * LANES, (k + 1) * LANES)
        xs = [x_ref[j * BLOCK : (j + 1) * BLOCK, lanes] for j in range(2)]
        gs = [g_ref[j * BLOCK : (j + 1) * BLOCK, lanes] for j in range(2)]
        zero = jnp.zeros_like(gs[0])
        halves = [
            jnp.concatenate([jnp.where(left, v, zero), jnp.where(left, zero, v)], 0) for v in gs
        ]
        inner = [dot(halves[t], xs[s], NT) for t, s in pairs]
        twice_x = [jnp.concatenate([v, v], 0) for v in xs]
        twice_g = [jnp.concatenate([v, v], 0) for v in gs]
        both_x = jnp.concatenate(twice_x, 0)
        both_g = jnp.concatenate(twice_g, 0)
        mixed_parts, gx_parts = [], []
        totals = [None] * 3
        for e in range(2):
            h = 2 * k + e
            parts = []
            for n, (t, s) in enumerate(pairs):
                row = across[s][h : h + 1]
                if t != s:
                    row = row - row[:, BLOCK - 1 :]
                weight = jnp.exp(jnp.minimum(down[t][:, h : h + 1] - row, 0.0) + bias[n])
                weight = weight * step_blk[h : h + 1, s * BLOCK : (s + 1) * BLOCK]
                term = weight * inner[n][e * BLOCK : (e + 1) * BLOCK]
                totals[n] = term if e == 0 else totals[n] + term
                parts.append(split2(weight * inter[n]))
            p00, p10, p11 = parts
            mixed_parts.append(
                (
                    dot(jnp.concatenate(p00, 1), twice_x[0], NN),
                    dot(jnp.concatenate(p10 + p11, 1), both_x, NN),
                )
            )
            gx_parts.append(
                (
                    dot(jnp.concatenate(p00 + p10, 0), both_g, TN),
                    dot(jnp.concatenate(p11, 0), twice_g[1], TN),
                )
            )
        for n in range(3):
            common[n] += totals[n]
        first = step_id * group + 2 * k
        skip = jnp.where(left, skip_ref[first], skip_ref[first + 1])
        for j in range(2):
            rows = slice(j * BLOCK, (j + 1) * BLOCK)
            mixed_ref[rows, lanes] = (
                jnp.where(left, mixed_parts[0][j], mixed_parts[1][j]) + skip * xs[j].astype(F32)
            )
            gx_ref[rows, lanes] = (
                jnp.where(left, gx_parts[0][j], gx_parts[1][j]) + skip * gs[j].astype(F32)
            )

    @pl.when(step_id == pl.num_programs(0) - 1)
    def _():
        c00, c10, c11 = [split2(common[n]) for n in range(3)]
        b0, b1 = b_ref[:BLOCK], b_ref[BLOCK:]
        c0, c1 = c_ref[:BLOCK], c_ref[BLOCK:]
        sums_s[0, :BLOCK] = sum(dot(v, c0, TN) for v in c00) + sum(dot(v, c1, TN) for v in c10)
        sums_s[0, BLOCK:] = sum(dot(v, c1, TN) for v in c11)
        sums_s[1, :BLOCK] = sum(dot(v, b0, NN) for v in c00)
        sums_s[1, BLOCK:] = sum(dot(v, b0, NN) for v in c10) + sum(dot(v, b1, NN) for v in c11)
        write_rows(masks, place_ref, sums_s, grads_ref)


def place_state(core, own, other, high, low):
    half = own.shape[1]
    for part, first in ((own, core), (other, 1 - core)):
        rows = pl.ds(pl.multiple_of(first * half, half), half)
        for k in range(own.shape[0]):
            lanes = slice(k * LANES, (k + 1) * LANES)
            hi, lo = split2(part[k])
            high[rows, lanes] = hi
            low[rows, lanes] = lo


def grads_kernel(
    group, width, masks, core_ref, place_ref, own_f, other_f, own_b, other_b, x_ref, g_ref, edges_ref,
    out_ref, both, total,
):
    step_id = pl.program_id(0)
    state = total.shape[2]

    @pl.when(step_id == 0)
    def _():
        total[...] = jnp.zeros_like(total)

    edges = edges_ref[...]
    for slot, own, other, ref in ((0, own_b, other_b, x_ref), (1, own_f, other_f, g_ref)):
        place_state(core_ref[0], own, other, both.at[slot], both.at[slot, state:])
        spread = SPREADS[slot](edges.shape[1], step_id * group, width, group * width)
        high, low = split2(ref[...].astype(F32) * dot(edges, spread, NN))
        product = dot(high, both[slot], NT)
        product = product[:, :state] + product[:, state:]
        total[slot] += product + dot(low, both[slot, :state], NT)

    @pl.when(step_id == pl.num_programs(0) - 1)
    def _():
        write_rows(masks, place_ref, total, out_ref)


def output_kernel(
    group, width, kind, core_ref, own, other, base_ref, edges_ref, proj_ref, out_ref, high, low
):
    place_state(core_ref[0], own, other, high, low)
    edges = edges_ref[...]
    wide = group * width
    spread = SPREADS[kind](edges.shape[1], pl.program_id(0) * group, width, wide)
    proj = proj_ref[...]
    for lanes in pieces(wide):
        scale = dot(edges, spread[:, lanes], NN)
        carried = dot(proj, high[:, lanes], NN) + dot(proj, low[:, lanes], NN)
        out_ref[:, lanes] = (base_ref[:, lanes] + scale * carried).astype(BF16)


def whole(shape):
    return pl.BlockSpec(shape, lambda i: (0,) * len(shape))


SMEM = pl.BlockSpec(memory_space=pltpu.SMEM)
HBM = pl.BlockSpec(memory_space=pltpu.HBM)


def grant(mib):
    return pltpu.CompilerParams(vmem_limit_bytes=mib << 20)


def swap_with(value, axis, mask):
    size = lax.axis_size(axis)
    return lax.ppermute(value, axis, [(i, i ^ mask) for i in range(size)])


def scan_chips(total_f, total_b, total_l, axis):
    size, index = lax.axis_size(axis), lax.axis_index(axis)
    before, after = jnp.zeros_like(total_f), jnp.zeros_like(total_b)
    log_before, log_after = jnp.zeros_like(total_l), jnp.zeros_like(total_l)
    bit = 2
    while bit < size:
        other_f, other_b, other_l = [swap_with(v, axis, bit) for v in (total_f, total_b, total_l)]
        upper = (index & bit) != 0
        before = jnp.where(upper, jnp.exp(log_before) * other_f + before, before)
        after = jnp.where(upper, after, jnp.exp(log_after) * other_b + after)
        log_before = jnp.where(upper, log_before + other_l, log_before)
        log_after = jnp.where(upper, log_after, log_after + other_l)
        scale, other_scale = jnp.exp(total_l), jnp.exp(other_l)
        total_f = jnp.where(upper, scale * other_f + total_f, other_scale * total_f + other_f)
        total_b = jnp.where(upper, other_b + other_scale * total_b, total_b + scale * other_b)
        total_l = jnp.maximum(total_l + other_l, NEVER)
        bit *= 2
    return before, after


def encode(state, bound, log_decay):
    power = jnp.clip(jnp.ceil(jnp.log2(bound)), -100.0, 120.0)
    data = state * jnp.exp2(14.0 - power)[:, None]
    first = lax.reduce_precision(log_decay, 5, 10)
    second = lax.reduce_precision(log_decay - first, 8, 10)
    rows = [data.reshape(-1, LANES), first, second * STEP, power]
    return jnp.concatenate([v.astype(jnp.float16) for v in rows], 0)


def decode(coded, chunks):
    size = coded.shape[0] - 3 * chunks
    rows = [coded[size + k * chunks : size + (k + 1) * chunks].astype(F32) for k in range(3)]
    state = coded[:size].reshape(chunks, -1, LANES)
    return state, jnp.exp2(rows[2] - 14.0), jnp.exp(rows[0] + rows[1] / STEP)


def chip_place(axis):
    index = lax.axis_index(axis)
    return (index >> 1) & 1, (index >> 2) & 1


def pack_chip(total_f, total_b, bound_f, bound_b, log_decay, axis):
    return [
        encode(
            jnp.where(first, total_f, total_b), jnp.where(first, bound_f, bound_b), log_decay
        )
        for first in [bit == 0 for bit in chip_place(axis)]
    ]


def join_chips(arrived, axis, chunks):
    x, y = chip_place(axis)
    states, scales, decays = zip(*[decode(v, chunks) for v in arrived])
    _, two, three = decays
    same, upper = x == y, y == 1
    beyond = jnp.where(same, decays[0], 1.0)
    weights = [
        jnp.ones_like(two),
        beyond * jnp.where(same, 1.0, three),
        beyond * jnp.where(same, two, 1.0),
    ]
    weights = [w * scale for w, scale in zip(weights, scales)]
    main = [jnp.where(same, weights[0], 0.0)] + weights[1:]
    side = [jnp.where(same, 0.0, weights[0]), 0.0, 0.0]
    before = [jnp.where(upper, m, s) for m, s in zip(main, side)]
    after = [jnp.where(upper, s, m) for m, s in zip(main, side)]
    return states, before, after


def weigh(terms):
    return functools.reduce(jnp.add, [w[:, None] * v.astype(F32) for w, v in terms])


def shards(inputs, step_size, decay_rate, skip, b_in, c_in, doc_start, cotangent):
    heads, tokens = step_size.shape
    channels = inputs.shape[1]
    width = channels // heads
    state = b_in.shape[1]
    half = state // 2
    group = min(8, heads)
    groups = heads // group
    wide = group * width
    per = wide // LANES
    chunks = channels // LANES
    context, tensor = lax.axis_size("context"), lax.axis_size("tensor")
    core = lax.axis_index("context") & 1
    flag = core.reshape(1).astype(jnp.int32)
    decay = decay_rate.reshape(1, heads)
    doc = doc_start.reshape(1, tokens)

    tok = pl.BlockSpec((tokens, wide), lambda i: (0, i))
    piece = pl.BlockSpec((per, state, LANES), lambda i: (i, 0, 0))
    sgroup = min(32, heads)
    sgroups = heads // sgroup
    swide = sgroup * width
    piece = pl.BlockSpec((swide // LANES, state, LANES), lambda i: (i, 0, 0))
    mine, send, raw_meta, edges = pl.pallas_call(
        functools.partial(states_kernel, sgroup, width),
        grid=(sgroups,),
        in_specs=[SMEM] + [HBM] * 7,
        out_specs=[piece, piece, whole((META, chunks, LANES)), whole((tokens, 4 * heads))],
        out_shape=[jax.ShapeDtypeStruct((chunks, state, LANES), F32)] * 2
        + [
            jax.ShapeDtypeStruct((META, chunks, LANES), F32),
            jax.ShapeDtypeStruct((tokens, 4 * heads), BF16),
        ],
        scratch_shapes=[
            pltpu.VMEM((sgroups, tokens, swide), BF16),
            pltpu.VMEM((sgroups, tokens, swide), BF16),
            pltpu.VMEM((heads, tokens), F32),
            pltpu.VMEM((1, heads), F32),
            pltpu.VMEM((1, tokens), jnp.int32),
            pltpu.VMEM((tokens, state), BF16),
            pltpu.VMEM((tokens, state), BF16),
            pltpu.VMEM((state, tokens), BF16),
            pltpu.VMEM((state, tokens), BF16),
            pltpu.VMEM((META, 4 * heads), BF16),
            pltpu.SemaphoreType.DMA((5,)),
            pltpu.SemaphoreType.DMA((2, sgroups)),
        ],
        compiler_params=grant(STATES_VMEM),
        name="states",
    )(flag, inputs, cotangent, step_size, decay, doc, b_in, c_in)

    least = float(jnp.finfo(F32).min)
    meta, mine = lax.optimization_barrier((jnp.maximum(raw_meta, NEVER), jnp.maximum(mine, least)))
    theirs = swap_with(send, "context", 1)
    sib_meta = swap_with(raw_meta, "context", 1)
    lower = core == 0
    own_f, own_b = mine[:, :half], mine[:, half:]
    sib_f, sib_b = theirs[:, :half], theirs[:, half:]
    own_l, own_e, own_mf, own_mb = [meta[k] for k in range(4)]
    sib_l, sib_e, sib_mf, sib_mb = [sib_meta[k] for k in range(4)]
    f_own, f_sib = jnp.where(lower, sib_e, 1.0), jnp.where(lower, 1.0, own_e)
    b_own, b_sib = jnp.where(lower, 1.0, sib_e), jnp.where(lower, own_e, 1.0)
    chip_f = f_own[:, None] * own_f + f_sib[:, None] * sib_f
    chip_b = b_own[:, None] * own_b + b_sib[:, None] * sib_b
    chip_l = jnp.maximum(own_l + sib_l, NEVER)
    if context == 8:
        near, far = pack_chip(
            chip_f,
            chip_b,
            f_own * own_mf + f_sib * sib_mf,
            b_own * own_mb + b_sib * sib_mb,
            chip_l,
            "context",
        )
        near, far, skip = lax.optimization_barrier((near, far, skip))
        arrived = [
            swap_with(near, "context", 2),
            swap_with(far, "context", 4),
            swap_with(far, "context", 6),
        ]

    full = jax.ShapeDtypeStruct((tokens, channels), F32)
    masks = (0, 2, 3, 1) if tensor == 4 else (0,)
    rows = tokens // len(masks)
    place = lax.axis_index("tensor")
    part = jax.ShapeDtypeStruct((len(masks), 2, rows, state), F32)
    spot = place.reshape(1) if tensor == 4 else jnp.zeros((1,), jnp.int32)
    mixed_loc, gx_loc, grads_loc = pl.pallas_call(
        functools.partial(local_kernel, group, width, masks),
        grid=(groups,),
        in_specs=[
            SMEM,
            SMEM,
            tok,
            tok,
            whole((heads, tokens)),
            pl.BlockSpec((group, tokens), lambda i: (i, 0)),
            whole((1, heads)),
            whole((1, tokens)),
            whole((tokens, state)),
            whole((tokens, state)),
        ],
        out_specs=[tok, tok, whole(part.shape)],
        out_shape=[full, full, part],
        scratch_shapes=[
            pltpu.VMEM((2, groups, BLOCK, group), F32),
            pltpu.VMEM((2, groups, group, BLOCK), F32),
            pltpu.VMEM((3, BLOCK, BLOCK), F32),
            pltpu.VMEM((3, BLOCK, BLOCK), F32),
            pltpu.VMEM((3, BLOCK, BLOCK), F32),
            pltpu.VMEM((2, tokens, state), F32),
        ],
        compiler_params=grant(LOCAL_VMEM),
        cost_estimate=pl.CostEstimate(
            flops=20 * tokens * tokens * channels,
            transcendentals=heads * tokens * tokens,
            bytes_accessed=12 * tokens * channels,
        ),
        name="local",
    )(skip, spot, inputs, cotangent, step_size, step_size, decay, doc, b_in, c_in)

    one, zero = jnp.ones_like(own_e), jnp.zeros_like(own_e)
    if context == 8:
        arrived, grads_loc = lax.optimization_barrier((arrived, grads_loc))
        states, before, after = join_chips(arrived, "context", chunks)
    else:
        states = scan_chips(chip_f, chip_b, chip_l[:, None], "context")
        before, after = [one, zero], [zero, one]
    pass_f = jnp.where(lower, own_e, 1.0)
    pass_b = jnp.where(lower, 1.0, own_e)
    keep_f = jnp.where(lower, 1.0, sib_e)
    keep_b = jnp.where(lower, sib_e, 1.0)
    at_lower = jnp.where(lower, one, zero)
    at_upper = jnp.where(lower, zero, one)
    weights = (
        [pass_f * w for w in before],
        [pass_b * w for w in after],
        [keep_f * w for w in before],
        [keep_b * w for w in after],
    )
    passed_f = weigh([*zip(weights[0], states), (at_lower, own_f)])
    passed_b = weigh([*zip(weights[1], states), (at_upper, own_b)])
    passed_f, passed_b, weights, states = lax.optimization_barrier(
        (passed_f, passed_b, weights, states)
    )
    other_f = swap_with(passed_f, "context", 1)
    other_b = swap_with(passed_b, "context", 1)
    enter_f = weigh([*zip(weights[2], states), (at_upper, sib_f)])
    enter_b = weigh([*zip(weights[3], states), (at_lower, sib_b)])

    ggroup = min(32, heads)
    gwide = ggroup * width
    gtok = pl.BlockSpec((tokens, gwide), lambda i: (0, i))
    gstate = pl.BlockSpec((gwide // LANES, half, LANES), lambda i: (i, 0, 0))
    carried = pl.pallas_call(
        functools.partial(grads_kernel, ggroup, width, masks),
        grid=(heads // ggroup,),
        in_specs=[SMEM, SMEM] + [gstate] * 4 + [gtok, gtok, whole((tokens, 4 * heads))],
        out_specs=whole(part.shape),
        out_shape=part,
        scratch_shapes=[
            pltpu.VMEM((2, 2 * state, gwide), BF16),
            pltpu.VMEM((2, tokens, state), F32),
        ],
        compiler_params=grant(GRADS_VMEM),
        name="grads",
    )(
        flag, spot, enter_f, other_f, enter_b, other_b, inputs, cotangent, edges
    )
    parts = [carried[k] + grads_loc[k] for k in range(len(masks))]

    state_spec = pl.BlockSpec((per, half, LANES), lambda i: (i, 0, 0))

    def finish(kind, first, own, other, base, proj, name):
        return pl.pallas_call(
            functools.partial(output_kernel, group, width, kind),
            grid=(groups,),
            in_specs=[
                SMEM,
                state_spec,
                state_spec,
                tok,
                whole((tokens, 4 * heads)),
                whole((tokens, state)),
            ],
            out_specs=tok,
            out_shape=jax.ShapeDtypeStruct((tokens, channels), BF16),
            scratch_shapes=[pltpu.VMEM((state, wide), BF16)] * 2,
            compiler_params=grant(OUTPUT_VMEM),
            cost_estimate=pl.CostEstimate(
                flops=4 * tokens * state * channels,
                transcendentals=0,
                bytes_accessed=8 * tokens * channels,
            ),
            name=name,
        )(first, own, other, base, edges, proj)

    if tensor == 4:
        (own, *leaving), first = lax.optimization_barrier((parts, flag))
        landed = [swap_with(v, "tensor", k) for k, v in zip(masks[1:], leaving)]
        mixed = finish(1, first, enter_f, other_f, mixed_loc, c_in, "mixed")
        landed, mixed = lax.optimization_barrier((landed, mixed))
        total = (own + landed[0] + landed[1] + landed[2]).astype(BF16)
        total, first = lax.optimization_barrier((total, first))
        landed = [swap_with(total, "tensor", k) for k in masks[1:]]
        grad_inputs = finish(0, first, enter_b, other_b, gx_loc, b_in, "grad_inputs")
        landed, grad_inputs = lax.optimization_barrier((landed, grad_inputs))
        summed = jnp.zeros((4,) + total.shape, BF16)
        for k, v in zip(masks, [total] + landed):
            summed = lax.dynamic_update_index_in_dim(summed, v, place ^ k, 0)
        grad_b, grad_c = summed[:, 0], summed[:, 1]
    else:
        mixed = finish(1, flag, enter_f, other_f, mixed_loc, c_in, "mixed")
        grad_inputs = finish(0, flag, enter_b, other_b, gx_loc, b_in, "grad_inputs")
        grad_b, grad_c = lax.psum(parts[0], "tensor").astype(BF16)
    return (mixed, grad_inputs, grad_b.reshape(tokens, state), grad_c.reshape(tokens, state))


def solution(mesh):
    in_specs = (
        P("context", "tensor"),
        P("tensor", "context"),
        P("tensor"),
        P("tensor"),
        P("context", None),
        P("context", None),
        P("context"),
        P("context", "tensor"),
    )
    out_specs = (
        P("context", "tensor"),
        P("context", "tensor"),
        P("context", None),
        P("context", None),
    )
    return jax.shard_map(shards, mesh=mesh, in_specs=in_specs, out_specs=out_specs, check_vma=False)
```

```python
import functools

import jax
import jax.numpy as jnp
from jax import lax
from jax.experimental import pallas as pl
from jax.experimental.pallas import tpu as pltpu
from jax.sharding import PartitionSpec as P

BLOCK = 128
LANES = 128
F32 = jnp.float32
BF16 = jnp.bfloat16
NEVER = -200.0
MASKED = -1e30
BOUND = 6.0 * 1.796875
STEP = 1024.0
META = 8
STATES_VMEM, LOCAL_VMEM, GRADS_VMEM, OUTPUT_VMEM = 62, 60, 48, 40

NN = (((1,), (0,)), ((), ()))
NT = (((1,), (1,)), ((), ()))
TN = (((0,), (0,)), ((), ()))


def dot(a, b, dims):
    return lax.dot_general(a, b, dims, preferred_element_type=F32)


def split2(x):
    hi = x.astype(BF16)
    lo = (x - hi.astype(F32)).astype(BF16)
    return hi, lo


def split3(x):
    hi = x.astype(BF16)
    rest = x - hi.astype(F32)
    mid = rest.astype(BF16)
    lo = (rest - mid.astype(F32)).astype(BF16)
    return hi, mid, lo


def iota(shape, axis):
    return lax.broadcasted_iota(jnp.int32, shape, axis)


def block_sums(step, decay, doc):
    log_decay = -step * decay
    tri = jnp.where(iota((BLOCK, BLOCK), 0) >= iota((BLOCK, BLOCK), 1), 1.0, 0.0).astype(BF16)
    out = []
    for first in range(0, step.shape[1], BLOCK):
        cols = slice(first, first + BLOCK)
        parts = split3(log_decay[:, cols])
        starts = jnp.broadcast_to(doc[:, cols].astype(F32), (16, BLOCK)).astype(BF16)
        down = functools.reduce(jnp.add, [dot(tri, part, NT) for part in parts])
        across = functools.reduce(jnp.add, [dot(part, tri, NT) for part in parts])
        count_down = dot(tri, starts, NT)[:, :1]
        count_across = dot(starts, tri, NT)[:1]
        out.append((down, across, count_down, count_across))
    return out


def edge_weights(step, sums):
    eye = jnp.where(iota((BLOCK, BLOCK), 0) == iota((BLOCK, BLOCK), 1), 1.0, 0.0).astype(BF16)
    blocks = len(sums)
    ends = [s[0][BLOCK - 1 :] for s in sums]
    counts = [s[2][BLOCK - 1 :] for s in sums]
    keep, last = [], []
    for k in range(blocks):
        down, _, count_down, _ = sums[k]
        sum_before = down
        starts_before = count_down
        sum_after = ends[k] - down
        starts_after = counts[k] - count_down
        for j in range(k):
            sum_before = sum_before + ends[j]
            starts_before = starts_before + counts[j]
        for j in range(k + 1, blocks):
            sum_after = sum_after + ends[j]
            starts_after = starts_after + counts[j]
        parts = split3(step[:, k * BLOCK : (k + 1) * BLOCK])
        step_down = functools.reduce(jnp.add, [dot(eye, part, NT) for part in parts])
        keep.append(jnp.where(starts_before == 0.0, jnp.exp(sum_before), 0.0))
        last.append(jnp.where(starts_after == 0.0, jnp.exp(sum_after) * step_down, 0.0))
    total = functools.reduce(jnp.add, ends)
    starts = functools.reduce(jnp.add, counts)
    total = jnp.where(starts == 0.0, jnp.maximum(total, NEVER), NEVER)
    return jnp.concatenate(keep, 0), jnp.concatenate(last, 0), total


def spread_rows(rows, first, width, columns, skipped):
    heads = rows // 4
    row = iota((rows, 1), 0) - skipped * heads
    head = jnp.where(row >= heads, row - heads, row)
    head = jnp.where((row >= 0) & (row < 2 * heads), head, -rows * rows)
    offset = iota((1, columns), 1) - (head - first) * width
    return jnp.where((offset >= 0) & (offset < width), 1.0, 0.0).astype(BF16)


def last_spread(rows, first, width, columns):
    return spread_rows(rows, first, width, columns, 0)


def keep_spread(rows, first, width, columns):
    return spread_rows(rows, first, width, columns, 2)


SPREADS = (last_spread, keep_spread)


def pieces(total, most=256):
    return [slice(k, min(k + most, total)) for k in range(0, total, most)]


def fetch(pairs, sems):
    copies = [pltpu.make_async_copy(src, dst, sems.at[k]) for k, (src, dst) in enumerate(pairs)]
    for copy in copies:
        copy.start()
    return copies


def column(row):
    shape = (row.shape[1], row.shape[1])
    spot = iota(shape, 0) == iota(shape, 1)
    return jnp.sum(jnp.where(spot, row, 0.0), axis=1, keepdims=True)


def states_kernel(
    group, width, core_ref, x_hbm, g_hbm, step_hbm, decay_hbm, doc_hbm, b_hbm, c_hbm,
    mine_ref, send_ref, meta_ref, edges_ref, x_ref, g_ref, step_ref, decay_ref, doc_ref, b_ref,
    c_ref, b_t, c_t, meta, small_sems, big_sems,
):
    step_id = pl.program_id(0)
    groups = x_ref.shape[0]
    half = b_t.shape[0] // 2
    wide = group * width
    chunks = wide // LANES

    def big(k):
        return [
            pltpu.make_async_copy(
                src.at[:, pl.ds(pl.multiple_of(k * wide, LANES), wide)], dst.at[k], big_sems.at[n, k]
            )
            for n, (src, dst) in enumerate(((x_hbm, x_ref), (g_hbm, g_ref)))
        ]

    @pl.when(step_id == 0)
    def _():
        small = fetch(
            (
                (step_hbm, step_ref),
                (decay_hbm, decay_ref),
                (doc_hbm, doc_ref),
                (b_hbm, b_ref),
                (c_hbm, c_ref),
            ),
            small_sems,
        )
        for k in range(groups):
            for copy in big(k):
                copy.start()
        for copy in small:
            copy.wait()
        swap = core_ref[0] == 1
        step = step_ref[...]
        sums = block_sums(step, column(decay_ref[...]), doc_ref[...])
        keep, last, total = edge_weights(step, sums)
        bound_f = BOUND * jnp.sum(last, axis=0, keepdims=True)
        bound_b = BOUND * jnp.sum(keep, axis=0, keepdims=True)
        rows = [total, jnp.exp(total), bound_f, bound_b]
        rows = jnp.concatenate(rows + [jnp.zeros((META - 4, total.shape[1]), F32)], 0)
        high, mid, low = split3(rows)
        meta[...] = jnp.concatenate([high, mid, low, jnp.zeros_like(high)], 1)
        edges_ref[...] = jnp.concatenate(split2(last) + split2(keep), 1)
        for ref, out in ((b_ref, b_t), (c_ref, c_t)):
            turned = ref[...].astype(F32).T
            swapped = jnp.concatenate([turned[half:], turned[:half]], 0)
            out[...] = jnp.where(swap, swapped, turned).astype(BF16)

    for copy in big(step_id):
        copy.wait()
    edges = edges_ref[...]
    spreads = [make(edges.shape[1], step_id * group, width, wide) for make in SPREADS]
    rows = dot(meta[...], spreads[0] + spreads[1], NN)
    for k in range(chunks):
        for n in range(META):
            meta_ref[n, pl.ds(step_id * chunks + k, 1)] = rows[n : n + 1, k * LANES : (k + 1) * LANES]
    for kind, (ref, turned) in enumerate(((x_ref, b_t), (g_ref, c_t))):
        turned = turned[...]
        for lanes in pieces(wide):
            scale = dot(edges, spreads[kind][:, lanes], NN)
            scaled = split2(ref[step_id, :, lanes].astype(F32) * scale)
            state = dot(turned, scaled[0], NN) + dot(turned, scaled[1], NN)
            for k in range(state.shape[1] // LANES):
                part = state[:, k * LANES : (k + 1) * LANES]
                at = lanes.start // LANES + k
                mine_ref[at, kind * half : (kind + 1) * half] = part[:half]
                send_ref[at, kind * half : (kind + 1) * half] = part[half:]


def write_rows(masks, place_ref, total, out_ref):
    rows = total.shape[1] // len(masks)
    for k, mask in enumerate(masks):
        at = pl.ds(pl.multiple_of((place_ref[0] ^ mask) * rows, rows), rows)
        for slot in range(2):
            out_ref[k, slot] = total[slot, at]


def local_kernel(
    group, width, masks, skip_ref, place_ref, x_ref, g_ref, step_ref, step_blk, decay_ref, doc_ref, b_ref, c_ref,
    mixed_ref, gx_ref, grads_ref, down_s, across_s, bias, inter, common, sums_s,
):
    step_id = pl.program_id(0)
    groups = down_s.shape[1]
    pairs = ((0, 0), (1, 0), (1, 1))

    @pl.when(step_id == 0)
    def _():
        step = step_ref[...]
        sums = block_sums(step, column(decay_ref[...]), doc_ref[...])
        for k in range(groups):
            heads = slice(k * group, (k + 1) * group)
            for j in range(2):
                down_s[j, k] = sums[j][0][:, heads]
                across_s[j, k] = sums[j][1][heads]
        for n, (t, s) in enumerate(pairs):
            if t == s:
                ok = sums[t][2] == sums[s][3]
                ok = ok & (iota((BLOCK, BLOCK), 0) >= iota((BLOCK, BLOCK), 1))
            else:
                ok = sums[t][2] == sums[s][3] - sums[s][3][:, BLOCK - 1 :]
            bias[n] = jnp.where(ok, 0.0, MASKED)
            inter[n] = dot(
                c_ref[t * BLOCK : (t + 1) * BLOCK], b_ref[s * BLOCK : (s + 1) * BLOCK], NT
            )
        common[...] = jnp.zeros_like(common)

    down = [down_s[j, step_id] for j in range(2)]
    across = [across_s[j, step_id] for j in range(2)]
    left = iota((BLOCK, LANES), 1) < width
    left2 = iota((2 * BLOCK, LANES), 1) < width
    for k in range(group * width // LANES):
        lanes = slice(k * LANES, (k + 1) * LANES)
        xs = [x_ref[j * BLOCK : (j + 1) * BLOCK, lanes] for j in range(2)]
        gs = [g_ref[j * BLOCK : (j + 1) * BLOCK, lanes] for j in range(2)]
        zero = jnp.zeros_like(gs[0])
        halves = [
            jnp.concatenate([jnp.where(left, v, zero), jnp.where(left, zero, v)], 0) for v in gs
        ]
        inner = [dot(halves[t], xs[s], NT) for t, s in pairs]
        twice_x = [jnp.concatenate([v, v], 0) for v in xs]
        twice_g = [jnp.concatenate([v, v], 0) for v in gs]
        both_x = jnp.concatenate(twice_x, 0)
        both_g = jnp.concatenate(twice_g, 0)
        mixed_parts, gx_parts = [], []
        totals = [None] * 3
        for e in range(2):
            h = 2 * k + e
            parts = []
            for n, (t, s) in enumerate(pairs):
                row = across[s][h : h + 1]
                if t != s:
                    row = row - row[:, BLOCK - 1 :]
                weight = jnp.exp(jnp.minimum(down[t][:, h : h + 1] - row, 0.0) + bias[n])
                weight = weight * step_blk[h : h + 1, s * BLOCK : (s + 1) * BLOCK]
                term = weight * inner[n][e * BLOCK : (e + 1) * BLOCK]
                totals[n] = term if e == 0 else totals[n] + term
                parts.append(split2(weight * inter[n]))
            p00, p10, p11 = parts
            mixed_parts.append(
                (
                    dot(jnp.concatenate(p00, 1), twice_x[0], NN),
                    dot(jnp.concatenate(p10 + p11, 1), both_x, NN),
                )
            )
            gx_parts.append(
                (
                    dot(jnp.concatenate(p00 + p10, 0), both_g, TN),
                    dot(jnp.concatenate(p11, 0), twice_g[1], TN),
                )
            )
        for n in range(3):
            common[n] += totals[n]
        first = step_id * group + 2 * k
        skip = jnp.where(left, skip_ref[first], skip_ref[first + 1])
        for j in range(2):
            rows = slice(j * BLOCK, (j + 1) * BLOCK)
            mixed_ref[rows, lanes] = (
                jnp.where(left, mixed_parts[0][j], mixed_parts[1][j]) + skip * xs[j].astype(F32)
            )
            gx_ref[rows, lanes] = (
                jnp.where(left, gx_parts[0][j], gx_parts[1][j]) + skip * gs[j].astype(F32)
            )

    @pl.when(step_id == pl.num_programs(0) - 1)
    def _():
        c00, c10, c11 = [split2(common[n]) for n in range(3)]
        b0, b1 = b_ref[:BLOCK], b_ref[BLOCK:]
        c0, c1 = c_ref[:BLOCK], c_ref[BLOCK:]
        sums_s[0, :BLOCK] = sum(dot(v, c0, TN) for v in c00) + sum(dot(v, c1, TN) for v in c10)
        sums_s[0, BLOCK:] = sum(dot(v, c1, TN) for v in c11)
        sums_s[1, :BLOCK] = sum(dot(v, b0, NN) for v in c00)
        sums_s[1, BLOCK:] = sum(dot(v, b0, NN) for v in c10) + sum(dot(v, b1, NN) for v in c11)
        write_rows(masks, place_ref, sums_s, grads_ref)


def place_state(core, own, other, high, low):
    half = own.shape[1]
    for part, first in ((own, core), (other, 1 - core)):
        rows = pl.ds(pl.multiple_of(first * half, half), half)
        for k in range(own.shape[0]):
            lanes = slice(k * LANES, (k + 1) * LANES)
            hi, lo = split2(part[k])
            high[rows, lanes] = hi
            low[rows, lanes] = lo


def grads_kernel(
    group, width, masks, core_ref, place_ref, own_f, other_f, own_b, other_b, x_ref, g_ref, edges_ref,
    out_ref, both, total,
):
    step_id = pl.program_id(0)
    state = total.shape[2]

    @pl.when(step_id == 0)
    def _():
        total[...] = jnp.zeros_like(total)

    edges = edges_ref[...]
    for slot, own, other, ref in ((0, own_b, other_b, x_ref), (1, own_f, other_f, g_ref)):
        place_state(core_ref[0], own, other, both.at[slot], both.at[slot, state:])
        spread = SPREADS[slot](edges.shape[1], step_id * group, width, group * width)
        high, low = split2(ref[...].astype(F32) * dot(edges, spread, NN))
        product = dot(high, both[slot], NT)
        product = product[:, :state] + product[:, state:]
        total[slot] += product + dot(low, both[slot, :state], NT)

    @pl.when(step_id == pl.num_programs(0) - 1)
    def _():
        write_rows(masks, place_ref, total, out_ref)


def output_kernel(
    group, width, kind, core_ref, own, other, base_ref, edges_ref, proj_ref, out_ref, high, low
):
    place_state(core_ref[0], own, other, high, low)
    edges = edges_ref[...]
    wide = group * width
    spread = SPREADS[kind](edges.shape[1], pl.program_id(0) * group, width, wide)
    proj = proj_ref[...]
    for lanes in pieces(wide):
        scale = dot(edges, spread[:, lanes], NN)
        carried = dot(proj, high[:, lanes], NN) + dot(proj, low[:, lanes], NN)
        out_ref[:, lanes] = (base_ref[:, lanes] + scale * carried).astype(BF16)


def whole(shape):
    return pl.BlockSpec(shape, lambda i: (0,) * len(shape))


SMEM = pl.BlockSpec(memory_space=pltpu.SMEM)
HBM = pl.BlockSpec(memory_space=pltpu.HBM)


def grant(mib):
    return pltpu.CompilerParams(vmem_limit_bytes=mib << 20)


def swap_with(value, axis, mask):
    size = lax.axis_size(axis)
    return lax.ppermute(value, axis, [(i, i ^ mask) for i in range(size)])


def scan_chips(total_f, total_b, total_l, axis):
    size, index = lax.axis_size(axis), lax.axis_index(axis)
    before, after = jnp.zeros_like(total_f), jnp.zeros_like(total_b)
    log_before, log_after = jnp.zeros_like(total_l), jnp.zeros_like(total_l)
    bit = 2
    while bit < size:
        other_f, other_b, other_l = [swap_with(v, axis, bit) for v in (total_f, total_b, total_l)]
        upper = (index & bit) != 0
        before = jnp.where(upper, jnp.exp(log_before) * other_f + before, before)
        after = jnp.where(upper, after, jnp.exp(log_after) * other_b + after)
        log_before = jnp.where(upper, log_before + other_l, log_before)
        log_after = jnp.where(upper, log_after, log_after + other_l)
        scale, other_scale = jnp.exp(total_l), jnp.exp(other_l)
        total_f = jnp.where(upper, scale * other_f + total_f, other_scale * total_f + other_f)
        total_b = jnp.where(upper, other_b + other_scale * total_b, total_b + scale * other_b)
        total_l = jnp.maximum(total_l + other_l, NEVER)
        bit *= 2
    return before, after


def encode(state, bound, log_decay):
    power = jnp.clip(jnp.ceil(jnp.log2(bound)), -100.0, 120.0)
    data = state * jnp.exp2(14.0 - power)[:, None]
    first = lax.reduce_precision(log_decay, 5, 10)
    second = lax.reduce_precision(log_decay - first, 8, 10)
    rows = [data.reshape(-1, LANES), first, second * STEP, power]
    return jnp.concatenate([v.astype(jnp.float16) for v in rows], 0)


def decode(coded, chunks):
    size = coded.shape[0] - 3 * chunks
    rows = [coded[size + k * chunks : size + (k + 1) * chunks].astype(F32) for k in range(3)]
    state = coded[:size].reshape(chunks, -1, LANES)
    return state, jnp.exp2(rows[2] - 14.0), jnp.exp(rows[0] + rows[1] / STEP)


def chip_place(axis):
    index = lax.axis_index(axis)
    return (index >> 1) & 1, (index >> 2) & 1


def pack_chip(total_f, total_b, bound_f, bound_b, log_decay, axis):
    return [
        encode(
            jnp.where(first, total_f, total_b), jnp.where(first, bound_f, bound_b), log_decay
        )
        for first in [bit == 0 for bit in chip_place(axis)]
    ]


def join_chips(arrived, axis, chunks):
    x, y = chip_place(axis)
    states, scales, decays = zip(*[decode(v, chunks) for v in arrived])
    _, two, three = decays
    same, upper = x == y, y == 1
    beyond = jnp.where(same, decays[0], 1.0)
    weights = [
        jnp.ones_like(two),
        beyond * jnp.where(same, 1.0, three),
        beyond * jnp.where(same, two, 1.0),
    ]
    weights = [w * scale for w, scale in zip(weights, scales)]
    main = [jnp.where(same, weights[0], 0.0)] + weights[1:]
    side = [jnp.where(same, 0.0, weights[0]), 0.0, 0.0]
    before = [jnp.where(upper, m, s) for m, s in zip(main, side)]
    after = [jnp.where(upper, s, m) for m, s in zip(main, side)]
    return states, before, after


def weigh(terms):
    return functools.reduce(jnp.add, [w[:, None] * v.astype(F32) for w, v in terms])


def shards(inputs, step_size, decay_rate, skip, b_in, c_in, doc_start, cotangent):
    heads, tokens = step_size.shape
    channels = inputs.shape[1]
    width = channels // heads
    state = b_in.shape[1]
    half = state // 2
    group = min(8, heads)
    groups = heads // group
    wide = group * width
    per = wide // LANES
    chunks = channels // LANES
    context, tensor = lax.axis_size("context"), lax.axis_size("tensor")
    core = lax.axis_index("context") & 1
    flag = core.reshape(1).astype(jnp.int32)
    decay = decay_rate.reshape(1, heads)
    doc = doc_start.reshape(1, tokens)

    tok = pl.BlockSpec((tokens, wide), lambda i: (0, i))
    piece = pl.BlockSpec((per, state, LANES), lambda i: (i, 0, 0))
    sgroup = min(32, heads)
    sgroups = heads // sgroup
    swide = sgroup * width
    piece = pl.BlockSpec((swide // LANES, state, LANES), lambda i: (i, 0, 0))
    mine, send, raw_meta, edges = pl.pallas_call(
        functools.partial(states_kernel, sgroup, width),
        grid=(sgroups,),
        in_specs=[SMEM] + [HBM] * 7,
        out_specs=[piece, piece, whole((META, chunks, LANES)), whole((tokens, 4 * heads))],
        out_shape=[jax.ShapeDtypeStruct((chunks, state, LANES), F32)] * 2
        + [
            jax.ShapeDtypeStruct((META, chunks, LANES), F32),
            jax.ShapeDtypeStruct((tokens, 4 * heads), BF16),
        ],
        scratch_shapes=[
            pltpu.VMEM((sgroups, tokens, swide), BF16),
            pltpu.VMEM((sgroups, tokens, swide), BF16),
            pltpu.VMEM((heads, tokens), F32),
            pltpu.VMEM((1, heads), F32),
            pltpu.VMEM((1, tokens), jnp.int32),
            pltpu.VMEM((tokens, state), BF16),
            pltpu.VMEM((tokens, state), BF16),
            pltpu.VMEM((state, tokens), BF16),
            pltpu.VMEM((state, tokens), BF16),
            pltpu.VMEM((META, 4 * heads), BF16),
            pltpu.SemaphoreType.DMA((5,)),
            pltpu.SemaphoreType.DMA((2, sgroups)),
        ],
        compiler_params=grant(STATES_VMEM),
        name="states",
    )(flag, inputs, cotangent, step_size, decay, doc, b_in, c_in)

    least = float(jnp.finfo(F32).min)
    meta, mine = lax.optimization_barrier((jnp.maximum(raw_meta, NEVER), jnp.maximum(mine, least)))
    theirs = swap_with(send, "context", 1)
    sib_meta = swap_with(raw_meta, "context", 1)
    lower = core == 0
    own_f, own_b = mine[:, :half], mine[:, half:]
    sib_f, sib_b = theirs[:, :half], theirs[:, half:]
    own_l, own_e, own_mf, own_mb = [meta[k] for k in range(4)]
    sib_l, sib_e, sib_mf, sib_mb = [sib_meta[k] for k in range(4)]
    f_own, f_sib = jnp.where(lower, sib_e, 1.0), jnp.where(lower, 1.0, own_e)
    b_own, b_sib = jnp.where(lower, 1.0, sib_e), jnp.where(lower, own_e, 1.0)
    chip_f = f_own[:, None] * own_f + f_sib[:, None] * sib_f
    chip_b = b_own[:, None] * own_b + b_sib[:, None] * sib_b
    chip_l = jnp.maximum(own_l + sib_l, NEVER)
    if context == 8:
        near, far = pack_chip(
            chip_f,
            chip_b,
            f_own * own_mf + f_sib * sib_mf,
            b_own * own_mb + b_sib * sib_mb,
            chip_l,
            "context",
        )
        near, far, skip = lax.optimization_barrier((near, far, skip))
        arrived = [
            swap_with(near, "context", 2),
            swap_with(far, "context", 4),
            swap_with(far, "context", 6),
        ]

    full = jax.ShapeDtypeStruct((tokens, channels), F32)
    masks = (0, 2, 3, 1) if tensor == 4 else (0,)
    rows = tokens // len(masks)
    place = lax.axis_index("tensor")
    part = jax.ShapeDtypeStruct((len(masks), 2, rows, state), F32)
    spot = place.reshape(1) if tensor == 4 else jnp.zeros((1,), jnp.int32)
    mixed_loc, gx_loc, grads_loc = pl.pallas_call(
        functools.partial(local_kernel, group, width, masks),
        grid=(groups,),
        in_specs=[
            SMEM,
            SMEM,
            tok,
            tok,
            whole((heads, tokens)),
            pl.BlockSpec((group, tokens), lambda i: (i, 0)),
            whole((1, heads)),
            whole((1, tokens)),
            whole((tokens, state)),
            whole((tokens, state)),
        ],
        out_specs=[tok, tok, whole(part.shape)],
        out_shape=[full, full, part],
        scratch_shapes=[
            pltpu.VMEM((2, groups, BLOCK, group), F32),
            pltpu.VMEM((2, groups, group, BLOCK), F32),
            pltpu.VMEM((3, BLOCK, BLOCK), F32),
            pltpu.VMEM((3, BLOCK, BLOCK), F32),
            pltpu.VMEM((3, BLOCK, BLOCK), F32),
            pltpu.VMEM((2, tokens, state), F32),
        ],
        compiler_params=grant(LOCAL_VMEM),
        cost_estimate=pl.CostEstimate(
            flops=20 * tokens * tokens * channels,
            transcendentals=heads * tokens * tokens,
            bytes_accessed=12 * tokens * channels,
        ),
        name="local",
    )(skip, spot, inputs, cotangent, step_size, step_size, decay, doc, b_in, c_in)

    one, zero = jnp.ones_like(own_e), jnp.zeros_like(own_e)
    if context == 8:
        arrived, grads_loc = lax.optimization_barrier((arrived, grads_loc))
        states, before, after = join_chips(arrived, "context", chunks)
    else:
        states = scan_chips(chip_f, chip_b, chip_l[:, None], "context")
        before, after = [one, zero], [zero, one]
    pass_f = jnp.where(lower, own_e, 1.0)
    pass_b = jnp.where(lower, 1.0, own_e)
    keep_f = jnp.where(lower, 1.0, sib_e)
    keep_b = jnp.where(lower, sib_e, 1.0)
    at_lower = jnp.where(lower, one, zero)
    at_upper = jnp.where(lower, zero, one)
    weights = (
        [pass_f * w for w in before],
        [pass_b * w for w in after],
        [keep_f * w for w in before],
        [keep_b * w for w in after],
    )
    passed_f = weigh([*zip(weights[0], states), (at_lower, own_f)])
    passed_b = weigh([*zip(weights[1], states), (at_upper, own_b)])
    passed_f, passed_b, weights, states = lax.optimization_barrier(
        (passed_f, passed_b, weights, states)
    )
    other_f = swap_with(passed_f, "context", 1)
    other_b = swap_with(passed_b, "context", 1)
    enter_f = weigh([*zip(weights[2], states), (at_upper, sib_f)])
    enter_b = weigh([*zip(weights[3], states), (at_lower, sib_b)])

    ggroup = min(32, heads)
    gwide = ggroup * width
    gtok = pl.BlockSpec((tokens, gwide), lambda i: (0, i))
    gstate = pl.BlockSpec((gwide // LANES, half, LANES), lambda i: (i, 0, 0))
    carried = pl.pallas_call(
        functools.partial(grads_kernel, ggroup, width, masks),
        grid=(heads // ggroup,),
        in_specs=[SMEM, SMEM] + [gstate] * 4 + [gtok, gtok, whole((tokens, 4 * heads))],
        out_specs=whole(part.shape),
        out_shape=part,
        scratch_shapes=[
            pltpu.VMEM((2, 2 * state, gwide), BF16),
            pltpu.VMEM((2, tokens, state), F32),
        ],
        compiler_params=grant(GRADS_VMEM),
        name="grads",
    )(
        flag, spot, enter_f, other_f, enter_b, other_b, inputs, cotangent, edges
    )
    parts = [carried[k] + grads_loc[k] for k in range(len(masks))]

    state_spec = pl.BlockSpec((per, half, LANES), lambda i: (i, 0, 0))

    def finish(kind, first, own, other, base, proj, name):
        return pl.pallas_call(
            functools.partial(output_kernel, group, width, kind),
            grid=(groups,),
            in_specs=[
                SMEM,
                state_spec,
                state_spec,
                tok,
                whole((tokens, 4 * heads)),
                whole((tokens, state)),
            ],
            out_specs=tok,
            out_shape=jax.ShapeDtypeStruct((tokens, channels), BF16),
            scratch_shapes=[pltpu.VMEM((state, wide), BF16)] * 2,
            compiler_params=grant(OUTPUT_VMEM),
            cost_estimate=pl.CostEstimate(
                flops=4 * tokens * state * channels,
                transcendentals=0,
                bytes_accessed=8 * tokens * channels,
            ),
            name=name,
        )(first, own, other, base, edges, proj)

    if tensor == 4:
        (own, *leaving), first = lax.optimization_barrier((parts, flag))
        landed = [swap_with(v, "tensor", k) for k, v in zip(masks[1:], leaving)]
        mixed = finish(1, first, enter_f, other_f, mixed_loc, c_in, "mixed")
        landed, mixed = lax.optimization_barrier((landed, mixed))
        total = (own + landed[0] + landed[1] + landed[2]).astype(BF16)
        total, first = lax.optimization_barrier((total, first))
        landed = [swap_with(total, "tensor", k) for k in masks[1:]]
        grad_inputs = finish(0, first, enter_b, other_b, gx_loc, b_in, "grad_inputs")
        landed, grad_inputs = lax.optimization_barrier((landed, grad_inputs))
        summed = jnp.zeros((4,) + total.shape, BF16)
        for k, v in zip(masks, [total] + landed):
            summed = lax.dynamic_update_index_in_dim(summed, v, place ^ k, 0)
        grad_b, grad_c = summed[:, 0], summed[:, 1]
    else:
        mixed = finish(1, flag, enter_f, other_f, mixed_loc, c_in, "mixed")
        grad_inputs = finish(0, flag, enter_b, other_b, gx_loc, b_in, "grad_inputs")
        grad_b, grad_c = lax.psum(parts[0], "tensor").astype(BF16)
    return (mixed, grad_inputs, grad_b.reshape(tokens, state), grad_c.reshape(tokens, state))


def solution(mesh):
    in_specs = (
        P("context", "tensor"),
        P("tensor", "context"),
        P("tensor"),
        P("tensor"),
        P("context", None),
        P("context", None),
        P("context"),
        P("context", "tensor"),
    )
    out_specs = (
        P("context", "tensor"),
        P("context", "tensor"),
        P("context", None),
        P("context", None),
    )
    return jax.shard_map(shards, mesh=mesh, in_specs=in_specs, out_specs=out_specs, check_vma=False)
```
